32 devices in a mesh: groups: 2 (over y), ctx: 4 (over z), mp: 4 (over x, core).
Axes of the slice: x: 2, y: 2, z: 4, core: 2. Of those that a mesh axis runs over, the one named last changes fastest.
Arguments:
- queries: bfloat16 [2048, 4096], P(('groups', 'ctx'), 'mp'), parts along dimension 0, may hold values from -18 to 18
- keyvals: bfloat16 [2048, 512], P(('groups', 'ctx', 'mp')), parts along dimension 0, may hold values from -6 to 6
- segment_ids: int32 [2048], P('groups'), parts along dimension 0, may hold values from 0 to 2, never falling along the last dimension, each value on 1 to 512 neighbouring positions
- residual: bfloat16 [2048, 4096], P(('groups', 'ctx', 'mp')), parts along dimension 0, may hold values from -180 to 180
- out_weight: bfloat16 [4096, 4096], P('mp', 'ctx'), may hold values from -0.375 to 0.375
- lru_weight: bfloat16 [4096, 4096], P('ctx', 'mp'), may hold values from -0.09375 to 0.09375
- conv_weight: float32 [4, 4096], P(None, 'mp'), may hold values from -3 to 3
- gate_decay_w: bfloat16 [16, 256, 256], P('mp'), may hold values from -0.375 to 0.375
- gate_input_w: bfloat16 [16, 256, 256], P('mp'), may hold values from -0.375 to 0.375
- gate_decay_b: float32 [4096], P('mp'), may hold values from -3 to 3
- gate_input_b: float32 [4096], P('mp'), may hold values from -3 to 3
- decay_codes: int32 [4096], P('mp'), may hold values from 0 to 15
- norm_gain: float32 [4096], replicated, may hold values from 0.1 to 1.9
Outputs:
- resid_out: bfloat16 [2048, 4096], P(('groups', 'ctx', 'mp')), parts along dimension 0
- lru_out: bfloat16 [2048, 4096], P(('groups', 'ctx'), 'mp'), parts along dimension 0
The draws below stay inside these ranges and needn't reach their ends.
There are 2 independent parts, one for each index of `groups`. The reference program is written for one: setup_inputs(seed, part) draws one part's arguments, and reference() takes and returns one part's arrays. A program takes and returns all parts, laid end to end along the dimension named above; an argument that names none is the same for every part. Nothing has to cross between parts.
All inputs are finite; a program needn't handle non-finite values.
Results may differ from the reference program's by a relative error of at most 0.017.
Values may be sent and summed in bfloat16 or wider, within the bound.
No kernel may reach another device: no remote copies, remote signals or barrier semaphores. Data moves between devices by JAX's collectives and lax.ppermute only.
A program may use at most 64 MiB of HBM per device.

```python
import math
import jax
import jax.numpy as jnp
import numpy as np
from jax import lax

D = 4096
H = 16
HD = 256
WIN = 2048
LRU = 4096
NBLK = 16
CONV = 4
LEVELS = 16
BW = 256
TOKENS = 1024
N_MP = 4


def draw_queries(key, part):
    values = jnp.clip(2.0 * jax.random.normal(jax.random.fold_in(key, 3), (TOKENS, H * HD), jnp.float32), -8.0, 8.0)
    return values.astype(jnp.bfloat16)


def draw_keyvals(key, part):
    values = jnp.clip(jax.random.normal(jax.random.fold_in(key, 4), (TOKENS, 2 * HD), jnp.float32), -6.0, 6.0)
    return values.astype(jnp.bfloat16)


def draw_residual(key, part):
    values = jnp.clip(jax.random.normal(jax.random.fold_in(key, 5), (TOKENS, D), jnp.float32), -6.0, 6.0)
    return values.astype(jnp.bfloat16)


def touch_ends(array, rng, low, high):
    index_at = [jax.random.randint(jax.random.fold_in(rng, axis), (), 0, length) for axis, length in enumerate(array.shape)]
    longest = array.shape.index(max(array.shape))
    beside = index_at[:longest] + [(index_at[longest] + 1) % array.shape[longest]] + index_at[longest + 1:]
    return array.at[tuple(index_at)].set(low).at[tuple(beside)].set(high)


def level_of(key, extent, pieces, least, largest):
    def one(axis_at, blocks):
        draws = jax.random.uniform(jax.random.fold_in(jax.random.fold_in(key, 6), axis_at), (blocks,), jnp.float32, least / len(pieces), largest / len(pieces))
        return jnp.repeat(jnp.exp(draws), extent[axis_at] // blocks).reshape((-1,) + (1,) * (len(extent) - axis_at - 1))

    level = one(*pieces[0])
    for cut in pieces[1:]:
        level = level * one(*cut)
    return level


def split_up(number_of, total, most, lean):
    weights = [(1 << 20) // math.isqrt(rank ** lean) + 1 for rank in range(2, number_of + 1)]
    spare, counts = total - most - (number_of - 1), [1] * (number_of - 1)
    while spare > 0:
        movable = [i for i in range(number_of - 1) if counts[i] < most]
        mass, remaining = sum([weights[i] for i in movable]), spare
        for i in movable:
            extra = min(most - counts[i], max(1, remaining * weights[i] // mass), spare)
            counts[i] = counts[i] + extra
            spare = spare - extra
    return np.array([most] + counts)


def ragged(stream_key, number_of, total, limit, lean):
    if number_of == 2:
        one = jax.random.randint(stream_key, (), max(1, total - limit), min(limit, total - 1) + 1)
        return jnp.stack([one, total - one])
    tallies = jnp.asarray(split_up(number_of, total, limit, lean), jnp.int32)
    twos = (number_of - 1) // 2
    giver, receiver = tallies[1:1 + 2 * twos:2], tallies[2:2 + 2 * twos:2]
    room = jnp.minimum(giver - 1, limit - receiver)
    moved = jax.random.randint(jax.random.fold_in(stream_key, 1), (twos,), 0, 1 << 20) % (room + 1)
    tallies = tallies.at[1:1 + 2 * twos:2].set(giver - moved).at[2:2 + 2 * twos:2].set(receiver + moved)
    return tallies[jax.random.permutation(jax.random.fold_in(stream_key, 2), number_of)]


def noise(own_key, extent, scale, most, cuts=(), held_as=jnp.bfloat16):
    array = jax.random.normal(own_key, extent, jnp.float32) * scale
    if len(cuts) > 0:
        array = level_of(own_key, extent, cuts, -0.22, 0.18) * array
    return jnp.clip(array, min=-most, max=most).astype(held_as)


def setup_inputs(seed: int = 0, part: int = 0) -> dict:
    streams_of = jax.random.split(jax.random.key(seed), 14)
    part_keys = jax.random.split(jax.random.fold_in(streams_of[13], part), 14)
    queries = draw_queries(jax.random.fold_in(jax.random.fold_in(streams_of[13], part), 71), part)
    keyvals = draw_keyvals(jax.random.fold_in(jax.random.fold_in(streams_of[13], part), 71), part)
    segment_ids = jnp.searchsorted(jnp.cumsum(ragged(part_keys[2], 3, TOKENS, TOKENS // 2, 0)), jnp.arange(TOKENS), side="right").astype(jnp.int32)
    residual = draw_residual(jax.random.fold_in(jax.random.fold_in(streams_of[13], part), 71), part)
    out_weight = noise(streams_of[4], (H * HD, D), HD ** -0.5, 0.375, ((0, 4), (1, 4)))
    lru_weight = noise(streams_of[5], (D, LRU), D ** -0.5, 0.09375, ((0, 4), (1, 4)))
    conv_weight = noise(streams_of[6], (CONV, LRU), 0.5, 3.0, ((1, 4),), jnp.float32)
    gate_decay_w = noise(streams_of[7], (NBLK, BW, BW), BW ** -0.5, 0.375, ((0, 4),))
    gate_input_w = noise(streams_of[8], (NBLK, BW, BW), BW ** -0.5, 0.375, ((0, 4),))
    gate_decay_b = noise(streams_of[9], (LRU,), 1.0, 3.0, ((0, 4),), jnp.float32)
    gate_input_b = noise(streams_of[10], (LRU,), 1.0, 3.0, ((0, 4),), jnp.float32)
    decay_codes = touch_ends(jax.random.randint(streams_of[11], (LRU,), 0, LEVELS), jax.random.fold_in(streams_of[11], 1), 0, LEVELS - 1).astype(jnp.int32)
    norm_gain = jnp.clip(1.0 + 0.18 * jax.random.normal(streams_of[12], (D,), jnp.float32), 0.1, 1.9)
    return dict(queries=queries, keyvals=keyvals, segment_ids=segment_ids, residual=residual, out_weight=out_weight, lru_weight=lru_weight, conv_weight=conv_weight, gate_decay_w=gate_decay_w, gate_input_w=gate_input_w, gate_decay_b=gate_decay_b, gate_input_b=gate_input_b, decay_codes=decay_codes, norm_gain=norm_gain)


def decay_rates():
    levels = jnp.arange(LEVELS, dtype=jnp.float32)
    return 0.006 * jnp.exp(-levels * (math.log(3000.0) / (LEVELS - 1)))

def chain_link(former, latter):
    return (former[0] * latter[0], latter[0] * former[1] + latter[1])

def reference(queries, keyvals, segment_ids, residual, out_weight, lru_weight, conv_weight, gate_decay_w, gate_input_w, gate_decay_b, gate_input_b, decay_codes, norm_gain):
    block_rows = min(512, TOKENS)
    block_count = TOKENS // block_rows
    pad_kv = jnp.concatenate([jnp.zeros((WIN, 2 * HD), keyvals.dtype), keyvals], axis=0)
    pad_seg = jnp.concatenate([jnp.full((WIN,), -1, jnp.int32), segment_ids.astype(jnp.int32)])
    score_scale = 1.0 / math.sqrt(HD)

    def attend(block_index):
        first_row = (block_index * block_rows).astype(jnp.int32)
        query_block = lax.dynamic_slice_in_dim(queries, first_row, block_rows, 0).reshape(block_rows, H, HD)
        key_block = lax.dynamic_slice_in_dim(pad_kv, first_row, WIN + block_rows, 0)
        key_seg = lax.dynamic_slice_in_dim(pad_seg, first_row, WIN + block_rows, 0)
        query_seg = lax.dynamic_slice_in_dim(segment_ids.astype(jnp.int32), first_row, block_rows, 0)
        query_pos = first_row + jnp.arange(block_rows, dtype=jnp.int32)
        key_pos = first_row - WIN + jnp.arange(WIN + block_rows, dtype=jnp.int32)
        distance = query_pos[:, None] - key_pos[None, :]
        allowed = (distance >= 0) & (distance < WIN) & (query_seg[:, None] == key_seg[None, :])
        scores = jnp.einsum('thd,kd->htk', query_block.astype(jnp.float32), key_block[:, :HD].astype(jnp.float32)) * score_scale
        scores = jnp.where(allowed[None], scores, -1e+30)
        row_top = lax.optimization_barrier(jnp.max(scores, axis=-1, keepdims=True))
        weights = jnp.exp(scores - row_top)
        probs = (weights / lax.optimization_barrier(jnp.sum(weights, axis=-1, keepdims=True))).astype(jnp.bfloat16)
        gathered = jnp.einsum('htk,kd->thd', probs.astype(jnp.float32), key_block[:, HD:].astype(jnp.float32))
        return gathered.reshape(block_rows, H * HD).astype(jnp.bfloat16)
    attended = lax.map(attend, jnp.arange(block_count, dtype=jnp.int32)).reshape(TOKENS, H * HD)
    group_cols = H * HD // N_MP
    running = residual.astype(jnp.float32)
    for member in range(N_MP):
        head_part = jnp.dot(attended[:, member * group_cols:(member + 1) * group_cols], out_weight[member * group_cols:(member + 1) * group_cols], preferred_element_type=jnp.float32)
        head_part = lax.optimization_barrier(head_part.astype(jnp.bfloat16))
        running = running + head_part.astype(jnp.float32)
    resid_out = running.astype(jnp.bfloat16)
    resid_f32 = resid_out.astype(jnp.float32)
    normed = (resid_f32 * lax.rsqrt(lax.optimization_barrier(jnp.mean(resid_f32 * resid_f32, axis=-1, keepdims=True)) + 1e-06) * norm_gain).astype(jnp.bfloat16)
    lru_in = jnp.dot(normed, lru_weight, preferred_element_type=jnp.float32).astype(jnp.bfloat16)
    seg_int = segment_ids.astype(jnp.int32)
    pad_in = jnp.concatenate([jnp.zeros((CONV - 1, LRU), jnp.bfloat16), lru_in], axis=0)
    pad_conv_seg = jnp.concatenate([jnp.full((CONV - 1,), -1, jnp.int32), seg_int])
    conv_acc = jnp.zeros((TOKENS, LRU), jnp.float32)
    for offset in range(CONV):
        lag_rows = CONV - 1 - offset
        shifted = pad_in[lag_rows:lag_rows + TOKENS].astype(jnp.float32)
        same_doc = (pad_conv_seg[lag_rows:lag_rows + TOKENS] == seg_int)[:, None]
        conv_acc = conv_acc + jnp.where(same_doc, conv_weight[offset] * shifted, 0.0)
    conv_out = conv_acc.astype(jnp.bfloat16)
    grouped = conv_out.reshape(TOKENS, NBLK, BW).astype(jnp.float32)
    decay_gate = jax.nn.sigmoid(jnp.einsum('tbi,bij->tbj', grouped, gate_decay_w.astype(jnp.float32)).reshape(TOKENS, LRU) + gate_decay_b)
    input_gate = jax.nn.sigmoid(jnp.einsum('tbi,bij->tbj', grouped, gate_input_w.astype(jnp.float32)).reshape(TOKENS, LRU) + gate_input_b)
    decay_rate = decay_rates()[decay_codes]
    log_decay = -8.0 * decay_gate * decay_rate
    prev_seg = jnp.concatenate([jnp.full((1,), -1, jnp.int32), seg_int[:-1]])
    restart = (seg_int != prev_seg)[:, None]
    keep_factor = jnp.where(restart, 0.0, jnp.exp(log_decay))
    input_scale = jnp.where(restart, 1.0, jnp.sqrt(-jnp.expm1(2.0 * log_decay)))
    driven = input_scale * input_gate * conv_out.astype(jnp.float32)
    cum_keep, states = lax.associative_scan(chain_link, (keep_factor, driven), axis=0)
    return (resid_out, states.astype(jnp.bfloat16))
```

```python
import functools
import math

import jax
import jax.numpy as jnp
from jax import lax
from jax.experimental import pallas as pl
from jax.experimental.pallas import tpu as pltpu
from jax.sharding import PartitionSpec as P

HD = 256
WIN = 2048
CONV = 4
LEVELS = 16
BW = 256


def shifted_2(value, axis, steps):
    count = lax.axis_size(axis)
    initial, last = (max(0, -steps), min(count, count - steps))
    return lax.ppermute(value, axis, [(source, source + steps) for source in range(initial, last)])


def decay_rates():
    levels = jnp.arange(LEVELS, dtype=jnp.float32)
    return 0.006 * jnp.exp(-levels * (math.log(3000.0) / (LEVELS - 1)))


def chain_link(former, latter):
    return (former[0] * latter[0], latter[0] * former[1] + latter[1])


def rms_scaled(values, norm_gain):
    value_f32 = values.astype(jnp.float32)
    inverse = lax.rsqrt(jnp.mean(value_f32 * value_f32, axis=-1, keepdims=True) + 1e-06)
    return (value_f32 * inverse * norm_gain).astype(jnp.bfloat16)


def attend_local(queries, keys_all, allowed):
    rows_here = queries.shape[0]
    heads_here = queries.shape[1] // HD
    query_heads = queries.reshape(rows_here, heads_here, HD)
    score_scale = 1.0 / math.sqrt(HD)
    scores = (
        jnp.einsum("thd,kd->htk", query_heads, keys_all[:, :HD], preferred_element_type=jnp.float32)
        * score_scale
    )
    scores = jnp.where(allowed[None], scores, -1e30)
    row_top = jnp.max(scores, axis=-1, keepdims=True)
    weights = jnp.exp(scores - row_top)
    probs = (weights / jnp.sum(weights, axis=-1, keepdims=True)).astype(jnp.bfloat16)
    gathered = jnp.einsum(
        "htk,kd->thd", probs, keys_all[:, HD:], preferred_element_type=jnp.float32
    )
    return gathered.reshape(rows_here, heads_here * HD).astype(jnp.bfloat16)


def local_wide(
    queries,
    keyvals,
    segment_ids,
    residual,
    out_weight,
    lru_weight,
    conv_weight,
    gate_decay_w,
    gate_input_w,
    gate_decay_b,
    gate_input_b,
    decay_codes,
    norm_gain,
):
    rows_here = queries.shape[0]
    ctx_index = lax.axis_index("ctx")
    back_blocks = WIN // rows_here
    own_kv = lax.all_gather(keyvals, "mp", axis=0, tiled=True)
    earlier = []
    moving = own_kv
    for offset in range(back_blocks):
        moving = shifted_2(moving, "ctx", 1)
        earlier = [moving] + earlier
    keys_all = jnp.concatenate(earlier + [own_kv], axis=0)
    pad_seg = jnp.concatenate([jnp.full((WIN,), -1, jnp.int32), segment_ids])
    query_seg = lax.dynamic_slice_in_dim(segment_ids, ctx_index * rows_here, rows_here)
    key_seg = lax.dynamic_slice_in_dim(
        pad_seg, ctx_index * rows_here, (back_blocks + 1) * rows_here
    )
    query_pos = ctx_index * rows_here + jnp.arange(rows_here, dtype=jnp.int32)
    key_pos = (ctx_index - back_blocks) * rows_here + jnp.arange(
        (back_blocks + 1) * rows_here, dtype=jnp.int32
    )
    distance = query_pos[:, None] - key_pos[None, :]
    allowed = (distance >= 0) & (distance < WIN) & (query_seg[:, None] == key_seg[None, :])
    attended = attend_local(queries, keys_all, allowed)
    head_part = jnp.dot(
        attended,
        lax.all_gather(out_weight, "ctx", axis=1, tiled=True),
        preferred_element_type=jnp.float32,
    )
    summed = lax.psum_scatter(
        head_part.astype(jnp.bfloat16), "mp", scatter_dimension=0, tiled=True
    ).astype(jnp.float32)
    resid_out = (summed + residual.astype(jnp.float32)).astype(jnp.bfloat16)
    normed = lax.all_gather(rms_scaled(resid_out, norm_gain), "mp", axis=0, tiled=True)
    channels = lru_weight.shape[1]
    lru_in = jnp.dot(
        normed,
        lax.all_gather(lru_weight, "ctx", axis=0, tiled=True),
        preferred_element_type=jnp.float32,
    ).astype(jnp.bfloat16)
    rim_rows = shifted_2(lru_in[rows_here - (CONV - 1) :], "ctx", 1)
    extended = jnp.concatenate([rim_rows, lru_in], axis=0)
    ext_seg = lax.dynamic_slice_in_dim(
        pad_seg, ctx_index * rows_here + WIN - (CONV - 1), rows_here + CONV - 1
    )
    conv_acc = jnp.zeros((rows_here, channels), jnp.float32)
    for offset in range(CONV):
        lag_rows = CONV - 1 - offset
        shifted = extended[lag_rows : lag_rows + rows_here].astype(jnp.float32)
        same_doc = (ext_seg[lag_rows : lag_rows + rows_here] == query_seg)[:, None]
        conv_acc = conv_acc + jnp.where(same_doc, conv_weight[offset] * shifted, 0.0)
    conv_out = conv_acc.astype(jnp.bfloat16)
    blocks_here = channels // BW
    grouped = conv_out.reshape(rows_here, blocks_here, BW)
    decay_gate = jax.nn.sigmoid(
        jnp.einsum(
            "tbi,bij->tbj", grouped, gate_decay_w, preferred_element_type=jnp.float32
        ).reshape(rows_here, channels)
        + gate_decay_b
    )
    input_gate = jax.nn.sigmoid(
        jnp.einsum(
            "tbi,bij->tbj", grouped, gate_input_w, preferred_element_type=jnp.float32
        ).reshape(rows_here, channels)
        + gate_input_b
    )
    levels = jnp.arange(LEVELS, dtype=jnp.int32)
    decay_rate = jnp.sum(
        jnp.where(decay_codes[:, None] == levels[None, :], decay_rates()[None, :], 0.0), axis=1
    )
    log_decay = -8.0 * decay_gate * decay_rate
    restart = (query_seg != ext_seg[CONV - 2 : CONV - 2 + rows_here])[:, None]
    keep_factor = jnp.where(restart, 0.0, jnp.exp(log_decay))
    input_scale = jnp.where(restart, 1.0, jnp.sqrt(-jnp.expm1(2.0 * log_decay)))
    driven = input_scale * input_gate * conv_out.astype(jnp.float32)
    cum_keep, local_state = lax.associative_scan(chain_link, (keep_factor, driven), axis=0)
    block_keep = cum_keep[rows_here - 1]
    block_state = local_state[rows_here - 1]

    def relay_turn(turn_index, state_in):
        return shifted_2(block_keep * state_in + block_state, "ctx", 1)

    incoming = lax.fori_loop(0, lax.axis_size("ctx") - 1, relay_turn, jnp.zeros_like(block_state))
    states = local_state + cum_keep * incoming[None, :]
    return (resid_out, states.astype(jnp.bfloat16))


F32 = jnp.float32
BF16 = jnp.bfloat16
VMEM = pl.BlockSpec(memory_space=pltpu.VMEM)
SMEM = pl.BlockSpec(memory_space=pltpu.SMEM)
TILE = 16
SUB = 8
LANES = 128


def rotated(value, axis, steps):
    count = lax.axis_size(axis)
    return lax.ppermute(value, axis, [(s, (s - steps) % count) for s in range(count)])


def swapped(value, axis, flip):
    count = lax.axis_size(axis)
    return lax.ppermute(value, axis, [(s, s ^ flip) for s in range(count)])


def segment_start(pos, low, high):
    return jnp.where(pos >= high, high, jnp.where(pos >= low, low, 0))


def assemble_kernel(rows, shard, nctx, scal, *refs):
    out = refs[-1]
    ctx_index, mp_index = scal[0], scal[1]
    for flip, piece in enumerate(refs[:-1]):
        member = jnp.bitwise_xor(mp_index, flip)
        for step in range(nctx):
            block = lax.rem(ctx_index + step, nctx)
            first = pl.multiple_of(block * rows + member * shard, shard)
            out[pl.ds(first, shard), :] = piece[step * shard : (step + 1) * shard, :]


def assemble(scal, pieces, rows, shard, nctx):
    tokens = nctx * rows
    width = pieces[0].shape[1]
    return pl.pallas_call(
        functools.partial(assemble_kernel, rows, shard, nctx),
        out_shape=jax.ShapeDtypeStruct((tokens, width), BF16),
        in_specs=[SMEM] + [VMEM] * len(pieces),
        out_specs=VMEM,
        name="assemble",
    )(scal, *pieces)


def attend_kernel(nctx, back, steps, shard, scal, *refs):
    count = len(steps)
    q_refs, resid_refs = refs[:count], refs[count : 2 * count]
    kv, weight, keep, send, att, acc = refs[2 * count :]
    rows, width = q_refs[0].shape
    heads = width // HD
    half = weight.shape[1] // 2
    ctx_index, mp_index, low, high = scal[0], scal[1], scal[2], scal[3]
    side = jnp.bitwise_and(mp_index, 1)
    window = min(back + 1, nctx) * rows
    scale = 1.0 / math.sqrt(HD)
    for j, step in enumerate(steps):
        block = lax.rem(ctx_index + step, nctx)
        first_key = pl.multiple_of(
            jnp.minimum(jnp.maximum(block - back, 0), nctx - window // rows) * rows, rows
        )
        qpos = block * rows + lax.broadcasted_iota(jnp.int32, (rows, 1), 0)
        start = segment_start(qpos, low, high)
        kpos = first_key + lax.broadcasted_iota(jnp.int32, (1, window), 1)
        allowed = (kpos <= qpos) & (kpos >= start) & (qpos - kpos < WIN)
        for h in range(heads):
            query = q_refs[j][:, h * HD : (h + 1) * HD]
            keys = kv[pl.ds(first_key, window), :HD]
            scores = lax.dot_general(
                query, keys, (((1,), (1,)), ((), ())), preferred_element_type=F32
            )
            scores = jnp.where(allowed, scores * scale, -1e30)
            top = jnp.max(scores, axis=1, keepdims=True)
            weights = jnp.exp(scores - top)
            total = jnp.sum(weights, axis=1, keepdims=True)
            values = kv[pl.ds(first_key, window), HD:]
            gathered = jnp.dot(weights.astype(BF16), values, preferred_element_type=F32)
            att[:, h * HD : (h + 1) * HD] = (gathered / total).astype(BF16)
        own = pl.ds(pl.multiple_of(mp_index * shard, shard), shard)
        for out, which in ((send, 1 - side), (keep, side)):
            cols = pl.ds(pl.multiple_of(which * half, half), half)
            acc[...] = jnp.dot(att[...], weight[:, cols], preferred_element_type=F32)
            acc[own, :] += resid_refs[j][:, cols].astype(F32)
            out[j * rows : (j + 1) * rows, :] = acc[...].astype(BF16)


def attend(scal, queries, residuals, kv, weight, nctx, back, steps, shard):
    rows, width = queries[0].shape
    count = len(steps)
    half = weight.shape[1] // 2
    shape = jax.ShapeDtypeStruct((count * rows, half), BF16)
    return pl.pallas_call(
        functools.partial(attend_kernel, nctx, back, steps, shard),
        out_shape=(shape, shape),
        in_specs=[SMEM] + [VMEM] * (2 * count + 2),
        out_specs=(VMEM, VMEM),
        scratch_shapes=[pltpu.VMEM((rows, width), BF16), pltpu.VMEM((rows, half), F32)],
        name="attend",
    )(scal, *queries, *residuals, kv, weight)


def project_kernel(jobs, nhalves, shard, scal, *refs):
    halves, (gain, weight), outs = refs[:nhalves], refs[nhalves : nhalves + 2], refs[nhalves + 2 :]
    ctx_index, mp_index = scal[0], scal[1]
    side = jnp.bitwise_and(mp_index, 1)
    channels = weight.shape[1]
    half = weight.shape[0] // 2
    gains, weights = [], []
    for which in (side, 1 - side):
        span = pl.multiple_of(which * half, half)
        gains.append(gain[:, pl.ds(pl.multiple_of(ctx_index * 2 * half + span, half), half)])
        weights.append(weight[pl.ds(span, half), :])
    ones = jnp.ones((SUB, half), BF16)

    def parts_of(source, last):
        (own_ref, other_ref), first, rows = source
        begin = first + rows - last if last else first
        stop = first + rows
        return own_ref[begin:stop, :].astype(F32), other_ref[begin:stop, :].astype(F32)

    def projected(parts):
        total = None
        for part, scale, matrix in zip(parts, gains, weights):
            term = jnp.dot((part * scale).astype(BF16), matrix, preferred_element_type=F32)
            total = term if total is None else total + term
        return total

    def squares(parts):
        total = None
        for part in parts:
            term = lax.dot_general(
                ones, (part * part).astype(BF16), (((1,), (1,)), ((), ())), preferred_element_type=F32
            )
            total = term if total is None else total + term
        return total

    at = 0
    for main, prior in jobs:
        sums = []
        if main is not None:
            source = ((halves[main[0]], halves[main[0] + 1]), main[1], main[2])
            rows = main[2]
            parts = parts_of(source, 0)
            outs[at][0:rows, :] = projected(parts).astype(BF16)
            sums = squares(parts)
            mine = pl.ds(pl.multiple_of(main[1] + mp_index * shard, TILE), shard)
            for which, ref in ((side, source[0][0]), (1 - side, source[0][1])):
                outs[at + 1][:, pl.ds(pl.multiple_of(which * half, half), half)] = ref[mine, :]
        if prior is not None:
            source = ((halves[prior[0]], halves[prior[0] + 1]), prior[1], prior[2])
            tail = projected(parts_of(source, TILE))[TILE - SUB :, :]
            tail_sums = squares(parts_of(source, LANES))
            line = outs[at]
            base = rows if main is not None else 0
            if main is None:
                own = ((halves[prior[3]], halves[prior[3] + 1]), prior[4], prior[5])
                sums = squares(parts_of(own, 0))
            spare = channels - sums.shape[1] - LANES
            pieces = [sums, tail_sums] + ([jnp.zeros((SUB, spare), F32)] if spare else [])
            sums = jnp.concatenate(pieces, axis=1)
            coarse = sums.astype(BF16).astype(F32)
            index = lax.broadcasted_iota(jnp.int32, sums.shape, 0)
            sums = jnp.where(index == 0, coarse, sums - coarse)
            line[base : base + TILE, :] = jnp.concatenate([sums, tail], axis=0).astype(BF16)
        at += 1 if main is None else 2


def project(scal, halves, gain, weight, jobs, shard):
    channels = weight.shape[1]
    shapes = []
    for main, prior in jobs:
        extra = TILE if prior is not None else 0
        shapes.append(jax.ShapeDtypeStruct(((main[2] if main else 0) + extra, channels), BF16))
        if main is not None:
            shapes.append(jax.ShapeDtypeStruct((shard, weight.shape[0]), BF16))
    return pl.pallas_call(
        functools.partial(project_kernel, jobs, len(halves), shard),
        out_shape=tuple(shapes),
        in_specs=[SMEM] + [VMEM] * (len(halves) + 2),
        out_specs=tuple([VMEM] * len(shapes)),
        name="project",
    )(scal, *halves, gain, weight)


def minus_expm1(x):
    series = jnp.full_like(x, 1.0 / 5040.0)
    for divisor in (720.0, 120.0, 24.0, 6.0, 2.0, 1.0):
        series = series * x + 1.0 / divisor
    return jnp.where(x > -0.3, -x * series, 1.0 - jnp.exp(x))


def recur_kernel(features, scal, *refs):
    count = (len(refs) - 12) // 2
    mains, lines = refs[:count], refs[count : 2 * count]
    conv_w, decay_w, input_w, decay_b, input_b, codes = refs[2 * count : 2 * count + 6]
    local_ref, cum_ref, last_ref, ext, keep_s, state_s = refs[2 * count + 6 :]
    rows = mains[0].shape[0]
    width = mains[0].shape[1]
    ctx_index, low, high = scal[0], scal[2], scal[3]
    stats = None
    for line in lines:
        both = line[:, : rows + LANES].astype(F32)
        term = both[0:1, :] + both[1:2, :]
        stats = term if stats is None else stats + term
    inverse = lax.rsqrt(stats * (1.0 / features) + 1e-06)
    inverse = jnp.transpose(jnp.broadcast_to(inverse, (LANES, rows + LANES)))[:, 0:1]
    lanes = pl.ds(pl.multiple_of(pl.program_id(0) * width, width), width)
    main = tail = None
    for piece, line in zip(mains, lines):
        term, tail_term = piece[...].astype(F32), line[:, lanes].astype(F32)[SUB:, :]
        main = term if main is None else main + term
        tail = tail_term if tail is None else tail + tail_term
    ext[0:SUB, :] = (tail * inverse[rows + LANES - SUB :, :]).astype(BF16).astype(F32)
    ext[SUB : SUB + rows, :] = (main * inverse[:rows, :]).astype(BF16).astype(F32)
    pos = ctx_index * rows + lax.broadcasted_iota(jnp.int32, (rows, 1), 0)
    start = segment_start(pos, low, high)
    conv = None
    for lag in range(CONV):
        shifted = ext[SUB - lag : SUB - lag + rows, :]
        term = jnp.where(pos - lag >= start, conv_w[lag : lag + 1, :] * shifted, 0.0)
        conv = term if conv is None else conv + term
    conv = conv.astype(BF16)
    gate_d = jax.nn.sigmoid(
        jnp.dot(conv, decay_w[0], preferred_element_type=F32) + decay_b[...]
    )
    gate_i = jax.nn.sigmoid(
        jnp.dot(conv, input_w[0], preferred_element_type=F32) + input_b[...]
    )
    rate = 0.006 * jnp.exp(-codes[...].astype(F32) * (math.log(3000.0) / (LEVELS - 1)))
    log_decay = -8.0 * gate_d * rate
    restart = pos == start
    keep = jnp.where(restart, 0.0, jnp.exp(log_decay))
    scale = jnp.where(restart, 1.0, jnp.sqrt(minus_expm1(2.0 * log_decay)))
    state = scale * gate_i * conv.astype(F32)
    tiles = rows // SUB
    keep = keep.reshape(tiles, SUB, width)
    state = state.reshape(tiles, SUB, width)
    index = lax.broadcasted_iota(jnp.int32, (tiles, SUB, width), 1)
    shift = 1
    while shift < SUB:
        inside = index >= shift
        prior_keep = jnp.where(inside, pltpu.roll(keep, shift, 1), 1.0)
        prior_state = jnp.where(inside, pltpu.roll(state, shift, 1), 0.0)
        state = keep * prior_state + state
        keep = keep * prior_keep
        shift *= 2
    keep_s[...] = keep
    state_s[...] = state
    run_keep = jnp.ones((1, width), F32)
    run_state = jnp.zeros((1, width), F32)
    for t in range(tiles):
        keep_t, state_t = keep_s[t], state_s[t]
        new_state = state_t + keep_t * run_state
        new_keep = keep_t * run_keep
        local_ref[t * SUB : (t + 1) * SUB, :] = new_state
        cum_ref[t * SUB : (t + 1) * SUB, :] = new_keep
        run_state, run_keep = new_state[SUB - 1 :, :], new_keep[SUB - 1 :, :]
    line = lax.broadcasted_iota(jnp.int32, (SUB, width), 0)
    last_ref[...] = jnp.where(line == 0, run_keep, run_state)


def recur(scal, mains, lines, conv_w, decay_w, input_w, decay_b, input_b, codes, rows, features):
    channels = conv_w.shape[1]
    tiles = rows // SUB
    by_block = pl.BlockSpec((rows, BW), lambda j: (0, j))
    row_spec = pl.BlockSpec((1, BW), lambda j: (0, j))
    gate_spec = pl.BlockSpec((1, BW, BW), lambda j: (j, 0, 0))
    line_specs = [
        pl.BlockSpec((TILE, channels), functools.partial(lambda at, j: (at, 0), at))
        for _, at in lines
    ]
    full = jax.ShapeDtypeStruct((rows, channels), F32)
    return pl.pallas_call(
        functools.partial(recur_kernel, features),
        grid=(channels // BW,),
        out_shape=(full, full, jax.ShapeDtypeStruct((SUB, channels), F32)),
        in_specs=[SMEM]
        + [by_block] * len(mains)
        + line_specs
        + [pl.BlockSpec((CONV, BW), lambda j: (0, j)), gate_spec, gate_spec]
        + [row_spec] * 3,
        out_specs=(by_block, by_block, pl.BlockSpec((SUB, BW), lambda j: (0, j))),
        scratch_shapes=[
            pltpu.VMEM((rows + SUB, BW), F32),
            pltpu.VMEM((tiles, SUB, BW), F32),
            pltpu.VMEM((tiles, SUB, BW), F32),
        ],
        name="recur",
    )(scal, *mains, *[line for line, _ in lines], conv_w, decay_w, input_w, decay_b, input_b, codes)


def local_near(
    queries,
    keyvals,
    segment_ids,
    residual,
    out_weight,
    lru_weight,
    conv_weight,
    gate_decay_w,
    gate_input_w,
    gate_decay_b,
    gate_input_b,
    decay_codes,
    norm_gain,
):
    rows = queries.shape[0]
    shard = keyvals.shape[0]
    tokens = segment_ids.shape[0]
    nctx, nmp = lax.axis_size("ctx"), lax.axis_size("mp")
    ctx_index, mp_index = lax.axis_index("ctx"), lax.axis_index("mp")
    features = residual.shape[1]
    cols = out_weight.shape[1]
    longest = tokens // 2
    back = -(-(min(WIN, longest) - 1) // rows)
    reach = min(nctx - 1, -(-longest // rows))
    low = jnp.sum((segment_ids < 1).astype(jnp.int32))
    high = jnp.sum((segment_ids < 2).astype(jnp.int32))
    scal = jnp.stack([ctx_index, mp_index, low, high]).astype(jnp.int32)

    own_kv = jnp.concatenate(
        [keyvals] + [rotated(keyvals, "ctx", step) for step in range(1, nctx)], axis=0
    )
    pieces = {0: own_kv}
    flip = nmp // 2
    while flip >= 1:
        for done in sorted(pieces):
            pieces[done | flip] = swapped(pieces[done], "mp", flip)
        flip //= 2
    kv = assemble(scal, [pieces[e] for e in range(nmp)], rows, shard, nctx)

    visiting = [queries] + [rotated(queries, "ctx", step) for step in range(1, nctx)]
    resid_parts = []
    for step in range(nctx):
        first = lax.rem(ctx_index + nctx - step, nctx) * cols
        part = lax.dynamic_slice_in_dim(residual, first, cols, axis=1)
        resid_parts.append(rotated(part, "ctx", step) if step else part)

    chunks = [tuple(range(i, min(i + 2, nctx))) for i in range(0, nctx, 2)]
    gain = norm_gain.reshape(1, features)
    where_is, halves = {}, []
    messages, lines, resid_rows = {}, {}, {}
    for steps in chunks:
        keep, send = attend(
            scal,
            [visiting[s] for s in steps],
            [resid_parts[s] for s in steps],
            kv,
            out_weight,
            nctx,
            back,
            steps,
            shard,
        )
        mine = (keep.astype(F32) + swapped(send, "mp", 1).astype(F32)).astype(BF16)
        flip = 2
        while flip < nmp:
            mine = (mine.astype(F32) + swapped(mine, "mp", flip).astype(F32)).astype(BF16)
            flip *= 2
        for j, s in enumerate(steps):
            where_is[s] = (len(halves), j * rows, rows)
        halves = halves + [mine, swapped(mine, "mp", 1)]
        jobs = [(where_is[s], where_is[s - 1] if s else None) for s in steps]
        if steps[-1] == nctx - 1:
            jobs.append((None, where_is[nctx - 1] + where_is[0]))
        outs = project(scal, halves, gain, lru_weight, jobs, shard)
        for j, s in enumerate(steps):
            messages[s], resid_rows[s] = outs[2 * j], outs[2 * j + 1]
        if steps[-1] == nctx - 1:
            own_line = outs[2 * len(steps)]
    mains, lines = [messages[0]], [(own_line, 0)]
    for step in range(1, nctx):
        got = rotated(messages[step], "ctx", -step)
        mains.append(got)
        lines.append((got, rows // TILE))
    local_state, cum_keep, last = recur(
        scal,
        mains,
        lines,
        conv_weight,
        gate_decay_w,
        gate_input_w,
        gate_decay_b.reshape(1, -1),
        gate_input_b.reshape(1, -1),
        decay_codes.reshape(1, -1),
        rows,
        features,
    )
    incoming = jnp.zeros_like(last[0])
    for step in range(reach, 0, -1):
        before = rotated(last, "ctx", -step)
        incoming = jnp.where(ctx_index >= step, before[0] * incoming + before[1], 0.0)
    states = local_state + cum_keep * incoming[None, :]
    resid_out = jnp.zeros(residual.shape, BF16)
    for step in range(nctx):
        part = rotated(resid_rows[step], "ctx", -step) if step else resid_rows[step]
        first = lax.rem(ctx_index + nctx - step, nctx) * cols
        resid_out = lax.dynamic_update_slice_in_dim(resid_out, part, first, axis=1)
    return (resid_out, states.astype(BF16))


def local(queries, keyvals, segment_ids, *rest):
    near = segment_ids.shape[0] <= WIN and lax.axis_size("mp") % 2 == 0
    return (local_near if near else local_wide)(queries, keyvals, segment_ids, *rest)


def solution(mesh):
    in_specs = (
        P(("groups", "ctx"), "mp"),
        P(("groups", "ctx", "mp"), None),
        P("groups"),
        P(("groups", "ctx", "mp"), None),
        P("mp", "ctx"),
        P("ctx", "mp"),
        P(None, "mp"),
        P("mp", None, None),
        P("mp", None, None),
        P("mp"),
        P("mp"),
        P("mp"),
        P(),
    )
    out_specs = (P(("groups", "ctx", "mp"), None), P(("groups", "ctx"), "mp"))
    return jax.shard_map(local, mesh=mesh, in_specs=in_specs, out_specs=out_specs, check_vma=False)
```

```python
import functools
import math

import jax
import jax.numpy as jnp
from jax import lax
from jax.experimental import pallas as pl
from jax.experimental.pallas import tpu as pltpu
from jax.sharding import PartitionSpec as P

HD = 256
WIN = 2048
CONV = 4
LEVELS = 16
BW = 256


def shifted_2(value, axis, steps):
    count = lax.axis_size(axis)
    initial, last = (max(0, -steps), min(count, count - steps))
    return lax.ppermute(value, axis, [(source, source + steps) for source in range(initial, last)])


def decay_rates():
    levels = jnp.arange(LEVELS, dtype=jnp.float32)
    return 0.006 * jnp.exp(-levels * (math.log(3000.0) / (LEVELS - 1)))


def chain_link(former, latter):
    return (former[0] * latter[0], latter[0] * former[1] + latter[1])


def rms_scaled(values, norm_gain):
    value_f32 = values.astype(jnp.float32)
    inverse = lax.rsqrt(jnp.mean(value_f32 * value_f32, axis=-1, keepdims=True) + 1e-06)
    return (value_f32 * inverse * norm_gain).astype(jnp.bfloat16)


def attend_local(queries, keys_all, allowed):
    rows_here = queries.shape[0]
    heads_here = queries.shape[1] // HD
    query_heads = queries.reshape(rows_here, heads_here, HD)
    score_scale = 1.0 / math.sqrt(HD)
    scores = (
        jnp.einsum("thd,kd->htk", query_heads, keys_all[:, :HD], preferred_element_type=jnp.float32)
        * score_scale
    )
    scores = jnp.where(allowed[None], scores, -1e30)
    row_top = jnp.max(scores, axis=-1, keepdims=True)
    weights = jnp.exp(scores - row_top)
    probs = (weights / jnp.sum(weights, axis=-1, keepdims=True)).astype(jnp.bfloat16)
    gathered = jnp.einsum(
        "htk,kd->thd", probs, keys_all[:, HD:], preferred_element_type=jnp.float32
    )
    return gathered.reshape(rows_here, heads_here * HD).astype(jnp.bfloat16)


def local_wide(
    queries,
    keyvals,
    segment_ids,
    residual,
    out_weight,
    lru_weight,
    conv_weight,
    gate_decay_w,
    gate_input_w,
    gate_decay_b,
    gate_input_b,
    decay_codes,
    norm_gain,
):
    rows_here = queries.shape[0]
    ctx_index = lax.axis_index("ctx")
    back_blocks = WIN // rows_here
    own_kv = lax.all_gather(keyvals, "mp", axis=0, tiled=True)
    earlier = []
    moving = own_kv
    for _ in range(back_blocks):
        moving = shifted_2(moving, "ctx", 1)
        earlier = [moving] + earlier
    keys_all = jnp.concatenate(earlier + [own_kv], axis=0)
    pad_seg = jnp.concatenate([jnp.full((WIN,), -1, jnp.int32), segment_ids])
    query_seg = lax.dynamic_slice_in_dim(segment_ids, ctx_index * rows_here, rows_here)
    key_seg = lax.dynamic_slice_in_dim(
        pad_seg, ctx_index * rows_here, (back_blocks + 1) * rows_here
    )
    query_pos = ctx_index * rows_here + jnp.arange(rows_here, dtype=jnp.int32)
    key_pos = (ctx_index - back_blocks) * rows_here + jnp.arange(
        (back_blocks + 1) * rows_here, dtype=jnp.int32
    )
    distance = query_pos[:, None] - key_pos[None, :]
    allowed = (distance >= 0) & (distance < WIN) & (query_seg[:, None] == key_seg[None, :])
    attended = attend_local(queries, keys_all, allowed)
    head_part = jnp.dot(
        attended,
        lax.all_gather(out_weight, "ctx", axis=1, tiled=True),
        preferred_element_type=jnp.float32,
    )
    summed = lax.psum_scatter(
        head_part.astype(jnp.bfloat16), "mp", scatter_dimension=0, tiled=True
    ).astype(jnp.float32)
    resid_out = (summed + residual.astype(jnp.float32)).astype(jnp.bfloat16)
    normed = lax.all_gather(rms_scaled(resid_out, norm_gain), "mp", axis=0, tiled=True)
    channels = lru_weight.shape[1]
    lru_in = jnp.dot(
        normed,
        lax.all_gather(lru_weight, "ctx", axis=0, tiled=True),
        preferred_element_type=jnp.float32,
    ).astype(jnp.bfloat16)
    rim_rows = shifted_2(lru_in[rows_here - (CONV - 1) :], "ctx", 1)
    extended = jnp.concatenate([rim_rows, lru_in], axis=0)
    ext_seg = lax.dynamic_slice_in_dim(
        pad_seg, ctx_index * rows_here + WIN - (CONV - 1), rows_here + CONV - 1
    )
    conv_acc = jnp.zeros((rows_here, channels), jnp.float32)
    for offset in range(CONV):
        lag_rows = CONV - 1 - offset
        shifted = extended[lag_rows : lag_rows + rows_here].astype(jnp.float32)
        same_doc = (ext_seg[lag_rows : lag_rows + rows_here] == query_seg)[:, None]
        conv_acc = conv_acc + jnp.where(same_doc, conv_weight[offset] * shifted, 0.0)
    conv_out = conv_acc.astype(jnp.bfloat16)
    blocks_here = channels // BW
    grouped = conv_out.reshape(rows_here, blocks_here, BW)
    decay_gate = jax.nn.sigmoid(
        jnp.einsum(
            "tbi,bij->tbj", grouped, gate_decay_w, preferred_element_type=jnp.float32
        ).reshape(rows_here, channels)
        + gate_decay_b
    )
    input_gate = jax.nn.sigmoid(
        jnp.einsum(
            "tbi,bij->tbj", grouped, gate_input_w, preferred_element_type=jnp.float32
        ).reshape(rows_here, channels)
        + gate_input_b
    )
    levels = jnp.arange(LEVELS, dtype=jnp.int32)
    decay_rate = jnp.sum(
        jnp.where(decay_codes[:, None] == levels[None, :], decay_rates()[None, :], 0.0), axis=1
    )
    log_decay = -8.0 * decay_gate * decay_rate
    restart = (query_seg != ext_seg[CONV - 2 : CONV - 2 + rows_here])[:, None]
    keep_factor = jnp.where(restart, 0.0, jnp.exp(log_decay))
    input_scale = jnp.where(restart, 1.0, jnp.sqrt(-jnp.expm1(2.0 * log_decay)))
    driven = input_scale * input_gate * conv_out.astype(jnp.float32)
    cum_keep, local_state = lax.associative_scan(chain_link, (keep_factor, driven), axis=0)
    block_keep = cum_keep[rows_here - 1]
    block_state = local_state[rows_here - 1]

    def relay_turn(turn_index, state_in):
        return shifted_2(block_keep * state_in + block_state, "ctx", 1)

    incoming = lax.fori_loop(0, lax.axis_size("ctx") - 1, relay_turn, jnp.zeros_like(block_state))
    states = local_state + cum_keep * incoming[None, :]
    return (resid_out, states.astype(jnp.bfloat16))


F32 = jnp.float32
BF16 = jnp.bfloat16
VMEM = pl.BlockSpec(memory_space=pltpu.VMEM)
SMEM = pl.BlockSpec(memory_space=pltpu.SMEM)
TILE = 16
SUB = 8
LANES = 128


def rotated(value, axis, steps):
    count = lax.axis_size(axis)
    return lax.ppermute(value, axis, [(s, (s - steps) % count) for s in range(count)])


def swapped(value, axis, flip):
    count = lax.axis_size(axis)
    return lax.ppermute(value, axis, [(s, s ^ flip) for s in range(count)])


def segment_start(pos, low, high):
    return jnp.where(pos >= high, high, jnp.where(pos >= low, low, 0))


def pack_kernel(nctx, scal, queries, residual, own, *outs):
    rows = queries.shape[0]
    cols = own.shape[1]
    for step in range(nctx):
        block = lax.rem(scal[0] + nctx - step, nctx)
        part = residual[:, pl.ds(pl.multiple_of(block * cols, cols), cols)]
        if step:
            outs[step - 1][0:rows, :] = queries[...]
            outs[step - 1][rows:, :] = part
        else:
            own[...] = part


def pack(scal, queries, residual, nctx):
    rows, width = queries.shape
    shard = residual.shape[0]
    message = jax.ShapeDtypeStruct((rows + shard, width), BF16)
    return pl.pallas_call(
        functools.partial(pack_kernel, nctx),
        out_shape=(jax.ShapeDtypeStruct((shard, width), BF16),) + (message,) * (nctx - 1),
        in_specs=[SMEM, VMEM, VMEM],
        out_specs=(VMEM,) * nctx,
        name="pack",
    )(scal, queries, residual)


def join_kernel(nctx, scal, *refs):
    out = refs[-1]
    cols = refs[0].shape[1]
    for step, part in enumerate(refs[:-1]):
        block = lax.rem(scal[0] + nctx - step, nctx)
        out[:, pl.ds(pl.multiple_of(block * cols, cols), cols)] = part[...]


def join(scal, parts):
    nctx = len(parts)
    shard, cols = parts[0].shape
    return pl.pallas_call(
        functools.partial(join_kernel, nctx),
        out_shape=jax.ShapeDtypeStruct((shard, nctx * cols), BF16),
        in_specs=[SMEM] + [VMEM] * nctx,
        out_specs=VMEM,
        name="join",
    )(scal, *parts)


def assemble_kernel(rows, shard, nctx, scal, *refs):
    out = refs[-1]
    ctx_index, mp_index = scal[0], scal[1]
    for flip, piece in enumerate(refs[:-1]):
        member = jnp.bitwise_xor(mp_index, flip)
        for step in range(nctx):
            block = lax.rem(ctx_index + step, nctx)
            first = pl.multiple_of(block * rows + member * shard, shard)
            out[pl.ds(first, shard), :] = piece[step * shard : (step + 1) * shard, :]


def assemble(scal, pieces, rows, shard, nctx):
    tokens = nctx * rows
    width = pieces[0].shape[1]
    return pl.pallas_call(
        functools.partial(assemble_kernel, rows, shard, nctx),
        out_shape=jax.ShapeDtypeStruct((tokens, width), BF16),
        in_specs=[SMEM] + [VMEM] * len(pieces),
        out_specs=VMEM,
        name="assemble",
    )(scal, *pieces)


def attend_kernel(nctx, back, steps, shard, scal, *refs):
    count = len(steps)
    q_refs, resid_refs = refs[:count], refs[count : 2 * count]
    kv, weight, keep, send, att, acc = refs[2 * count :]
    rows, width = att.shape
    heads = width // HD
    half = weight.shape[1] // 2
    ctx_index, mp_index, low, high = scal[0], scal[1], scal[2], scal[3]
    side = jnp.bitwise_and(mp_index, 1)
    window = min(back + 1, nctx) * rows
    scale = 1.0 / math.sqrt(HD)
    for j, step in enumerate(steps):
        block = lax.rem(ctx_index + step, nctx)
        first_key = pl.multiple_of(
            jnp.minimum(jnp.maximum(block - back, 0), nctx - window // rows) * rows, rows
        )
        qpos = block * rows + lax.broadcasted_iota(jnp.int32, (rows, 1), 0)
        start = segment_start(qpos, low, high)
        kpos = first_key + lax.broadcasted_iota(jnp.int32, (1, window), 1)
        allowed = (kpos <= qpos) & (kpos >= start) & (qpos - kpos < WIN)
        for h in range(heads):
            query = q_refs[j][0:rows, h * HD : (h + 1) * HD]
            keys = kv[pl.ds(first_key, window), :HD]
            scores = lax.dot_general(
                query, keys, (((1,), (1,)), ((), ())), preferred_element_type=F32
            )
            scores = jnp.where(allowed, scores * scale, -1e30)
            top = jnp.max(scores, axis=1, keepdims=True)
            weights = jnp.exp(scores - top)
            total = jnp.sum(weights, axis=1, keepdims=True)
            values = kv[pl.ds(first_key, window), HD:]
            gathered = jnp.dot(weights.astype(BF16), values, preferred_element_type=F32)
            att[:, h * HD : (h + 1) * HD] = (gathered / total).astype(BF16)
        own = pl.ds(pl.multiple_of(mp_index * shard, shard), shard)
        for out, which in ((send, 1 - side), (keep, side)):
            cols = pl.ds(pl.multiple_of(which * half, half), half)
            acc[...] = jnp.dot(att[...], weight[:, cols], preferred_element_type=F32)
            mine = resid_refs[j][resid_refs[j].shape[0] - shard :, cols]
            acc[own, :] += mine.astype(F32)
            out[j * rows : (j + 1) * rows, :] = acc[...].astype(BF16)


def attend(scal, queries, residuals, kv, weight, nctx, back, steps, shard):
    rows, width = kv.shape[0] // nctx, queries[0].shape[1]
    count = len(steps)
    half = weight.shape[1] // 2
    shape = jax.ShapeDtypeStruct((count * rows, half), BF16)
    return pl.pallas_call(
        functools.partial(attend_kernel, nctx, back, steps, shard),
        out_shape=(shape, shape),
        in_specs=[SMEM] + [VMEM] * (2 * count + 2),
        out_specs=(VMEM, VMEM),
        scratch_shapes=[pltpu.VMEM((rows, width), BF16), pltpu.VMEM((rows, half), F32)],
        name="attend",
    )(scal, *queries, *residuals, kv, weight)


def project_kernel(jobs, nhalves, shard, scal, *refs):
    halves, (gain, weight), outs = refs[:nhalves], refs[nhalves : nhalves + 2], refs[nhalves + 2 :]
    ctx_index, mp_index = scal[0], scal[1]
    side = jnp.bitwise_and(mp_index, 1)
    channels = weight.shape[1]
    half = weight.shape[0] // 2
    gains, weights = [], []
    for which in (side, 1 - side):
        span = pl.multiple_of(which * half, half)
        gains.append(gain[:, pl.ds(pl.multiple_of(ctx_index * 2 * half + span, half), half)])
        weights.append(weight[pl.ds(span, half), :])
    ones = jnp.ones((SUB, half), BF16)

    def parts_of(source, last):
        (own_ref, other_ref), first, rows = source
        begin = first + rows - last if last else first
        stop = first + rows
        return own_ref[begin:stop, :].astype(F32), other_ref[begin:stop, :].astype(F32)

    def projected(parts):
        total = None
        for part, scale, matrix in zip(parts, gains, weights):
            term = jnp.dot((part * scale).astype(BF16), matrix, preferred_element_type=F32)
            total = term if total is None else total + term
        return total

    def squares(parts):
        total = None
        for part in parts:
            term = lax.dot_general(
                ones, (part * part).astype(BF16), (((1,), (1,)), ((), ())), preferred_element_type=F32
            )
            total = term if total is None else total + term
        return total

    at = 0
    for main, prior in jobs:
        sums = []
        if main is not None:
            source = ((halves[main[0]], halves[main[0] + 1]), main[1], main[2])
            rows = main[2]
            parts = parts_of(source, 0)
            outs[at][0:rows, :] = projected(parts).astype(BF16)
            sums = squares(parts)
            mine = pl.ds(pl.multiple_of(main[1] + mp_index * shard, TILE), shard)
            for which, ref in ((side, source[0][0]), (1 - side, source[0][1])):
                outs[at + 1][:, pl.ds(pl.multiple_of(which * half, half), half)] = ref[mine, :]
        if prior is not None:
            source = ((halves[prior[0]], halves[prior[0] + 1]), prior[1], prior[2])
            tail = projected(parts_of(source, TILE))[TILE - SUB :, :]
            tail_sums = squares(parts_of(source, LANES))
            line = outs[at]
            base = rows if main is not None else 0
            if main is None:
                own = ((halves[prior[3]], halves[prior[3] + 1]), prior[4], prior[5])
                sums = squares(parts_of(own, 0))
            spare = channels - sums.shape[1] - LANES
            pieces = [sums, tail_sums] + ([jnp.zeros((SUB, spare), F32)] if spare else [])
            sums = jnp.concatenate(pieces, axis=1)
            coarse = sums.astype(BF16).astype(F32)
            index = lax.broadcasted_iota(jnp.int32, sums.shape, 0)
            sums = jnp.where(index == 0, coarse, sums - coarse)
            line[base : base + TILE, :] = jnp.concatenate([sums, tail], axis=0).astype(BF16)
        at += 1 if main is None else 2


def project(scal, halves, gain, weight, jobs, shard):
    channels = weight.shape[1]
    shapes = []
    for main, prior in jobs:
        extra = TILE if prior is not None else 0
        shapes.append(jax.ShapeDtypeStruct(((main[2] if main else 0) + extra, channels), BF16))
        if main is not None:
            shapes.append(jax.ShapeDtypeStruct((shard, weight.shape[0]), BF16))
    return pl.pallas_call(
        functools.partial(project_kernel, jobs, len(halves), shard),
        out_shape=tuple(shapes),
        in_specs=[SMEM] + [VMEM] * (len(halves) + 2),
        out_specs=tuple([VMEM] * len(shapes)),
        name="project",
    )(scal, *halves, gain, weight)


def minus_expm1(x):
    series = jnp.full_like(x, 1.0 / 5040.0)
    for divisor in (720.0, 120.0, 24.0, 6.0, 2.0, 1.0):
        series = series * x + 1.0 / divisor
    return jnp.where(x > -0.3, -x * series, 1.0 - jnp.exp(x))


def recur_kernel(features, scal, *refs):
    count = (len(refs) - 12) // 2
    mains, lines = refs[:count], refs[count : 2 * count]
    conv_w, decay_w, input_w, decay_b, input_b, codes = refs[2 * count : 2 * count + 6]
    local_ref, cum_ref, last_ref, ext, keep_s, state_s = refs[2 * count + 6 :]
    rows = mains[0].shape[0]
    width = mains[0].shape[1]
    ctx_index, low, high = scal[0], scal[2], scal[3]
    stats = None
    for line in lines:
        both = line[:, : rows + LANES].astype(F32)
        term = both[0:1, :] + both[1:2, :]
        stats = term if stats is None else stats + term
    inverse = lax.rsqrt(stats * (1.0 / features) + 1e-06)
    inverse = jnp.transpose(jnp.broadcast_to(inverse, (LANES, rows + LANES)))[:, 0:1]
    lanes = pl.ds(pl.multiple_of(pl.program_id(0) * width, width), width)
    main = tail = None
    for piece, line in zip(mains, lines):
        term, tail_term = piece[...].astype(F32), line[:, lanes].astype(F32)[SUB:, :]
        main = term if main is None else main + term
        tail = tail_term if tail is None else tail + tail_term
    ext[0:SUB, :] = (tail * inverse[rows + LANES - SUB :, :]).astype(BF16).astype(F32)
    ext[SUB : SUB + rows, :] = (main * inverse[:rows, :]).astype(BF16).astype(F32)
    pos = ctx_index * rows + lax.broadcasted_iota(jnp.int32, (rows, 1), 0)
    start = segment_start(pos, low, high)
    conv = None
    for lag in range(CONV):
        shifted = ext[SUB - lag : SUB - lag + rows, :]
        term = jnp.where(pos - lag >= start, conv_w[lag : lag + 1, :] * shifted, 0.0)
        conv = term if conv is None else conv + term
    conv = conv.astype(BF16)
    gate_d = jax.nn.sigmoid(
        jnp.dot(conv, decay_w[0], preferred_element_type=F32) + decay_b[...]
    )
    gate_i = jax.nn.sigmoid(
        jnp.dot(conv, input_w[0], preferred_element_type=F32) + input_b[...]
    )
    rate = 0.006 * jnp.exp(-codes[...].astype(F32) * (math.log(3000.0) / (LEVELS - 1)))
    log_decay = -8.0 * gate_d * rate
    restart = pos == start
    keep = jnp.where(restart, 0.0, jnp.exp(log_decay))
    scale = jnp.where(restart, 1.0, jnp.sqrt(minus_expm1(2.0 * log_decay)))
    state = scale * gate_i * conv.astype(F32)
    tiles = rows // SUB
    keep = keep.reshape(tiles, SUB, width)
    state = state.reshape(tiles, SUB, width)
    index = lax.broadcasted_iota(jnp.int32, (tiles, SUB, width), 1)
    shift = 1
    while shift < SUB:
        inside = index >= shift
        prior_keep = jnp.where(inside, pltpu.roll(keep, shift, 1), 1.0)
        prior_state = jnp.where(inside, pltpu.roll(state, shift, 1), 0.0)
        state = keep * prior_state + state
        keep = keep * prior_keep
        shift *= 2
    keep_s[...] = keep
    state_s[...] = state
    run_keep = jnp.ones((1, width), F32)
    run_state = jnp.zeros((1, width), F32)
    for t in range(tiles):
        keep_t, state_t = keep_s[t], state_s[t]
        new_state = state_t + keep_t * run_state
        new_keep = keep_t * run_keep
        local_ref[t * SUB : (t + 1) * SUB, :] = new_state
        cum_ref[t * SUB : (t + 1) * SUB, :] = new_keep
        run_state, run_keep = new_state[SUB - 1 :, :], new_keep[SUB - 1 :, :]
    line = lax.broadcasted_iota(jnp.int32, (SUB, width), 0)
    last_ref[...] = jnp.where(line == 0, run_keep, run_state)


def recur(scal, mains, lines, conv_w, decay_w, input_w, decay_b, input_b, codes, rows, features):
    channels = conv_w.shape[1]
    tiles = rows // SUB
    by_block = pl.BlockSpec((rows, BW), lambda j: (0, j))
    row_spec = pl.BlockSpec((1, BW), lambda j: (0, j))
    gate_spec = pl.BlockSpec((1, BW, BW), lambda j: (j, 0, 0))
    line_specs = [
        pl.BlockSpec((TILE, channels), functools.partial(lambda at, j: (at, 0), at))
        for _, at in lines
    ]
    full = jax.ShapeDtypeStruct((rows, channels), F32)
    return pl.pallas_call(
        functools.partial(recur_kernel, features),
        grid=(channels // BW,),
        out_shape=(full, full, jax.ShapeDtypeStruct((SUB, channels), F32)),
        in_specs=[SMEM]
        + [by_block] * len(mains)
        + line_specs
        + [pl.BlockSpec((CONV, BW), lambda j: (0, j)), gate_spec, gate_spec]
        + [row_spec] * 3,
        out_specs=(by_block, by_block, pl.BlockSpec((SUB, BW), lambda j: (0, j))),
        scratch_shapes=[
            pltpu.VMEM((rows + SUB, BW), F32),
            pltpu.VMEM((tiles, SUB, BW), F32),
            pltpu.VMEM((tiles, SUB, BW), F32),
        ],
        name="recur",
    )(scal, *mains, *[line for line, _ in lines], conv_w, decay_w, input_w, decay_b, input_b, codes)


def local_near(
    queries,
    keyvals,
    segment_ids,
    residual,
    out_weight,
    lru_weight,
    conv_weight,
    gate_decay_w,
    gate_input_w,
    gate_decay_b,
    gate_input_b,
    decay_codes,
    norm_gain,
):
    rows = queries.shape[0]
    shard = keyvals.shape[0]
    tokens = segment_ids.shape[0]
    nctx, nmp = lax.axis_size("ctx"), lax.axis_size("mp")
    ctx_index, mp_index = lax.axis_index("ctx"), lax.axis_index("mp")
    features = residual.shape[1]
    longest = tokens // 2
    back = -(-(min(WIN, longest) - 1) // rows)
    reach = min(nctx - 1, -(-longest // rows))
    place = jnp.stack([ctx_index, mp_index]).astype(jnp.int32)

    kv_parts = [keyvals]
    for step in range(1, nctx):
        kv_parts.append(rotated(keyvals, "ctx", step))
    own_resid, *messages_out = pack(place, queries, residual, nctx)
    visiting = [queries]
    for step in range(1, nctx):
        visiting.append(rotated(messages_out[step - 1], "ctx", step))
    pieces = {0: jnp.concatenate(kv_parts, axis=0)}
    flip = nmp // 2
    while flip >= 1:
        for done in sorted(pieces):
            pieces[done | flip] = swapped(pieces[done], "mp", flip)
        flip //= 2
    kv = assemble(place, [pieces[e] for e in range(nmp)], rows, shard, nctx)
    low = jnp.sum((segment_ids < 1).astype(jnp.int32))
    high = jnp.sum((segment_ids < 2).astype(jnp.int32))
    scal = jnp.stack([ctx_index, mp_index, low, high]).astype(jnp.int32)

    chunks = [tuple(range(min(2, nctx)))] + [(step,) for step in range(2, nctx)]
    gain = norm_gain.reshape(1, features)
    where_is, chunk_halves = {}, []
    messages, resid_rows = {}, {}
    for at, steps in enumerate(chunks):
        keep, send = attend(
            scal,
            [visiting[s] for s in steps],
            [visiting[s] if s else own_resid for s in steps],
            kv,
            out_weight,
            nctx,
            back,
            steps,
            shard,
        )
        other = swapped(send, "mp", 1)
        mine = (keep.astype(F32) + other.astype(F32)).astype(BF16)
        flip = 2
        while flip < nmp:
            other = swapped(mine, "mp", flip)
            mine = (mine.astype(F32) + other.astype(F32)).astype(BF16)
            flip *= 2
        other = swapped(mine, "mp", 1)
        for j, s in enumerate(steps):
            where_is[s] = (at, j * rows, rows)
        chunk_halves.append((mine, other))
        ends = steps[-1] == nctx - 1
        used = sorted({where_is[s][0] for s in steps} | {where_is[s - 1][0] for s in steps if s} | ({0} if ends else set()))
        slot = {c: 2 * i for i, c in enumerate(used)}
        held = [piece for c in used for piece in chunk_halves[c]]

        def found(s):
            c, first, length = where_is[s]
            return (slot[c], first, length)

        jobs = [(found(s), found(s - 1) if s else None) for s in steps]
        if ends:
            jobs.append((None, found(nctx - 1) + found(0)))
        outs = project(scal, held, gain, lru_weight, jobs, shard)
        for j, s in enumerate(steps):
            messages[s], resid_rows[s] = outs[2 * j], outs[2 * j + 1]
        if ends:
            own_line = outs[2 * len(steps)]
    mains, lines = [messages[0]], [(own_line, 0)]
    for step in range(1, nctx):
        got = rotated(messages[step], "ctx", -step)
        mains.append(got)
        lines.append((got, rows // TILE))
    resid_parts = [resid_rows[0]]
    for step in range(1, nctx):
        resid_parts.append(rotated(resid_rows[step], "ctx", -step))
    local_state, cum_keep, last = recur(
        scal,
        mains,
        lines,
        conv_weight,
        gate_decay_w,
        gate_input_w,
        gate_decay_b.reshape(1, -1),
        gate_input_b.reshape(1, -1),
        decay_codes.reshape(1, -1),
        rows,
        features,
    )
    before = []
    for step in range(1, reach + 1):
        before.append(rotated(last, "ctx", -step))
    resid_out = join(place, resid_parts)
    incoming = jnp.zeros_like(last[0])
    for step in range(reach, 0, -1):
        piece = before[step - 1]
        incoming = jnp.where(ctx_index >= step, piece[0] * incoming + piece[1], 0.0)
    states = local_state + cum_keep * incoming[None, :]
    return (resid_out, states.astype(BF16))


def local(queries, keyvals, segment_ids, residual, out_weight, *rest):
    near = (
        segment_ids.shape[0] <= WIN
        and lax.axis_size("mp") % 2 == 0
        and queries.shape[1] == out_weight.shape[1]
    )
    form = local_near if near else local_wide
    return form(queries, keyvals, segment_ids, residual, out_weight, *rest)


def solution(mesh):
    in_specs = (
        P(("groups", "ctx"), "mp"),
        P(("groups", "ctx", "mp"), None),
        P("groups"),
        P(("groups", "ctx", "mp"), None),
        P("mp", "ctx"),
        P("ctx", "mp"),
        P(None, "mp"),
        P("mp", None, None),
        P("mp", None, None),
        P("mp"),
        P("mp"),
        P("mp"),
        P(),
    )
    out_specs = (P(("groups", "ctx", "mp"), None), P(("groups", "ctx"), "mp"))
    return jax.shard_map(local, mesh=mesh, in_specs=in_specs, out_specs=out_specs, check_vma=False)
```

```python
import functools
import math

import jax
import jax.numpy as jnp
from jax import lax
from jax.experimental import pallas as pl
from jax.experimental.pallas import tpu as pltpu
from jax.sharding import PartitionSpec as P

HD = 256
WIN = 2048
CONV = 4
LEVELS = 16
BW = 256


def shifted_2(value, axis, steps):
    count = lax.axis_size(axis)
    initial, last = (max(0, -steps), min(count, count - steps))
    return lax.ppermute(value, axis, [(source, source + steps) for source in range(initial, last)])


def decay_rates():
    levels = jnp.arange(LEVELS, dtype=jnp.float32)
    return 0.006 * jnp.exp(-levels * (math.log(3000.0) / (LEVELS - 1)))


def chain_link(former, latter):
    return (former[0] * latter[0], latter[0] * former[1] + latter[1])


def rms_scaled(values, norm_gain):
    value_f32 = values.astype(jnp.float32)
    inverse = lax.rsqrt(jnp.mean(value_f32 * value_f32, axis=-1, keepdims=True) + 1e-06)
    return (value_f32 * inverse * norm_gain).astype(jnp.bfloat16)


def attend_local(queries, keys_all, allowed):
    rows_here = queries.shape[0]
    heads_here = queries.shape[1] // HD
    query_heads = queries.reshape(rows_here, heads_here, HD)
    score_scale = 1.0 / math.sqrt(HD)
    scores = (
        jnp.einsum("thd,kd->htk", query_heads, keys_all[:, :HD], preferred_element_type=jnp.float32)
        * score_scale
    )
    scores = jnp.where(allowed[None], scores, -1e30)
    row_top = jnp.max(scores, axis=-1, keepdims=True)
    weights = jnp.exp(scores - row_top)
    probs = (weights / jnp.sum(weights, axis=-1, keepdims=True)).astype(jnp.bfloat16)
    gathered = jnp.einsum(
        "htk,kd->thd", probs, keys_all[:, HD:], preferred_element_type=jnp.float32
    )
    return gathered.reshape(rows_here, heads_here * HD).astype(jnp.bfloat16)


def local_wide(
    queries,
    keyvals,
    segment_ids,
    residual,
    out_weight,
    lru_weight,
    conv_weight,
    gate_decay_w,
    gate_input_w,
    gate_decay_b,
    gate_input_b,
    decay_codes,
    norm_gain,
):
    rows_here = queries.shape[0]
    ctx_index = lax.axis_index("ctx")
    back_blocks = WIN // rows_here
    own_kv = lax.all_gather(keyvals, "mp", axis=0, tiled=True)
    earlier = []
    moving = own_kv
    for _ in range(back_blocks):
        moving = shifted_2(moving, "ctx", 1)
        earlier = [moving] + earlier
    keys_all = jnp.concatenate(earlier + [own_kv], axis=0)
    pad_seg = jnp.concatenate([jnp.full((WIN,), -1, jnp.int32), segment_ids])
    query_seg = lax.dynamic_slice_in_dim(segment_ids, ctx_index * rows_here, rows_here)
    key_seg = lax.dynamic_slice_in_dim(
        pad_seg, ctx_index * rows_here, (back_blocks + 1) * rows_here
    )
    query_pos = ctx_index * rows_here + jnp.arange(rows_here, dtype=jnp.int32)
    key_pos = (ctx_index - back_blocks) * rows_here + jnp.arange(
        (back_blocks + 1) * rows_here, dtype=jnp.int32
    )
    distance = query_pos[:, None] - key_pos[None, :]
    allowed = (distance >= 0) & (distance < WIN) & (query_seg[:, None] == key_seg[None, :])
    attended = attend_local(queries, keys_all, allowed)
    head_part = jnp.dot(
        attended,
        lax.all_gather(out_weight, "ctx", axis=1, tiled=True),
        preferred_element_type=jnp.float32,
    )
    summed = lax.psum_scatter(
        head_part.astype(jnp.bfloat16), "mp", scatter_dimension=0, tiled=True
    ).astype(jnp.float32)
    resid_out = (summed + residual.astype(jnp.float32)).astype(jnp.bfloat16)
    normed = lax.all_gather(rms_scaled(resid_out, norm_gain), "mp", axis=0, tiled=True)
    channels = lru_weight.shape[1]
    lru_in = jnp.dot(
        normed,
        lax.all_gather(lru_weight, "ctx", axis=0, tiled=True),
        preferred_element_type=jnp.float32,
    ).astype(jnp.bfloat16)
    rim_rows = shifted_2(lru_in[rows_here - (CONV - 1) :], "ctx", 1)
    extended = jnp.concatenate([rim_rows, lru_in], axis=0)
    ext_seg = lax.dynamic_slice_in_dim(
        pad_seg, ctx_index * rows_here + WIN - (CONV - 1), rows_here + CONV - 1
    )
    conv_acc = jnp.zeros((rows_here, channels), jnp.float32)
    for offset in range(CONV):
        lag_rows = CONV - 1 - offset
        shifted = extended[lag_rows : lag_rows + rows_here].astype(jnp.float32)
        same_doc = (ext_seg[lag_rows : lag_rows + rows_here] == query_seg)[:, None]
        conv_acc = conv_acc + jnp.where(same_doc, conv_weight[offset] * shifted, 0.0)
    conv_out = conv_acc.astype(jnp.bfloat16)
    blocks_here = channels // BW
    grouped = conv_out.reshape(rows_here, blocks_here, BW)
    decay_gate = jax.nn.sigmoid(
        jnp.einsum(
            "tbi,bij->tbj", grouped, gate_decay_w, preferred_element_type=jnp.float32
        ).reshape(rows_here, channels)
        + gate_decay_b
    )
    input_gate = jax.nn.sigmoid(
        jnp.einsum(
            "tbi,bij->tbj", grouped, gate_input_w, preferred_element_type=jnp.float32
        ).reshape(rows_here, channels)
        + gate_input_b
    )
    levels = jnp.arange(LEVELS, dtype=jnp.int32)
    decay_rate = jnp.sum(
        jnp.where(decay_codes[:, None] == levels[None, :], decay_rates()[None, :], 0.0), axis=1
    )
    log_decay = -8.0 * decay_gate * decay_rate
    restart = (query_seg != ext_seg[CONV - 2 : CONV - 2 + rows_here])[:, None]
    keep_factor = jnp.where(restart, 0.0, jnp.exp(log_decay))
    input_scale = jnp.where(restart, 1.0, jnp.sqrt(-jnp.expm1(2.0 * log_decay)))
    driven = input_scale * input_gate * conv_out.astype(jnp.float32)
    cum_keep, local_state = lax.associative_scan(chain_link, (keep_factor, driven), axis=0)
    block_keep = cum_keep[rows_here - 1]
    block_state = local_state[rows_here - 1]

    def relay_turn(turn_index, state_in):
        return shifted_2(block_keep * state_in + block_state, "ctx", 1)

    incoming = lax.fori_loop(0, lax.axis_size("ctx") - 1, relay_turn, jnp.zeros_like(block_state))
    states = local_state + cum_keep * incoming[None, :]
    return (resid_out, states.astype(jnp.bfloat16))


F32 = jnp.float32
BF16 = jnp.bfloat16
VMEM = pl.BlockSpec(memory_space=pltpu.VMEM)
SMEM = pl.BlockSpec(memory_space=pltpu.SMEM)
TILE = 16
SUB = 8
LANES = 128
GRANT = 20 << 20


def rotated(value, axis, steps):
    count = lax.axis_size(axis)
    return lax.ppermute(value, axis, [(s, (s - steps) % count) for s in range(count)])


def swapped(value, axis, flip):
    count = lax.axis_size(axis)
    return lax.ppermute(value, axis, [(s, s ^ flip) for s in range(count)])


def segment_start(pos, low, high):
    return jnp.where(pos >= high, high, jnp.where(pos >= low, low, 0))


def pack_kernel(scal, residual, *outs):
    cols = outs[0].shape[1]
    for flip, out in enumerate(outs):
        block = jnp.bitwise_xor(scal[0], flip)
        out[...] = residual[:, pl.ds(pl.multiple_of(block * cols, cols), cols)]


def pack(scal, residual, nctx):
    shard, width = residual.shape
    part = jax.ShapeDtypeStruct((shard, width // nctx), BF16)
    return pl.pallas_call(
        pack_kernel,
        out_shape=(part,) * nctx,
        in_specs=[SMEM, VMEM],
        out_specs=(VMEM,) * nctx,
        name="pack",
        compiler_params=pltpu.CompilerParams(vmem_limit_bytes=GRANT),
    )(scal, residual)


def join_kernel(scal, *refs):
    out = refs[-1]
    cols = refs[0].shape[1]
    for flip, part in enumerate(refs[:-1]):
        block = jnp.bitwise_xor(scal[0], flip)
        out[:, pl.ds(pl.multiple_of(block * cols, cols), cols)] = part[...]


def join(scal, parts):
    nctx = len(parts)
    shard, cols = parts[0].shape
    return pl.pallas_call(
        join_kernel,
        out_shape=jax.ShapeDtypeStruct((shard, nctx * cols), BF16),
        in_specs=[SMEM] + [VMEM] * nctx,
        out_specs=VMEM,
        name="join",
        compiler_params=pltpu.CompilerParams(vmem_limit_bytes=GRANT),
    )(scal, *parts)


def assemble_kernel(rows, shard, nctx, scal, *refs):
    out = refs[-1]
    ctx_index, mp_index = scal[0], scal[1]
    for flip, piece in enumerate(refs[:-1]):
        member = jnp.bitwise_xor(mp_index, flip)
        for step in range(nctx):
            block = jnp.bitwise_xor(ctx_index, step)
            first = pl.multiple_of(block * rows + member * shard, shard)
            out[pl.ds(first, shard), :] = piece[step * shard : (step + 1) * shard, :]


def assemble(scal, pieces, rows, shard, nctx):
    tokens = nctx * rows
    width = pieces[0].shape[1]
    return pl.pallas_call(
        functools.partial(assemble_kernel, rows, shard, nctx),
        out_shape=jax.ShapeDtypeStruct((tokens, width), BF16),
        in_specs=[SMEM] + [VMEM] * len(pieces),
        out_specs=VMEM,
        name="assemble",
        compiler_params=pltpu.CompilerParams(vmem_limit_bytes=GRANT),
    )(scal, *pieces)


def attend_kernel(nctx, back, steps, shard, scal, *refs):
    count = len(steps)
    q_refs, resid_refs = refs[:count], refs[count : 2 * count]
    kv, weight, keep, send, att, acc = refs[2 * count :]
    rows, width = att.shape
    heads = width // HD
    half = weight.shape[1] // 2
    ctx_index, mp_index, low, high = scal[0], scal[1], scal[2], scal[3]
    side = jnp.bitwise_and(mp_index, 1)
    window = min(back + 1, nctx) * rows
    scale = 1.0 / math.sqrt(HD)
    for j, step in enumerate(steps):
        block = jnp.bitwise_xor(ctx_index, step)
        first_key = pl.multiple_of(
            jnp.minimum(jnp.maximum(block - back, 0), nctx - window // rows) * rows, rows
        )
        qpos = block * rows + lax.broadcasted_iota(jnp.int32, (rows, 1), 0)
        start = segment_start(qpos, low, high)
        kpos = first_key + lax.broadcasted_iota(jnp.int32, (1, window), 1)
        allowed = (kpos <= qpos) & (kpos >= start) & (qpos - kpos < WIN)
        for h in range(heads):
            query = q_refs[j][:, h * HD : (h + 1) * HD]
            keys = kv[pl.ds(first_key, window), :HD]
            scores = lax.dot_general(
                query, keys, (((1,), (1,)), ((), ())), preferred_element_type=F32
            )
            scores = jnp.where(allowed, scores * scale, -1e30)
            top = jnp.max(scores, axis=1, keepdims=True)
            weights = jnp.exp(scores - top)
            total = jnp.sum(weights, axis=1, keepdims=True)
            values = kv[pl.ds(first_key, window), HD:]
            gathered = jnp.dot(weights.astype(BF16), values, preferred_element_type=F32)
            att[:, h * HD : (h + 1) * HD] = (gathered / total).astype(BF16)
        own = pl.ds(pl.multiple_of(mp_index * shard, shard), shard)
        for out, which in ((send, 1 - side), (keep, side)):
            cols = pl.ds(pl.multiple_of(which * half, half), half)
            acc[...] = jnp.dot(att[...], weight[:, cols], preferred_element_type=F32)
            acc[own, :] += resid_refs[j][:, cols].astype(F32)
            out[j * rows : (j + 1) * rows, :] = acc[...].astype(BF16)


def attend(scal, queries, residuals, kv, weight, nctx, back, steps, shard):
    rows, width = kv.shape[0] // nctx, queries[0].shape[1]
    count = len(steps)
    half = weight.shape[1] // 2
    shape = jax.ShapeDtypeStruct((count * rows, half), BF16)
    return pl.pallas_call(
        functools.partial(attend_kernel, nctx, back, steps, shard),
        out_shape=(shape, shape),
        in_specs=[SMEM] + [VMEM] * (2 * count + 2),
        out_specs=(VMEM, VMEM),
        scratch_shapes=[pltpu.VMEM((rows, width), BF16), pltpu.VMEM((rows, half), F32)],
        name="attend",
        compiler_params=pltpu.CompilerParams(vmem_limit_bytes=GRANT),
    )(scal, *queries, *residuals, kv, weight)


def split_weights(gain, weight, ctx_index, side):
    half = weight.shape[0] // 2
    out = []
    for which in (side, 1 - side):
        span = pl.multiple_of(which * half, half)
        cols = pl.ds(pl.multiple_of(ctx_index * 2 * half + span, half), half)
        out.append((gain[:, cols], weight[pl.ds(span, half), :]))
    return out


def project_kernel(count, scal, own, other, gain, weight, *outs):
    ctx_index, mp_index = scal[0], scal[1]
    side = jnp.bitwise_and(mp_index, 1)
    rows = own.shape[0] // count
    half = weight.shape[0] // 2
    shard = outs[1].shape[0]
    (gain_own, weight_own), (gain_other, weight_other) = split_weights(gain, weight, ctx_index, side)
    for j in range(count):
        span = slice(j * rows, (j + 1) * rows)
        scaled_own = (own[span, :].astype(F32) * gain_own).astype(BF16)
        scaled_other = (other[span, :].astype(F32) * gain_other).astype(BF16)
        outs[2 * j][...] = (
            jnp.dot(scaled_own, weight_own, preferred_element_type=F32)
            + jnp.dot(scaled_other, weight_other, preferred_element_type=F32)
        ).astype(BF16)
        mine = pl.ds(pl.multiple_of(j * rows + mp_index * shard, TILE), shard)
        for which, ref in ((side, own), (1 - side, other)):
            outs[2 * j + 1][:, pl.ds(pl.multiple_of(which * half, half), half)] = ref[mine, :]


def project(scal, own, other, gain, weight, count, shard):
    rows = own.shape[0] // count
    features, channels = weight.shape
    shapes = []
    for _ in range(count):
        shapes.append(jax.ShapeDtypeStruct((rows, channels), BF16))
        shapes.append(jax.ShapeDtypeStruct((shard, features), BF16))
    return pl.pallas_call(
        functools.partial(project_kernel, count),
        out_shape=tuple(shapes),
        in_specs=[SMEM] + [VMEM] * 4,
        out_specs=(VMEM,) * len(shapes),
        name="project",
        compiler_params=pltpu.CompilerParams(vmem_limit_bytes=GRANT),
    )(scal, own, other, gain, weight)


def tails_kernel(places, nhalves, rows, scal, *refs):
    nctx = len(places)
    halves, (gain, weight) = refs[:nhalves], refs[nhalves : nhalves + 2]
    outs = refs[nhalves + 2 : nhalves + 2 + nctx]
    edges, ends = refs[nhalves + 2 + nctx :]
    ctx_index = scal[0]
    side = jnp.bitwise_and(scal[1], 1)
    channels = weight.shape[1]
    half = weight.shape[0] // 2
    split = split_weights(gain, weight, ctx_index, side)
    ones = jnp.ones((SUB, half), BF16)

    def squares(piece):
        value = piece.astype(F32)
        return lax.dot_general(
            ones, (value * value).astype(BF16), (((1,), (1,)), ((), ())), preferred_element_type=F32
        )

    for flip, (at, first) in enumerate(places):
        block = jnp.bitwise_xor(ctx_index, flip)
        for k in range(2):
            piece = halves[2 * at + k][first + rows - LANES : first + rows, :]
            edges[k, pl.ds(pl.multiple_of(block * LANES, LANES), LANES), :] = piece
    sums = []
    for flip, (at, first) in enumerate(places):
        before = lax.rem(jnp.bitwise_xor(ctx_index, flip) + nctx - 1, nctx)
        main = edge = None
        for k in range(2):
            part = edges[k, pl.ds(pl.multiple_of(before * LANES, LANES), LANES), :]
            ends[k, flip * TILE : (flip + 1) * TILE, :] = part[LANES - TILE :, :]
            term, edge_term = squares(halves[2 * at + k][first : first + rows, :]), squares(part)
            main = term if main is None else main + term
            edge = edge_term if edge is None else edge + edge_term
        sums.append((main, edge))
    tails = None
    for k, (scale, matrix) in enumerate(split):
        term = jnp.dot(
            (ends[k].astype(F32) * scale).astype(BF16), matrix, preferred_element_type=F32
        )
        tails = term if tails is None else tails + term
    spare = channels - rows - LANES
    for flip, (main, edge) in enumerate(sums):
        pieces = [main, edge] + ([jnp.zeros((SUB, spare), F32)] if spare else [])
        line = jnp.concatenate(pieces, axis=1)
        coarse = line.astype(BF16).astype(F32)
        index = lax.broadcasted_iota(jnp.int32, line.shape, 0)
        line = jnp.where(index == 0, coarse, line - coarse)
        tail = tails[(flip + 1) * TILE - SUB : (flip + 1) * TILE, :]
        outs[flip][...] = jnp.concatenate([line, tail], axis=0).astype(BF16)


def tails(scal, halves, places, gain, weight, rows):
    nctx = len(places)
    half, channels = weight.shape[0] // 2, weight.shape[1]
    return pl.pallas_call(
        functools.partial(tails_kernel, places, len(halves), rows),
        out_shape=(jax.ShapeDtypeStruct((TILE, channels), BF16),) * nctx,
        in_specs=[SMEM] + [VMEM] * (len(halves) + 2),
        out_specs=(VMEM,) * nctx,
        scratch_shapes=[
            pltpu.VMEM((2, nctx * LANES, half), BF16),
            pltpu.VMEM((2, nctx * TILE, half), BF16),
        ],
        name="tails",
        compiler_params=pltpu.CompilerParams(vmem_limit_bytes=GRANT),
    )(scal, *halves, gain, weight)


def minus_expm1(x):
    series = jnp.full_like(x, 1.0 / 5040.0)
    for divisor in (720.0, 120.0, 24.0, 6.0, 2.0, 1.0):
        series = series * x + 1.0 / divisor
    return jnp.where(x > -0.3, -x * series, 1.0 - jnp.exp(x))


def stats_kernel(features, *refs):
    lines, (factor_ref, ahead_ref) = refs[:-2], refs[-2:]
    length = factor_ref.shape[0]
    sums = tail = None
    for line in lines:
        term = line[0:1, :length].astype(F32) + line[1:2, :length].astype(F32)
        tail_term = line[...].astype(F32)[SUB:, :]
        sums = term if sums is None else sums + term
        tail = tail_term if tail is None else tail + tail_term
    factor = lax.rsqrt(sums * (1.0 / features) + 1e-06)
    factor = jnp.transpose(jnp.broadcast_to(factor, (LANES, length)))
    factor_ref[...] = factor
    ahead_ref[...] = (tail * factor[length - SUB :, 0:1]).astype(BF16).astype(F32)


def stats(lines, rows, features):
    channels = lines[0].shape[1]
    return pl.pallas_call(
        functools.partial(stats_kernel, features),
        out_shape=(
            jax.ShapeDtypeStruct((rows + LANES, LANES), F32),
            jax.ShapeDtypeStruct((SUB, channels), F32),
        ),
        in_specs=[VMEM] * len(lines),
        out_specs=(VMEM, VMEM),
        name="stats",
        compiler_params=pltpu.CompilerParams(vmem_limit_bytes=GRANT),
    )(*lines)


def recur_kernel(count, scal, *refs):
    mains, (factor, ahead) = refs[:count], refs[count : count + 2]
    conv_w, decay_w, input_w, decay_b, input_b, codes = refs[count + 2 : count + 8]
    local_ref, cum_ref, last_ref, ext, keep_s, state_s = refs[count + 8 :]
    rows = mains[0].shape[0]
    width = mains[0].shape[1]
    ctx_index, low, high = scal[0], scal[2], scal[3]
    main = None
    for piece in mains:
        term = piece[...].astype(F32)
        main = term if main is None else main + term
    ext[0:SUB, :] = ahead[...]
    ext[SUB : SUB + rows, :] = (main * factor[:rows, 0:1]).astype(BF16).astype(F32)
    pos = ctx_index * rows + lax.broadcasted_iota(jnp.int32, (rows, 1), 0)
    start = segment_start(pos, low, high)
    conv = None
    for lag in range(CONV):
        shifted = ext[SUB - lag : SUB - lag + rows, :]
        term = jnp.where(pos - lag >= start, conv_w[lag : lag + 1, :] * shifted, 0.0)
        conv = term if conv is None else conv + term
    conv = conv.astype(BF16)
    gate_d = jax.nn.sigmoid(
        jnp.dot(conv, decay_w[0], preferred_element_type=F32) + decay_b[...]
    )
    gate_i = jax.nn.sigmoid(
        jnp.dot(conv, input_w[0], preferred_element_type=F32) + input_b[...]
    )
    rate = 0.006 * jnp.exp(-codes[...].astype(F32) * (math.log(3000.0) / (LEVELS - 1)))
    log_decay = -8.0 * gate_d * rate
    restart = pos == start
    keep = jnp.where(restart, 0.0, jnp.exp(log_decay))
    scale = jnp.where(restart, 1.0, jnp.sqrt(minus_expm1(2.0 * log_decay)))
    state = scale * gate_i * conv.astype(F32)
    tiles = rows // SUB
    keep = keep.reshape(tiles, SUB, width)
    state = state.reshape(tiles, SUB, width)
    index = lax.broadcasted_iota(jnp.int32, (tiles, SUB, width), 1)
    shift = 1
    while shift < SUB:
        inside = index >= shift
        prior_keep = jnp.where(inside, pltpu.roll(keep, shift, 1), 1.0)
        prior_state = jnp.where(inside, pltpu.roll(state, shift, 1), 0.0)
        state = keep * prior_state + state
        keep = keep * prior_keep
        shift *= 2
    keep_s[...] = keep
    state_s[...] = state
    run_keep = jnp.ones((1, width), F32)
    run_state = jnp.zeros((1, width), F32)
    for t in range(tiles):
        keep_t, state_t = keep_s[t], state_s[t]
        new_state = state_t + keep_t * run_state
        new_keep = keep_t * run_keep
        local_ref[t * SUB : (t + 1) * SUB, :] = new_state
        cum_ref[t * SUB : (t + 1) * SUB, :] = new_keep
        run_state, run_keep = new_state[SUB - 1 :, :], new_keep[SUB - 1 :, :]
    line = lax.broadcasted_iota(jnp.int32, (SUB, width), 0)
    last_ref[...] = jnp.where(line == 0, run_keep, run_state)


def recur(scal, mains, factor, ahead, conv_w, decay_w, input_w, decay_b, input_b, codes, rows):
    channels = conv_w.shape[1]
    tiles = rows // SUB
    by_block = pl.BlockSpec((rows, BW), lambda j: (0, j))
    row_spec = pl.BlockSpec((1, BW), lambda j: (0, j))
    gate_spec = pl.BlockSpec((1, BW, BW), lambda j: (j, 0, 0))
    factor_spec = pl.BlockSpec(factor.shape, lambda j: (0, 0))
    ahead_spec = pl.BlockSpec((SUB, BW), lambda j: (0, j))
    full = jax.ShapeDtypeStruct((rows, channels), F32)
    return pl.pallas_call(
        functools.partial(recur_kernel, len(mains)),
        grid=(channels // BW,),
        out_shape=(full, full, jax.ShapeDtypeStruct((SUB, channels), F32)),
        in_specs=[SMEM]
        + [by_block] * len(mains)
        + [factor_spec, ahead_spec]
        + [pl.BlockSpec((CONV, BW), lambda j: (0, j)), gate_spec, gate_spec]
        + [row_spec] * 3,
        out_specs=(by_block, by_block, pl.BlockSpec((SUB, BW), lambda j: (0, j))),
        scratch_shapes=[
            pltpu.VMEM((rows + SUB, BW), F32),
            pltpu.VMEM((tiles, SUB, BW), F32),
            pltpu.VMEM((tiles, SUB, BW), F32),
        ],
        name="recur",
        compiler_params=pltpu.CompilerParams(vmem_limit_bytes=GRANT),
    )(scal, *mains, factor, ahead, conv_w, decay_w, input_w, decay_b, input_b, codes)


def local_near(
    queries,
    keyvals,
    segment_ids,
    residual,
    out_weight,
    lru_weight,
    conv_weight,
    gate_decay_w,
    gate_input_w,
    gate_decay_b,
    gate_input_b,
    decay_codes,
    norm_gain,
):
    rows = queries.shape[0]
    shard = keyvals.shape[0]
    tokens = segment_ids.shape[0]
    nctx, nmp = lax.axis_size("ctx"), lax.axis_size("mp")
    ctx_index, mp_index = lax.axis_index("ctx"), lax.axis_index("mp")
    features = residual.shape[1]
    longest = tokens // 2
    back = -(-(min(WIN, longest) - 1) // rows)
    reach = min(nctx - 1, -(-longest // rows))
    place = jnp.stack([ctx_index, mp_index]).astype(jnp.int32)

    visiting = {0: queries}
    for flip in range(nctx - 1, 0, -2):
        visiting[flip] = swapped(queries, "ctx", flip)
    for flip in range(nctx - 2, 0, -2):
        visiting[flip] = swapped(visiting[flip + 1], "ctx", 1)
    kv_parts = [keyvals]
    for flip in range(1, nctx):
        kv_parts.append(swapped(keyvals, "ctx", flip))
    resid_parts = list(pack(place, residual, nctx))
    for flip in range(1, nctx):
        resid_parts[flip] = swapped(resid_parts[flip], "ctx", flip)
    pieces = {0: jnp.concatenate(kv_parts, axis=0)}
    flip = nmp // 2
    while flip >= 1:
        for done in sorted(pieces):
            pieces[done | flip] = swapped(pieces[done], "mp", flip)
        flip //= 2
    kv = assemble(place, [pieces[e] for e in range(nmp)], rows, shard, nctx)
    low = jnp.sum((segment_ids < 1).astype(jnp.int32))
    high = jnp.sum((segment_ids < 2).astype(jnp.int32))
    scal = jnp.stack([ctx_index, mp_index, low, high]).astype(jnp.int32)

    chunks = [(0,)] + [(nctx - 1,)] + ([tuple(range(1, nctx - 1))] if nctx > 2 else [])
    gain = norm_gain.reshape(1, features)
    halves, places = [], {}
    messages, give = {}, {}
    for at, flips in enumerate(chunks):
        keep, send = attend(
            scal,
            [visiting[e] for e in flips],
            [resid_parts[e] for e in flips],
            kv,
            out_weight,
            nctx,
            back,
            flips,
            shard,
        )
        other = swapped(send, "mp", 1)
        mine = (keep.astype(F32) + other.astype(F32)).astype(BF16)
        flip = 2
        while flip < nmp:
            other = swapped(mine, "mp", flip)
            mine = (mine.astype(F32) + other.astype(F32)).astype(BF16)
            flip *= 2
        other = swapped(mine, "mp", 1)
        halves += [mine, other]
        outs = project(scal, mine, other, gain, lru_weight, len(flips), shard)
        for j, e in enumerate(flips):
            places[e] = (at, j * rows)
            messages[e], give[e] = outs[2 * j], outs[2 * j + 1]
    lines = list(tails(scal, halves, [places[e] for e in range(nctx)], gain, lru_weight, rows))
    mains = [messages[0]]
    for flip in range(1, nctx):
        mains.append(swapped(messages[flip], "ctx", flip))
        lines[flip] = swapped(lines[flip], "ctx", flip)
    factor, ahead = stats(lines, rows, features)
    given = [give[0]]
    for flip in range(1, nctx):
        given.append(swapped(give[flip], "ctx", flip))
    local_state, cum_keep, last = recur(
        scal,
        mains,
        factor,
        ahead,
        conv_weight,
        gate_decay_w,
        gate_input_w,
        gate_decay_b.reshape(1, -1),
        gate_input_b.reshape(1, -1),
        decay_codes.reshape(1, -1),
        rows,
    )
    before = []
    for step in range(1, reach + 1):
        before.append(rotated(last, "ctx", -step))
    resid_out = join(place, given)
    incoming = jnp.zeros_like(last[0])
    for step in range(reach, 0, -1):
        piece = before[step - 1]
        incoming = jnp.where(ctx_index >= step, piece[0] * incoming + piece[1], 0.0)
    states = local_state + cum_keep * incoming[None, :]
    return (resid_out, states.astype(BF16))


def local(queries, keyvals, segment_ids, residual, out_weight, *rest):
    nctx = lax.axis_size("ctx")
    near = (
        segment_ids.shape[0] <= WIN
        and nctx & (nctx - 1) == 0
        and lax.axis_size("mp") % 2 == 0
        and queries.shape[1] == out_weight.shape[1]
    )
    form = local_near if near else local_wide
    return form(queries, keyvals, segment_ids, residual, out_weight, *rest)


def solution(mesh):
    in_specs = (
        P(("groups", "ctx"), "mp"),
        P(("groups", "ctx", "mp"), None),
        P("groups"),
        P(("groups", "ctx", "mp"), None),
        P("mp", "ctx"),
        P("ctx", "mp"),
        P(None, "mp"),
        P("mp", None, None),
        P("mp", None, None),
        P("mp"),
        P("mp"),
        P("mp"),
        P(),
    )
    out_specs = (P(("groups", "ctx", "mp"), None), P(("groups", "ctx"), "mp"))
    return jax.shard_map(local, mesh=mesh, in_specs=in_specs, out_specs=out_specs, check_vma=False)
```

```python
import functools
import math

import jax
import jax.numpy as jnp
from jax import lax
from jax.experimental import pallas as pl
from jax.experimental.pallas import tpu as pltpu
from jax.sharding import PartitionSpec as P

HD = 256
WIN = 2048
CONV = 4
LEVELS = 16
BW = 256


def shifted_2(value, axis, steps):
    count = lax.axis_size(axis)
    initial, last = (max(0, -steps), min(count, count - steps))
    return lax.ppermute(value, axis, [(source, source + steps) for source in range(initial, last)])


def decay_rates():
    levels = jnp.arange(LEVELS, dtype=jnp.float32)
    return 0.006 * jnp.exp(-levels * (math.log(3000.0) / (LEVELS - 1)))


def chain_link(former, latter):
    return (former[0] * latter[0], latter[0] * former[1] + latter[1])


def rms_scaled(values, norm_gain):
    value_f32 = values.astype(jnp.float32)
    inverse = lax.rsqrt(jnp.mean(value_f32 * value_f32, axis=-1, keepdims=True) + 1e-06)
    return (value_f32 * inverse * norm_gain).astype(jnp.bfloat16)


def attend_local(queries, keys_all, allowed):
    rows_here = queries.shape[0]
    heads_here = queries.shape[1] // HD
    query_heads = queries.reshape(rows_here, heads_here, HD)
    score_scale = 1.0 / math.sqrt(HD)
    scores = (
        jnp.einsum("thd,kd->htk", query_heads, keys_all[:, :HD], preferred_element_type=jnp.float32)
        * score_scale
    )
    scores = jnp.where(allowed[None], scores, -1e30)
    row_top = jnp.max(scores, axis=-1, keepdims=True)
    weights = jnp.exp(scores - row_top)
    probs = (weights / jnp.sum(weights, axis=-1, keepdims=True)).astype(jnp.bfloat16)
    gathered = jnp.einsum(
        "htk,kd->thd", probs, keys_all[:, HD:], preferred_element_type=jnp.float32
    )
    return gathered.reshape(rows_here, heads_here * HD).astype(jnp.bfloat16)


def local_wide(
    queries,
    keyvals,
    segment_ids,
    residual,
    out_weight,
    lru_weight,
    conv_weight,
    gate_decay_w,
    gate_input_w,
    gate_decay_b,
    gate_input_b,
    decay_codes,
    norm_gain,
):
    rows_here = queries.shape[0]
    ctx_index = lax.axis_index("ctx")
    back_blocks = WIN // rows_here
    own_kv = lax.all_gather(keyvals, "mp", axis=0, tiled=True)
    earlier = []
    moving = own_kv
    for _ in range(back_blocks):
        moving = shifted_2(moving, "ctx", 1)
        earlier = [moving] + earlier
    keys_all = jnp.concatenate(earlier + [own_kv], axis=0)
    pad_seg = jnp.concatenate([jnp.full((WIN,), -1, jnp.int32), segment_ids])
    query_seg = lax.dynamic_slice_in_dim(segment_ids, ctx_index * rows_here, rows_here)
    key_seg = lax.dynamic_slice_in_dim(
        pad_seg, ctx_index * rows_here, (back_blocks + 1) * rows_here
    )
    query_pos = ctx_index * rows_here + jnp.arange(rows_here, dtype=jnp.int32)
    key_pos = (ctx_index - back_blocks) * rows_here + jnp.arange(
        (back_blocks + 1) * rows_here, dtype=jnp.int32
    )
    distance = query_pos[:, None] - key_pos[None, :]
    allowed = (distance >= 0) & (distance < WIN) & (query_seg[:, None] == key_seg[None, :])
    attended = attend_local(queries, keys_all, allowed)
    head_part = jnp.dot(
        attended,
        lax.all_gather(out_weight, "ctx", axis=1, tiled=True),
        preferred_element_type=jnp.float32,
    )
    summed = lax.psum_scatter(
        head_part.astype(jnp.bfloat16), "mp", scatter_dimension=0, tiled=True
    ).astype(jnp.float32)
    resid_out = (summed + residual.astype(jnp.float32)).astype(jnp.bfloat16)
    normed = lax.all_gather(rms_scaled(resid_out, norm_gain), "mp", axis=0, tiled=True)
    channels = lru_weight.shape[1]
    lru_in = jnp.dot(
        normed,
        lax.all_gather(lru_weight, "ctx", axis=0, tiled=True),
        preferred_element_type=jnp.float32,
    ).astype(jnp.bfloat16)
    rim_rows = shifted_2(lru_in[rows_here - (CONV - 1) :], "ctx", 1)
    extended = jnp.concatenate([rim_rows, lru_in], axis=0)
    ext_seg = lax.dynamic_slice_in_dim(
        pad_seg, ctx_index * rows_here + WIN - (CONV - 1), rows_here + CONV - 1
    )
    conv_acc = jnp.zeros((rows_here, channels), jnp.float32)
    for offset in range(CONV):
        lag_rows = CONV - 1 - offset
        shifted = extended[lag_rows : lag_rows + rows_here].astype(jnp.float32)
        same_doc = (ext_seg[lag_rows : lag_rows + rows_here] == query_seg)[:, None]
        conv_acc = conv_acc + jnp.where(same_doc, conv_weight[offset] * shifted, 0.0)
    conv_out = conv_acc.astype(jnp.bfloat16)
    blocks_here = channels // BW
    grouped = conv_out.reshape(rows_here, blocks_here, BW)
    decay_gate = jax.nn.sigmoid(
        jnp.einsum(
            "tbi,bij->tbj", grouped, gate_decay_w, preferred_element_type=jnp.float32
        ).reshape(rows_here, channels)
        + gate_decay_b
    )
    input_gate = jax.nn.sigmoid(
        jnp.einsum(
            "tbi,bij->tbj", grouped, gate_input_w, preferred_element_type=jnp.float32
        ).reshape(rows_here, channels)
        + gate_input_b
    )
    levels = jnp.arange(LEVELS, dtype=jnp.int32)
    decay_rate = jnp.sum(
        jnp.where(decay_codes[:, None] == levels[None, :], decay_rates()[None, :], 0.0), axis=1
    )
    log_decay = -8.0 * decay_gate * decay_rate
    restart = (query_seg != ext_seg[CONV - 2 : CONV - 2 + rows_here])[:, None]
    keep_factor = jnp.where(restart, 0.0, jnp.exp(log_decay))
    input_scale = jnp.where(restart, 1.0, jnp.sqrt(-jnp.expm1(2.0 * log_decay)))
    driven = input_scale * input_gate * conv_out.astype(jnp.float32)
    cum_keep, local_state = lax.associative_scan(chain_link, (keep_factor, driven), axis=0)
    block_keep = cum_keep[rows_here - 1]
    block_state = local_state[rows_here - 1]

    def relay_turn(turn_index, state_in):
        return shifted_2(block_keep * state_in + block_state, "ctx", 1)

    incoming = lax.fori_loop(0, lax.axis_size("ctx") - 1, relay_turn, jnp.zeros_like(block_state))
    states = local_state + cum_keep * incoming[None, :]
    return (resid_out, states.astype(jnp.bfloat16))


F32 = jnp.float32
BF16 = jnp.bfloat16
VMEM = pl.BlockSpec(memory_space=pltpu.VMEM)
SMEM = pl.BlockSpec(memory_space=pltpu.SMEM)
TILE = 16
SUB = 8
LANES = 128
GRANT = 20 << 20


def rotated(value, axis, steps):
    count = lax.axis_size(axis)
    return lax.ppermute(value, axis, [(s, (s - steps) % count) for s in range(count)])


def swapped(value, axis, flip):
    count = lax.axis_size(axis)
    return lax.ppermute(value, axis, [(s, s ^ flip) for s in range(count)])


def segment_start(pos, low, high):
    return jnp.where(pos >= high, high, jnp.where(pos >= low, low, 0))


def pack_kernel(residual, segments, scal, *outs):
    cols = outs[0].shape[1]
    ctx_index = lax.axis_index("ctx")
    ids = segments[...]
    scal[0] = ctx_index
    scal[1] = lax.axis_index("mp")
    for at in (1, 2):
        scal[at + 1] = jnp.sum((ids < at).astype(F32)).astype(jnp.int32)
    for flip, out in enumerate(outs):
        block = jnp.bitwise_xor(ctx_index, flip)
        out[...] = residual[:, pl.ds(pl.multiple_of(block * cols, cols), cols)]


def pack(residual, segments, nctx):
    shard, width = residual.shape
    part = jax.ShapeDtypeStruct((shard, width // nctx), BF16)
    scal, *parts = pl.pallas_call(
        pack_kernel,
        out_shape=(jax.ShapeDtypeStruct((4,), jnp.int32),) + (part,) * nctx,
        in_specs=[VMEM, VMEM],
        out_specs=(SMEM,) + (VMEM,) * nctx,
        name="pack",
        compiler_params=pltpu.CompilerParams(vmem_limit_bytes=GRANT),
    )(residual, segments)
    return scal, parts


def join_kernel(scal, *refs):
    out = refs[-1]
    cols = refs[0].shape[1]
    for flip, part in enumerate(refs[:-1]):
        block = jnp.bitwise_xor(scal[0], flip)
        out[:, pl.ds(pl.multiple_of(block * cols, cols), cols)] = part[...]


def join(scal, parts):
    nctx = len(parts)
    shard, cols = parts[0].shape
    return pl.pallas_call(
        join_kernel,
        out_shape=jax.ShapeDtypeStruct((shard, nctx * cols), BF16),
        in_specs=[SMEM] + [VMEM] * nctx,
        out_specs=VMEM,
        name="join",
        compiler_params=pltpu.CompilerParams(vmem_limit_bytes=GRANT),
    )(scal, *parts)


def assemble_kernel(rows, shard, nctx, scal, *refs):
    out = refs[-1]
    ctx_index, mp_index = scal[0], scal[1]
    for flip, piece in enumerate(refs[:-1]):
        member = jnp.bitwise_xor(mp_index, flip)
        for step in range(nctx):
            block = jnp.bitwise_xor(ctx_index, step)
            first = pl.multiple_of(block * rows + member * shard, shard)
            out[pl.ds(first, shard), :] = piece[step * shard : (step + 1) * shard, :]


def assemble(scal, pieces, rows, shard, nctx):
    tokens = nctx * rows
    width = pieces[0].shape[1]
    return pl.pallas_call(
        functools.partial(assemble_kernel, rows, shard, nctx),
        out_shape=jax.ShapeDtypeStruct((tokens, width), BF16),
        in_specs=[SMEM] + [VMEM] * len(pieces),
        out_specs=VMEM,
        name="assemble",
        compiler_params=pltpu.CompilerParams(vmem_limit_bytes=GRANT),
    )(scal, *pieces)


def attend_kernel(nctx, back, steps, shard, scal, *refs):
    count = len(steps)
    q_refs, resid_refs = refs[:count], refs[count : 2 * count]
    kv, weight, keep, send, att, acc = refs[2 * count :]
    rows, width = att.shape
    heads = width // HD
    half = weight.shape[1] // 2
    ctx_index, mp_index, low, high = scal[0], scal[1], scal[2], scal[3]
    side = jnp.bitwise_and(mp_index, 1)
    window = min(back + 1, nctx) * rows
    scale = 1.0 / math.sqrt(HD)
    for j, step in enumerate(steps):
        block = jnp.bitwise_xor(ctx_index, step)
        first_key = pl.multiple_of(
            jnp.minimum(jnp.maximum(block - back, 0), nctx - window // rows) * rows, rows
        )
        qpos = block * rows + lax.broadcasted_iota(jnp.int32, (rows, 1), 0)
        start = segment_start(qpos, low, high)
        kpos = first_key + lax.broadcasted_iota(jnp.int32, (1, window), 1)
        allowed = (kpos <= qpos) & (kpos >= start) & (qpos - kpos < WIN)
        for h in range(heads):
            query = q_refs[j][:, h * HD : (h + 1) * HD]
            keys = kv[pl.ds(first_key, window), :HD]
            scores = lax.dot_general(
                query, keys, (((1,), (1,)), ((), ())), preferred_element_type=F32
            )
            scores = jnp.where(allowed, scores * scale, -1e30)
            top = jnp.max(scores, axis=1, keepdims=True)
            weights = jnp.exp(scores - top)
            total = jnp.sum(weights, axis=1, keepdims=True)
            values = kv[pl.ds(first_key, window), HD:]
            gathered = jnp.dot(weights.astype(BF16), values, preferred_element_type=F32)
            att[:, h * HD : (h + 1) * HD] = (gathered / total).astype(BF16)
        own = pl.ds(pl.multiple_of(mp_index * shard, shard), shard)
        for out, which in ((send, 1 - side), (keep, side)):
            cols = pl.ds(pl.multiple_of(which * half, half), half)
            acc[...] = jnp.dot(att[...], weight[:, cols], preferred_element_type=F32)
            acc[own, :] += resid_refs[j][:, cols].astype(F32)
            out[j * rows : (j + 1) * rows, :] = acc[...].astype(BF16)


def attend(scal, queries, residuals, kv, weight, nctx, back, steps, shard):
    rows, width = kv.shape[0] // nctx, queries[0].shape[1]
    count = len(steps)
    half = weight.shape[1] // 2
    shape = jax.ShapeDtypeStruct((count * rows, half), BF16)
    return pl.pallas_call(
        functools.partial(attend_kernel, nctx, back, steps, shard),
        out_shape=(shape, shape),
        in_specs=[SMEM] + [VMEM] * (2 * count + 2),
        out_specs=(VMEM, VMEM),
        scratch_shapes=[pltpu.VMEM((rows, width), BF16), pltpu.VMEM((rows, half), F32)],
        name="attend",
        compiler_params=pltpu.CompilerParams(vmem_limit_bytes=GRANT),
    )(scal, *queries, *residuals, kv, weight)


def split_weights(gain, weight, ctx_index, side):
    half = weight.shape[0] // 2
    out = []
    for which in (side, 1 - side):
        span = pl.multiple_of(which * half, half)
        cols = pl.ds(pl.multiple_of(ctx_index * 2 * half + span, half), half)
        out.append((gain[:, cols], weight[pl.ds(span, half), :]))
    return out


def project_kernel(count, scal, own, other, gain, weight, *outs):
    ctx_index, mp_index = scal[0], scal[1]
    side = jnp.bitwise_and(mp_index, 1)
    rows = own.shape[0] // count
    half = weight.shape[0] // 2
    shard = outs[1].shape[0]
    (gain_own, weight_own), (gain_other, weight_other) = split_weights(gain, weight, ctx_index, side)
    for j in range(count):
        span = slice(j * rows, (j + 1) * rows)
        scaled_own = (own[span, :].astype(F32) * gain_own).astype(BF16)
        scaled_other = (other[span, :].astype(F32) * gain_other).astype(BF16)
        outs[2 * j][...] = (
            jnp.dot(scaled_own, weight_own, preferred_element_type=F32)
            + jnp.dot(scaled_other, weight_other, preferred_element_type=F32)
        ).astype(BF16)
        mine = pl.ds(pl.multiple_of(j * rows + mp_index * shard, TILE), shard)
        for which, ref in ((side, own), (1 - side, other)):
            outs[2 * j + 1][:, pl.ds(pl.multiple_of(which * half, half), half)] = ref[mine, :]


def project(scal, own, other, gain, weight, count, shard):
    rows = own.shape[0] // count
    features, channels = weight.shape
    shapes = []
    for _ in range(count):
        shapes.append(jax.ShapeDtypeStruct((rows, channels), BF16))
        shapes.append(jax.ShapeDtypeStruct((shard, features), BF16))
    return pl.pallas_call(
        functools.partial(project_kernel, count),
        out_shape=tuple(shapes),
        in_specs=[SMEM] + [VMEM] * 4,
        out_specs=(VMEM,) * len(shapes),
        name="project",
        compiler_params=pltpu.CompilerParams(vmem_limit_bytes=GRANT),
    )(scal, own, other, gain, weight)


def tails_kernel(places, nhalves, rows, scal, *refs):
    nctx = len(places)
    halves, (gain, weight) = refs[:nhalves], refs[nhalves : nhalves + 2]
    outs = refs[nhalves + 2 : nhalves + 2 + nctx]
    edges, ends = refs[nhalves + 2 + nctx :]
    ctx_index = scal[0]
    side = jnp.bitwise_and(scal[1], 1)
    channels = weight.shape[1]
    half = weight.shape[0] // 2
    split = split_weights(gain, weight, ctx_index, side)
    ones = jnp.ones((SUB, half), BF16)

    def squares(piece):
        value = piece.astype(F32)
        return lax.dot_general(
            ones, (value * value).astype(BF16), (((1,), (1,)), ((), ())), preferred_element_type=F32
        )

    for flip, (at, first) in enumerate(places):
        block = jnp.bitwise_xor(ctx_index, flip)
        for k in range(2):
            piece = halves[2 * at + k][first + rows - LANES : first + rows, :]
            edges[k, pl.ds(pl.multiple_of(block * LANES, LANES), LANES), :] = piece
    sums = []
    for flip, (at, first) in enumerate(places):
        before = lax.rem(jnp.bitwise_xor(ctx_index, flip) + nctx - 1, nctx)
        main = edge = None
        for k in range(2):
            part = edges[k, pl.ds(pl.multiple_of(before * LANES, LANES), LANES), :]
            ends[k, flip * TILE : (flip + 1) * TILE, :] = part[LANES - TILE :, :]
            term, edge_term = squares(halves[2 * at + k][first : first + rows, :]), squares(part)
            main = term if main is None else main + term
            edge = edge_term if edge is None else edge + edge_term
        sums.append((main, edge))
    tails = None
    for k, (scale, matrix) in enumerate(split):
        term = jnp.dot(
            (ends[k].astype(F32) * scale).astype(BF16), matrix, preferred_element_type=F32
        )
        tails = term if tails is None else tails + term
    spare = channels - rows - LANES
    for flip, (main, edge) in enumerate(sums):
        pieces = [main, edge] + ([jnp.zeros((SUB, spare), F32)] if spare else [])
        line = jnp.concatenate(pieces, axis=1)
        coarse = line.astype(BF16).astype(F32)
        index = lax.broadcasted_iota(jnp.int32, line.shape, 0)
        line = jnp.where(index == 0, coarse, line - coarse)
        tail = tails[(flip + 1) * TILE - SUB : (flip + 1) * TILE, :]
        outs[flip][...] = jnp.concatenate([line, tail], axis=0).astype(BF16)


def tails(scal, halves, places, gain, weight, rows):
    nctx = len(places)
    half, channels = weight.shape[0] // 2, weight.shape[1]
    return pl.pallas_call(
        functools.partial(tails_kernel, places, len(halves), rows),
        out_shape=(jax.ShapeDtypeStruct((TILE, channels), BF16),) * nctx,
        in_specs=[SMEM] + [VMEM] * (len(halves) + 2),
        out_specs=(VMEM,) * nctx,
        scratch_shapes=[
            pltpu.VMEM((2, nctx * LANES, half), BF16),
            pltpu.VMEM((2, nctx * TILE, half), BF16),
        ],
        name="tails",
        compiler_params=pltpu.CompilerParams(vmem_limit_bytes=GRANT),
    )(scal, *halves, gain, weight)


def minus_expm1(x):
    series = jnp.full_like(x, 1.0 / 5040.0)
    for divisor in (720.0, 120.0, 24.0, 6.0, 2.0, 1.0):
        series = series * x + 1.0 / divisor
    return jnp.where(x > -0.3, -x * series, 1.0 - jnp.exp(x))


def stats_kernel(features, *refs):
    lines, (factor_ref, ahead_ref) = refs[:-2], refs[-2:]
    length = factor_ref.shape[0]
    sums = tail = None
    for line in lines:
        term = line[0:1, :length].astype(F32) + line[1:2, :length].astype(F32)
        tail_term = line[...].astype(F32)[SUB:, :]
        sums = term if sums is None else sums + term
        tail = tail_term if tail is None else tail + tail_term
    factor = lax.rsqrt(sums * (1.0 / features) + 1e-06)
    factor = jnp.transpose(jnp.broadcast_to(factor, (LANES, length)))
    factor_ref[...] = factor
    ahead_ref[...] = (tail * factor[length - SUB :, 0:1]).astype(BF16).astype(F32)


def stats(lines, rows, features):
    channels = lines[0].shape[1]
    return pl.pallas_call(
        functools.partial(stats_kernel, features),
        out_shape=(
            jax.ShapeDtypeStruct((rows + LANES, LANES), F32),
            jax.ShapeDtypeStruct((SUB, channels), F32),
        ),
        in_specs=[VMEM] * len(lines),
        out_specs=(VMEM, VMEM),
        name="stats",
        compiler_params=pltpu.CompilerParams(vmem_limit_bytes=GRANT),
    )(*lines)


def recur_kernel(count, scal, *refs):
    mains, (factor, ahead) = refs[:count], refs[count : count + 2]
    conv_w, decay_w, input_w, decay_b, input_b, codes = refs[count + 2 : count + 8]
    local_ref, cum_ref, last_ref, ext, keep_s, state_s = refs[count + 8 :]
    rows = mains[0].shape[0]
    width = mains[0].shape[1]
    ctx_index, low, high = scal[0], scal[2], scal[3]
    main = None
    for piece in mains:
        term = piece[...].astype(F32)
        main = term if main is None else main + term
    ext[0:SUB, :] = ahead[...]
    ext[SUB : SUB + rows, :] = (main * factor[:rows, 0:1]).astype(BF16).astype(F32)
    pos = ctx_index * rows + lax.broadcasted_iota(jnp.int32, (rows, 1), 0)
    start = segment_start(pos, low, high)
    conv = None
    for lag in range(CONV):
        shifted = ext[SUB - lag : SUB - lag + rows, :]
        term = jnp.where(pos - lag >= start, conv_w[lag : lag + 1, :] * shifted, 0.0)
        conv = term if conv is None else conv + term
    conv = conv.astype(BF16)
    gate_d = jax.nn.sigmoid(
        jnp.dot(conv, decay_w[0], preferred_element_type=F32) + decay_b[...]
    )
    gate_i = jax.nn.sigmoid(
        jnp.dot(conv, input_w[0], preferred_element_type=F32) + input_b[...]
    )
    rate = 0.006 * jnp.exp(-codes[...].astype(F32) * (math.log(3000.0) / (LEVELS - 1)))
    log_decay = -8.0 * gate_d * rate
    restart = pos == start
    keep = jnp.where(restart, 0.0, jnp.exp(log_decay))
    scale = jnp.where(restart, 1.0, jnp.sqrt(minus_expm1(2.0 * log_decay)))
    state = scale * gate_i * conv.astype(F32)
    tiles = rows // SUB
    keep = keep.reshape(tiles, SUB, width)
    state = state.reshape(tiles, SUB, width)
    index = lax.broadcasted_iota(jnp.int32, (tiles, SUB, width), 1)
    shift = 1
    while shift < SUB:
        inside = index >= shift
        prior_keep = jnp.where(inside, pltpu.roll(keep, shift, 1), 1.0)
        prior_state = jnp.where(inside, pltpu.roll(state, shift, 1), 0.0)
        state = keep * prior_state + state
        keep = keep * prior_keep
        shift *= 2
    keep_s[...] = keep
    state_s[...] = state
    run_keep = jnp.ones((1, width), F32)
    run_state = jnp.zeros((1, width), F32)
    for t in range(tiles):
        keep_t, state_t = keep_s[t], state_s[t]
        new_state = state_t + keep_t * run_state
        new_keep = keep_t * run_keep
        local_ref[t * SUB : (t + 1) * SUB, :] = new_state
        cum_ref[t * SUB : (t + 1) * SUB, :] = new_keep
        run_state, run_keep = new_state[SUB - 1 :, :], new_keep[SUB - 1 :, :]
    line = lax.broadcasted_iota(jnp.int32, (SUB, width), 0)
    last_ref[...] = jnp.where(line == 0, run_keep, run_state)


def recur(scal, mains, factor, ahead, conv_w, decay_w, input_w, decay_b, input_b, codes, rows):
    channels = conv_w.shape[1]
    tiles = rows // SUB
    by_block = pl.BlockSpec((rows, BW), lambda j: (0, j))
    row_spec = pl.BlockSpec((1, BW), lambda j: (0, j))
    gate_spec = pl.BlockSpec((1, BW, BW), lambda j: (j, 0, 0))
    factor_spec = pl.BlockSpec(factor.shape, lambda j: (0, 0))
    ahead_spec = pl.BlockSpec((SUB, BW), lambda j: (0, j))
    full = jax.ShapeDtypeStruct((rows, channels), F32)
    return pl.pallas_call(
        functools.partial(recur_kernel, len(mains)),
        grid=(channels // BW,),
        out_shape=(full, full, jax.ShapeDtypeStruct((SUB, channels), F32)),
        in_specs=[SMEM]
        + [by_block] * len(mains)
        + [factor_spec, ahead_spec]
        + [pl.BlockSpec((CONV, BW), lambda j: (0, j)), gate_spec, gate_spec]
        + [row_spec] * 3,
        out_specs=(by_block, by_block, pl.BlockSpec((SUB, BW), lambda j: (0, j))),
        scratch_shapes=[
            pltpu.VMEM((rows + SUB, BW), F32),
            pltpu.VMEM((tiles, SUB, BW), F32),
            pltpu.VMEM((tiles, SUB, BW), F32),
        ],
        name="recur",
        compiler_params=pltpu.CompilerParams(vmem_limit_bytes=GRANT),
    )(scal, *mains, factor, ahead, conv_w, decay_w, input_w, decay_b, input_b, codes)


def local_near(
    queries,
    keyvals,
    segment_ids,
    residual,
    out_weight,
    lru_weight,
    conv_weight,
    gate_decay_w,
    gate_input_w,
    gate_decay_b,
    gate_input_b,
    decay_codes,
    norm_gain,
):
    rows = queries.shape[0]
    shard = keyvals.shape[0]
    tokens = segment_ids.shape[0]
    nctx, nmp = lax.axis_size("ctx"), lax.axis_size("mp")
    ctx_index = lax.axis_index("ctx")
    features = residual.shape[1]
    longest = tokens // 2
    back = -(-(min(WIN, longest) - 1) // rows)
    reach = min(nctx - 1, -(-longest // rows))

    visiting = {0: queries}
    for flip in range(nctx - 1, 0, -2):
        visiting[flip] = swapped(queries, "ctx", flip)
    for flip in range(nctx - 2, 0, -2):
        visiting[flip] = swapped(visiting[flip + 1], "ctx", 1)
    kv_parts = [keyvals]
    for flip in range(1, nctx):
        kv_parts.append(swapped(keyvals, "ctx", flip))
    scal, resid_parts = pack(residual, segment_ids.reshape(-1, LANES), nctx)
    for flip in range(1, nctx):
        resid_parts[flip] = swapped(resid_parts[flip], "ctx", flip)
    pieces = {0: jnp.concatenate(kv_parts, axis=0)}
    flip = nmp // 2
    while flip >= 1:
        for done in sorted(pieces):
            pieces[done | flip] = swapped(pieces[done], "mp", flip)
        flip //= 2
    kv = assemble(scal, [pieces[e] for e in range(nmp)], rows, shard, nctx)
    chunks = [(0,)] + [(flip,) for flip in range(nctx - 1, 0, -1)]
    gain = norm_gain.reshape(1, features)
    halves, places = [], {}
    messages, give = {}, {}
    for at, flips in enumerate(chunks):
        keep, send = attend(
            scal,
            [visiting[e] for e in flips],
            [resid_parts[e] for e in flips],
            kv,
            out_weight,
            nctx,
            back,
            flips,
            shard,
        )
        other = swapped(send, "mp", 1)
        mine = (keep.astype(F32) + other.astype(F32)).astype(BF16)
        flip = 2
        while flip < nmp:
            other = swapped(mine, "mp", flip)
            mine = (mine.astype(F32) + other.astype(F32)).astype(BF16)
            flip *= 2
        other = swapped(mine, "mp", 1)
        halves += [mine, other]
        outs = project(scal, mine, other, gain, lru_weight, len(flips), shard)
        for j, e in enumerate(flips):
            places[e] = (at, j * rows)
            messages[e], give[e] = outs[2 * j], outs[2 * j + 1]
    lines = list(tails(scal, halves, [places[e] for e in range(nctx)], gain, lru_weight, rows))
    mains = [messages[0]]
    for flip in range(nctx - 1, 0, -1):
        if flip % 2 and flip > 1:
            passed = swapped(messages[flip], "ctx", 1)
            both = messages[flip - 1].astype(F32) + passed.astype(F32)
            messages[flip - 1] = both.astype(BF16)
        else:
            mains.append(swapped(messages[flip], "ctx", flip))
    for flip in range(1, nctx):
        lines[flip] = swapped(lines[flip], "ctx", flip)
    factor, ahead = stats(lines, rows, features)
    given = [give[0]]
    for flip in range(1, nctx):
        given.append(swapped(give[flip], "ctx", flip))
    local_state, cum_keep, last = recur(
        scal,
        mains,
        factor,
        ahead,
        conv_weight,
        gate_decay_w,
        gate_input_w,
        gate_decay_b.reshape(1, -1),
        gate_input_b.reshape(1, -1),
        decay_codes.reshape(1, -1),
        rows,
    )
    before = []
    for step in range(1, reach + 1):
        before.append(rotated(last, "ctx", -step))
    resid_out = join(scal, given)
    incoming = jnp.zeros_like(last[0])
    for step in range(reach, 0, -1):
        piece = before[step - 1]
        incoming = jnp.where(ctx_index >= step, piece[0] * incoming + piece[1], 0.0)
    states = local_state + cum_keep * incoming[None, :]
    return (resid_out, states.astype(BF16))


def local(queries, keyvals, segment_ids, residual, out_weight, *rest):
    nctx = lax.axis_size("ctx")
    near = (
        segment_ids.shape[0] <= WIN
        and nctx & (nctx - 1) == 0
        and lax.axis_size("mp") % 2 == 0
        and queries.shape[1] == out_weight.shape[1]
    )
    form = local_near if near else local_wide
    return form(queries, keyvals, segment_ids, residual, out_weight, *rest)


def solution(mesh):
    in_specs = (
        P(("groups", "ctx"), "mp"),
        P(("groups", "ctx", "mp"), None),
        P("groups"),
        P(("groups", "ctx", "mp"), None),
        P("mp", "ctx"),
        P("ctx", "mp"),
        P(None, "mp"),
        P("mp", None, None),
        P("mp", None, None),
        P("mp"),
        P("mp"),
        P("mp"),
        P(),
    )
    out_specs = (P(("groups", "ctx", "mp"), None), P(("groups", "ctx"), "mp"))
    return jax.shard_map(local, mesh=mesh, in_specs=in_specs, out_specs=out_specs, check_vma=False)
```

```python
import functools
import math

import jax
import jax.numpy as jnp
from jax import lax
from jax.experimental import pallas as pl
from jax.experimental.pallas import tpu as pltpu
from jax.sharding import PartitionSpec as P

HD = 256
WIN = 2048
CONV = 4
LEVELS = 16
BW = 256


def shifted_2(value, axis, steps):
    count = lax.axis_size(axis)
    initial, last = (max(0, -steps), min(count, count - steps))
    return lax.ppermute(value, axis, [(source, source + steps) for source in range(initial, last)])


def decay_rates():
    levels = jnp.arange(LEVELS, dtype=jnp.float32)
    return 0.006 * jnp.exp(-levels * (math.log(3000.0) / (LEVELS - 1)))


def chain_link(former, latter):
    return (former[0] * latter[0], latter[0] * former[1] + latter[1])


def rms_scaled(values, norm_gain):
    value_f32 = values.astype(jnp.float32)
    inverse = lax.rsqrt(jnp.mean(value_f32 * value_f32, axis=-1, keepdims=True) + 1e-06)
    return (value_f32 * inverse * norm_gain).astype(jnp.bfloat16)


def attend_local(queries, keys_all, allowed):
    rows_here = queries.shape[0]
    heads_here = queries.shape[1] // HD
    query_heads = queries.reshape(rows_here, heads_here, HD)
    score_scale = 1.0 / math.sqrt(HD)
    scores = (
        jnp.einsum("thd,kd->htk", query_heads, keys_all[:, :HD], preferred_element_type=jnp.float32)
        * score_scale
    )
    scores = jnp.where(allowed[None], scores, -1e30)
    row_top = jnp.max(scores, axis=-1, keepdims=True)
    weights = jnp.exp(scores - row_top)
    probs = (weights / jnp.sum(weights, axis=-1, keepdims=True)).astype(jnp.bfloat16)
    gathered = jnp.einsum(
        "htk,kd->thd", probs, keys_all[:, HD:], preferred_element_type=jnp.float32
    )
    return gathered.reshape(rows_here, heads_here * HD).astype(jnp.bfloat16)


def local_wide(
    queries,
    keyvals,
    segment_ids,
    residual,
    out_weight,
    lru_weight,
    conv_weight,
    gate_decay_w,
    gate_input_w,
    gate_decay_b,
    gate_input_b,
    decay_codes,
    norm_gain,
):
    rows_here = queries.shape[0]
    ctx_index = lax.axis_index("ctx")
    back_blocks = WIN // rows_here
    own_kv = lax.all_gather(keyvals, "mp", axis=0, tiled=True)
    earlier = []
    moving = own_kv
    for _ in range(back_blocks):
        moving = shifted_2(moving, "ctx", 1)
        earlier = [moving] + earlier
    keys_all = jnp.concatenate(earlier + [own_kv], axis=0)
    pad_seg = jnp.concatenate([jnp.full((WIN,), -1, jnp.int32), segment_ids])
    query_seg = lax.dynamic_slice_in_dim(segment_ids, ctx_index * rows_here, rows_here)
    key_seg = lax.dynamic_slice_in_dim(
        pad_seg, ctx_index * rows_here, (back_blocks + 1) * rows_here
    )
    query_pos = ctx_index * rows_here + jnp.arange(rows_here, dtype=jnp.int32)
    key_pos = (ctx_index - back_blocks) * rows_here + jnp.arange(
        (back_blocks + 1) * rows_here, dtype=jnp.int32
    )
    distance = query_pos[:, None] - key_pos[None, :]
    allowed = (distance >= 0) & (distance < WIN) & (query_seg[:, None] == key_seg[None, :])
    attended = attend_local(queries, keys_all, allowed)
    head_part = jnp.dot(
        attended,
        lax.all_gather(out_weight, "ctx", axis=1, tiled=True),
        preferred_element_type=jnp.float32,
    )
    summed = lax.psum_scatter(
        head_part.astype(jnp.bfloat16), "mp", scatter_dimension=0, tiled=True
    ).astype(jnp.float32)
    resid_out = (summed + residual.astype(jnp.float32)).astype(jnp.bfloat16)
    normed = lax.all_gather(rms_scaled(resid_out, norm_gain), "mp", axis=0, tiled=True)
    channels = lru_weight.shape[1]
    lru_in = jnp.dot(
        normed,
        lax.all_gather(lru_weight, "ctx", axis=0, tiled=True),
        preferred_element_type=jnp.float32,
    ).astype(jnp.bfloat16)
    rim_rows = shifted_2(lru_in[rows_here - (CONV - 1) :], "ctx", 1)
    extended = jnp.concatenate([rim_rows, lru_in], axis=0)
    ext_seg = lax.dynamic_slice_in_dim(
        pad_seg, ctx_index * rows_here + WIN - (CONV - 1), rows_here + CONV - 1
    )
    conv_acc = jnp.zeros((rows_here, channels), jnp.float32)
    for offset in range(CONV):
        lag_rows = CONV - 1 - offset
        shifted = extended[lag_rows : lag_rows + rows_here].astype(jnp.float32)
        same_doc = (ext_seg[lag_rows : lag_rows + rows_here] == query_seg)[:, None]
        conv_acc = conv_acc + jnp.where(same_doc, conv_weight[offset] * shifted, 0.0)
    conv_out = conv_acc.astype(jnp.bfloat16)
    blocks_here = channels // BW
    grouped = conv_out.reshape(rows_here, blocks_here, BW)
    decay_gate = jax.nn.sigmoid(
        jnp.einsum(
            "tbi,bij->tbj", grouped, gate_decay_w, preferred_element_type=jnp.float32
        ).reshape(rows_here, channels)
        + gate_decay_b
    )
    input_gate = jax.nn.sigmoid(
        jnp.einsum(
            "tbi,bij->tbj", grouped, gate_input_w, preferred_element_type=jnp.float32
        ).reshape(rows_here, channels)
        + gate_input_b
    )
    levels = jnp.arange(LEVELS, dtype=jnp.int32)
    decay_rate = jnp.sum(
        jnp.where(decay_codes[:, None] == levels[None, :], decay_rates()[None, :], 0.0), axis=1
    )
    log_decay = -8.0 * decay_gate * decay_rate
    restart = (query_seg != ext_seg[CONV - 2 : CONV - 2 + rows_here])[:, None]
    keep_factor = jnp.where(restart, 0.0, jnp.exp(log_decay))
    input_scale = jnp.where(restart, 1.0, jnp.sqrt(-jnp.expm1(2.0 * log_decay)))
    driven = input_scale * input_gate * conv_out.astype(jnp.float32)
    cum_keep, local_state = lax.associative_scan(chain_link, (keep_factor, driven), axis=0)
    block_keep = cum_keep[rows_here - 1]
    block_state = local_state[rows_here - 1]

    def relay_turn(turn_index, state_in):
        return shifted_2(block_keep * state_in + block_state, "ctx", 1)

    incoming = lax.fori_loop(0, lax.axis_size("ctx") - 1, relay_turn, jnp.zeros_like(block_state))
    states = local_state + cum_keep * incoming[None, :]
    return (resid_out, states.astype(jnp.bfloat16))


F32 = jnp.float32
BF16 = jnp.bfloat16
VMEM = pl.BlockSpec(memory_space=pltpu.VMEM)
SMEM = pl.BlockSpec(memory_space=pltpu.SMEM)
TILE = 16
SUB = 8
LANES = 128
GRANT = 20 << 20


def rotated(value, axis, steps):
    count = lax.axis_size(axis)
    return lax.ppermute(value, axis, [(s, (s - steps) % count) for s in range(count)])


def swapped(value, axis, flip):
    count = lax.axis_size(axis)
    return lax.ppermute(value, axis, [(s, s ^ flip) for s in range(count)])


def segment_start(pos, low, high):
    return jnp.where(pos >= high, high, jnp.where(pos >= low, low, 0))


def pack_kernel(residual, segments, scal, *outs):
    cols = outs[0].shape[1]
    ctx_index = lax.axis_index("ctx")
    ids = segments[...]
    scal[0] = ctx_index
    scal[1] = lax.axis_index("mp")
    for at in (1, 2):
        scal[at + 1] = jnp.sum((ids < at).astype(F32)).astype(jnp.int32)
    for flip, out in enumerate(outs):
        block = jnp.bitwise_xor(ctx_index, flip)
        out[...] = residual[:, pl.ds(pl.multiple_of(block * cols, cols), cols)]


def pack(residual, segments, nctx):
    shard, width = residual.shape
    part = jax.ShapeDtypeStruct((shard, width // nctx), BF16)
    scal, *parts = pl.pallas_call(
        pack_kernel,
        out_shape=(jax.ShapeDtypeStruct((4,), jnp.int32),) + (part,) * nctx,
        in_specs=[VMEM, VMEM],
        out_specs=(SMEM,) + (VMEM,) * nctx,
        name="pack",
        compiler_params=pltpu.CompilerParams(vmem_limit_bytes=GRANT),
    )(residual, segments)
    return scal, parts


def join_kernel(scal, *refs):
    out = refs[-1]
    cols = refs[0].shape[1]
    for flip, part in enumerate(refs[:-1]):
        block = jnp.bitwise_xor(scal[0], flip)
        out[:, pl.ds(pl.multiple_of(block * cols, cols), cols)] = part[...]


def join(scal, parts):
    nctx = len(parts)
    shard, cols = parts[0].shape
    return pl.pallas_call(
        join_kernel,
        out_shape=jax.ShapeDtypeStruct((shard, nctx * cols), BF16),
        in_specs=[SMEM] + [VMEM] * nctx,
        out_specs=VMEM,
        name="join",
        compiler_params=pltpu.CompilerParams(vmem_limit_bytes=GRANT),
    )(scal, *parts)


def assemble_kernel(rows, shard, nctx, scal, *refs):
    out = refs[-1]
    ctx_index, mp_index = scal[0], scal[1]
    for flip, piece in enumerate(refs[:-1]):
        member = jnp.bitwise_xor(mp_index, flip)
        for step in range(nctx):
            block = jnp.bitwise_xor(ctx_index, step)
            first = pl.multiple_of(block * rows + member * shard, shard)
            out[pl.ds(first, shard), :] = piece[step * shard : (step + 1) * shard, :]


def assemble(scal, pieces, rows, shard, nctx):
    tokens = nctx * rows
    width = pieces[0].shape[1]
    return pl.pallas_call(
        functools.partial(assemble_kernel, rows, shard, nctx),
        out_shape=jax.ShapeDtypeStruct((tokens, width), BF16),
        in_specs=[SMEM] + [VMEM] * len(pieces),
        out_specs=VMEM,
        name="assemble",
        compiler_params=pltpu.CompilerParams(vmem_limit_bytes=GRANT),
    )(scal, *pieces)


def attend_kernel(nctx, back, steps, shard, scal, *refs):
    count = len(steps)
    q_refs, resid_refs = refs[:count], refs[count : 2 * count]
    kv, weight, keep, send, att, acc = refs[2 * count :]
    rows, width = att.shape
    heads = width // HD
    half = weight.shape[1] // 2
    ctx_index, mp_index, low, high = scal[0], scal[1], scal[2], scal[3]
    side = jnp.bitwise_and(mp_index, 1)
    window = min(back + 1, nctx) * rows
    scale = 1.0 / math.sqrt(HD)
    for j, step in enumerate(steps):
        block = jnp.bitwise_xor(ctx_index, step)
        first_key = pl.multiple_of(
            jnp.minimum(jnp.maximum(block - back, 0), nctx - window // rows) * rows, rows
        )
        qpos = block * rows + lax.broadcasted_iota(jnp.int32, (rows, 1), 0)
        start = segment_start(qpos, low, high)
        kpos = first_key + lax.broadcasted_iota(jnp.int32, (1, window), 1)
        allowed = (kpos <= qpos) & (kpos >= start) & (qpos - kpos < WIN)
        for h in range(heads):
            query = q_refs[j][:, h * HD : (h + 1) * HD]
            keys = kv[pl.ds(first_key, window), :HD]
            scores = lax.dot_general(
                query, keys, (((1,), (1,)), ((), ())), preferred_element_type=F32
            )
            scores = jnp.where(allowed, scores * scale, -1e30)
            top = jnp.max(scores, axis=1, keepdims=True)
            weights = jnp.exp(scores - top)
            total = jnp.sum(weights, axis=1, keepdims=True)
            values = kv[pl.ds(first_key, window), HD:]
            gathered = jnp.dot(weights.astype(BF16), values, preferred_element_type=F32)
            att[:, h * HD : (h + 1) * HD] = (gathered / total).astype(BF16)
        own = pl.ds(pl.multiple_of(mp_index * shard, shard), shard)
        for out, which in ((send, 1 - side), (keep, side)):
            cols = pl.ds(pl.multiple_of(which * half, half), half)
            acc[...] = jnp.dot(att[...], weight[:, cols], preferred_element_type=F32)
            acc[own, :] += resid_refs[j][:, cols].astype(F32)
            out[j * rows : (j + 1) * rows, :] = acc[...].astype(BF16)


def attend(scal, queries, residuals, kv, weight, nctx, back, steps, shard):
    rows, width = kv.shape[0] // nctx, queries[0].shape[1]
    count = len(steps)
    half = weight.shape[1] // 2
    shape = jax.ShapeDtypeStruct((count * rows, half), BF16)
    return pl.pallas_call(
        functools.partial(attend_kernel, nctx, back, steps, shard),
        out_shape=(shape, shape),
        in_specs=[SMEM] + [VMEM] * (2 * count + 2),
        out_specs=(VMEM, VMEM),
        scratch_shapes=[pltpu.VMEM((rows, width), BF16), pltpu.VMEM((rows, half), F32)],
        name="attend",
        compiler_params=pltpu.CompilerParams(vmem_limit_bytes=GRANT),
    )(scal, *queries, *residuals, kv, weight)


def split_weights(gain, weight, ctx_index, side):
    half = weight.shape[0] // 2
    out = []
    for which in (side, 1 - side):
        span = pl.multiple_of(which * half, half)
        cols = pl.ds(pl.multiple_of(ctx_index * 2 * half + span, half), half)
        out.append((gain[:, cols], weight[pl.ds(span, half), :]))
    return out


def project_kernel(count, scal, own, other, gain, weight, *outs):
    ctx_index, mp_index = scal[0], scal[1]
    side = jnp.bitwise_and(mp_index, 1)
    rows = own.shape[0] // count
    half = weight.shape[0] // 2
    shard = outs[1].shape[0]
    (gain_own, weight_own), (gain_other, weight_other) = split_weights(gain, weight, ctx_index, side)
    for j in range(count):
        span = slice(j * rows, (j + 1) * rows)
        scaled_own = (own[span, :].astype(F32) * gain_own).astype(BF16)
        scaled_other = (other[span, :].astype(F32) * gain_other).astype(BF16)
        outs[2 * j][...] = (
            jnp.dot(scaled_own, weight_own, preferred_element_type=F32)
            + jnp.dot(scaled_other, weight_other, preferred_element_type=F32)
        ).astype(BF16)
        mine = pl.ds(pl.multiple_of(j * rows + mp_index * shard, TILE), shard)
        for which, ref in ((side, own), (1 - side, other)):
            outs[2 * j + 1][:, pl.ds(pl.multiple_of(which * half, half), half)] = ref[mine, :]


def project(scal, own, other, gain, weight, count, shard):
    rows = own.shape[0] // count
    features, channels = weight.shape
    shapes = []
    for _ in range(count):
        shapes.append(jax.ShapeDtypeStruct((rows, channels), BF16))
        shapes.append(jax.ShapeDtypeStruct((shard, features), BF16))
    return pl.pallas_call(
        functools.partial(project_kernel, count),
        out_shape=tuple(shapes),
        in_specs=[SMEM] + [VMEM] * 4,
        out_specs=(VMEM,) * len(shapes),
        name="project",
        compiler_params=pltpu.CompilerParams(vmem_limit_bytes=GRANT),
    )(scal, own, other, gain, weight)


def tails_kernel(places, nhalves, rows, near, scal, *refs):
    nctx = len(places)
    halves, (gain, weight, message) = refs[:nhalves], refs[nhalves : nhalves + 3]
    outs = refs[nhalves + 3 : nhalves + 3 + nctx]
    edges, ends = refs[nhalves + 3 + nctx :]
    outs[near][0:rows, :] = message[...]
    ctx_index = scal[0]
    side = jnp.bitwise_and(scal[1], 1)
    channels = weight.shape[1]
    half = weight.shape[0] // 2
    split = split_weights(gain, weight, ctx_index, side)
    ones = jnp.ones((SUB, half), BF16)

    def squares(piece):
        value = piece.astype(F32)
        return lax.dot_general(
            ones, (value * value).astype(BF16), (((1,), (1,)), ((), ())), preferred_element_type=F32
        )

    for flip, (at, first) in enumerate(places):
        block = jnp.bitwise_xor(ctx_index, flip)
        for k in range(2):
            piece = halves[2 * at + k][first + rows - LANES : first + rows, :]
            edges[k, pl.ds(pl.multiple_of(block * LANES, LANES), LANES), :] = piece
    sums = []
    for flip, (at, first) in enumerate(places):
        before = lax.rem(jnp.bitwise_xor(ctx_index, flip) + nctx - 1, nctx)
        main = edge = None
        for k in range(2):
            part = edges[k, pl.ds(pl.multiple_of(before * LANES, LANES), LANES), :]
            ends[k, flip * TILE : (flip + 1) * TILE, :] = part[LANES - TILE :, :]
            term, edge_term = squares(halves[2 * at + k][first : first + rows, :]), squares(part)
            main = term if main is None else main + term
            edge = edge_term if edge is None else edge + edge_term
        sums.append((main, edge))
    tails = None
    for k, (scale, matrix) in enumerate(split):
        term = jnp.dot(
            (ends[k].astype(F32) * scale).astype(BF16), matrix, preferred_element_type=F32
        )
        tails = term if tails is None else tails + term
    spare = channels - rows - LANES
    for flip, (main, edge) in enumerate(sums):
        pieces = [main, edge] + ([jnp.zeros((SUB, spare), F32)] if spare else [])
        line = jnp.concatenate(pieces, axis=1)
        coarse = line.astype(BF16).astype(F32)
        index = lax.broadcasted_iota(jnp.int32, line.shape, 0)
        line = jnp.where(index == 0, coarse, line - coarse)
        tail = tails[(flip + 1) * TILE - SUB : (flip + 1) * TILE, :]
        base = rows if flip == near else 0
        outs[flip][base : base + TILE, :] = jnp.concatenate([line, tail], axis=0).astype(BF16)


def tails(scal, halves, places, gain, weight, message, near):
    nctx = len(places)
    half, channels = weight.shape[0] // 2, weight.shape[1]
    rows = message.shape[0]
    return pl.pallas_call(
        functools.partial(tails_kernel, places, len(halves), rows, near),
        out_shape=tuple(
            jax.ShapeDtypeStruct((TILE + (rows if flip == near else 0), channels), BF16)
            for flip in range(nctx)
        ),
        in_specs=[SMEM] + [VMEM] * (len(halves) + 3),
        out_specs=(VMEM,) * nctx,
        scratch_shapes=[
            pltpu.VMEM((2, nctx * LANES, half), BF16),
            pltpu.VMEM((2, nctx * TILE, half), BF16),
        ],
        name="tails",
        compiler_params=pltpu.CompilerParams(vmem_limit_bytes=GRANT),
    )(scal, *halves, gain, weight, message)


def merge_kernel(message, passed, line, out):
    rows = message.shape[0]
    out[0:rows, :] = (message[...].astype(F32) + passed[...].astype(F32)).astype(BF16)
    out[rows:, :] = line[...]


def merge(message, passed, line):
    rows, channels = message.shape
    return pl.pallas_call(
        merge_kernel,
        out_shape=jax.ShapeDtypeStruct((rows + TILE, channels), BF16),
        in_specs=[VMEM] * 3,
        out_specs=VMEM,
        name="merge",
        compiler_params=pltpu.CompilerParams(vmem_limit_bytes=GRANT),
    )(message, passed, line)


def minus_expm1(x):
    series = jnp.full_like(x, 1.0 / 5040.0)
    for divisor in (720.0, 120.0, 24.0, 6.0, 2.0, 1.0):
        series = series * x + 1.0 / divisor
    return jnp.where(x > -0.3, -x * series, 1.0 - jnp.exp(x))


def recur_kernel(count, nlines, features, scal, *refs):
    mains, lines = refs[:count], refs[count : count + nlines]
    conv_w, decay_w, input_w, decay_b, input_b, codes = refs[count + nlines : count + nlines + 6]
    local_ref, cum_ref, last_ref, ext, keep_s, state_s, factor_s = refs[count + nlines + 6 :]
    rows, width = mains[0].shape
    ctx_index, low, high = scal[0], scal[2], scal[3]

    @pl.when(pl.program_id(0) == 0)
    def _():
        sums = None
        for line in lines:
            both = line[...].astype(F32)[0:2, : rows + LANES]
            term = both[0:1, :] + both[1:2, :]
            sums = term if sums is None else sums + term
        factor = lax.rsqrt(sums * (1.0 / features) + 1e-06)
        factor_s[...] = jnp.transpose(jnp.broadcast_to(factor, (LANES, rows + LANES)))

    lanes = pl.ds(pl.multiple_of(pl.program_id(0) * width, width), width)
    main = tail = None
    for piece in mains:
        term = piece[...].astype(F32)
        main = term if main is None else main + term
    for line in lines:
        term = line[:, lanes].astype(F32)[SUB:, :]
        tail = term if tail is None else tail + term
    ext[0:SUB, :] = (tail * factor_s[rows + LANES - SUB :, 0:1]).astype(BF16).astype(F32)
    ext[SUB : SUB + rows, :] = (main * factor_s[:rows, 0:1]).astype(BF16).astype(F32)
    pos = ctx_index * rows + lax.broadcasted_iota(jnp.int32, (rows, 1), 0)
    start = segment_start(pos, low, high)
    conv = None
    for lag in range(CONV):
        shifted = ext[SUB - lag : SUB - lag + rows, :]
        term = conv_w[lag : lag + 1, :] * shifted
        if lag:
            term = jnp.where(pos - lag >= start, term, 0.0)
        conv = term if conv is None else conv + term
    conv = conv.astype(BF16)
    gate_d = jax.nn.sigmoid(
        jnp.dot(conv, decay_w[0], preferred_element_type=F32) + decay_b[...]
    )
    gate_i = jax.nn.sigmoid(
        jnp.dot(conv, input_w[0], preferred_element_type=F32) + input_b[...]
    )
    rate = 0.006 * jnp.exp(-codes[...].astype(F32) * (math.log(3000.0) / (LEVELS - 1)))
    log_decay = -8.0 * gate_d * rate
    restart = pos == start
    keep = jnp.where(restart, 0.0, jnp.exp(log_decay))
    scale = jnp.where(restart, 1.0, jnp.sqrt(minus_expm1(2.0 * log_decay)))
    state = scale * gate_i * conv.astype(F32)
    tiles = rows // SUB
    keep = keep.reshape(tiles, SUB, width)
    state = state.reshape(tiles, SUB, width)
    index = lax.broadcasted_iota(jnp.int32, (tiles, SUB, width), 1)
    shift = 1
    while shift < SUB:
        inside = index >= shift
        prior_keep = jnp.where(inside, pltpu.roll(keep, shift, 1), 1.0)
        prior_state = jnp.where(inside, pltpu.roll(state, shift, 1), 0.0)
        state = keep * prior_state + state
        keep = keep * prior_keep
        shift *= 2
    keep_s[...] = keep
    state_s[...] = state
    run_keep = jnp.ones((1, width), F32)
    run_state = jnp.zeros((1, width), F32)
    for t in range(tiles):
        keep_t, state_t = keep_s[t], state_s[t]
        new_state = state_t + keep_t * run_state
        new_keep = keep_t * run_keep
        local_ref[t * SUB : (t + 1) * SUB, :] = new_state
        cum_ref[t * SUB : (t + 1) * SUB, :] = new_keep
        run_state, run_keep = new_state[SUB - 1 :, :], new_keep[SUB - 1 :, :]
    line = lax.broadcasted_iota(jnp.int32, (SUB, width), 0)
    last_ref[...] = jnp.where(line == 0, run_keep, run_state)


def recur(scal, mains, lines, conv_w, decay_w, input_w, decay_b, input_b, codes, rows, features):
    channels = conv_w.shape[1]
    tiles = rows // SUB
    by_block = pl.BlockSpec((rows, BW), lambda j: (0, j))
    row_spec = pl.BlockSpec((1, BW), lambda j: (0, j))
    gate_spec = pl.BlockSpec((1, BW, BW), lambda j: (j, 0, 0))
    line_specs = [
        pl.BlockSpec((TILE, channels), functools.partial(lambda at, j: (at, 0), at)) for _, at in lines
    ]
    full = jax.ShapeDtypeStruct((rows, channels), F32)
    return pl.pallas_call(
        functools.partial(recur_kernel, len(mains), len(lines), features),
        grid=(channels // BW,),
        out_shape=(full, full, jax.ShapeDtypeStruct((SUB, channels), F32)),
        in_specs=[SMEM]
        + [by_block] * len(mains)
        + line_specs
        + [pl.BlockSpec((CONV, BW), lambda j: (0, j)), gate_spec, gate_spec]
        + [row_spec] * 3,
        out_specs=(by_block, by_block, pl.BlockSpec((SUB, BW), lambda j: (0, j))),
        scratch_shapes=[
            pltpu.VMEM((rows + SUB, BW), F32),
            pltpu.VMEM((tiles, SUB, BW), F32),
            pltpu.VMEM((tiles, SUB, BW), F32),
            pltpu.VMEM((rows + LANES, LANES), F32),
        ],
        name="recur",
        compiler_params=pltpu.CompilerParams(vmem_limit_bytes=GRANT),
    )(scal, *mains, *[line for line, _ in lines], conv_w, decay_w, input_w, decay_b, input_b, codes)


def local_near(
    queries,
    keyvals,
    segment_ids,
    residual,
    out_weight,
    lru_weight,
    conv_weight,
    gate_decay_w,
    gate_input_w,
    gate_decay_b,
    gate_input_b,
    decay_codes,
    norm_gain,
):
    rows = queries.shape[0]
    shard = keyvals.shape[0]
    tokens = segment_ids.shape[0]
    nctx, nmp = lax.axis_size("ctx"), lax.axis_size("mp")
    ctx_index = lax.axis_index("ctx")
    features = residual.shape[1]
    longest = tokens // 2
    back = -(-(min(WIN, longest) - 1) // rows)
    reach = min(nctx - 1, -(-longest // rows))

    visiting = {0: queries}
    for flip in range(nctx - 1, 0, -2):
        visiting[flip] = swapped(queries, "ctx", flip)
    for flip in range(nctx - 2, 0, -2):
        visiting[flip] = swapped(visiting[flip + 1], "ctx", 1)
    kv_parts = [keyvals]
    for flip in range(1, nctx):
        kv_parts.append(swapped(keyvals, "ctx", flip))
    scal, resid_parts = pack(residual, segment_ids.reshape(-1, LANES), nctx)
    for flip in range(1, nctx):
        resid_parts[flip] = swapped(resid_parts[flip], "ctx", flip)
    pieces = {0: jnp.concatenate(kv_parts, axis=0)}
    flip = nmp // 2
    while flip >= 1:
        for done in sorted(pieces):
            pieces[done | flip] = swapped(pieces[done], "mp", flip)
        flip //= 2
    kv = assemble(scal, [pieces[e] for e in range(nmp)], rows, shard, nctx)
    chunks = [0, 1] + list(range(nctx - 1, 1, -1))
    gain = norm_gain.reshape(1, features)
    halves, places = [], {}
    messages, give = {}, {}
    for at, e in enumerate(chunks):
        keep, send = attend(
            scal, [visiting[e]], [resid_parts[e]], kv, out_weight, nctx, back, (e,), shard
        )
        other = swapped(send, "mp", 1)
        mine = (keep.astype(F32) + other.astype(F32)).astype(BF16)
        flip = 2
        while flip < nmp:
            other = swapped(mine, "mp", flip)
            mine = (mine.astype(F32) + other.astype(F32)).astype(BF16)
            flip *= 2
        other = swapped(mine, "mp", 1)
        halves += [mine, other]
        places[e] = (at, 0)
        messages[e], give[e] = project(scal, mine, other, gain, lru_weight, 1, shard)
    tail_lines = tails(
        scal, halves, [places[e] for e in range(nctx)], gain, lru_weight, messages[1], 1
    )
    mains, lines = [messages[0]], []
    lines.append((tail_lines[0], 0))
    got = swapped(tail_lines[1], "ctx", 1)
    mains.append(got)
    lines.append((got, rows // TILE))
    for flip in range(nctx - 1, 1, -2):
        passed = swapped(messages[flip], "ctx", 1)
        lines.append((swapped(tail_lines[flip], "ctx", flip), 0))
        both = merge(messages[flip - 1], passed, tail_lines[flip - 1])
        got = swapped(both, "ctx", flip - 1)
        mains.append(got)
        lines.append((got, rows // TILE))
    given = [give[0]]
    for flip in range(1, nctx):
        given.append(swapped(give[flip], "ctx", flip))
    local_state, cum_keep, last = recur(
        scal,
        mains,
        lines,
        conv_weight,
        gate_decay_w,
        gate_input_w,
        gate_decay_b.reshape(1, -1),
        gate_input_b.reshape(1, -1),
        decay_codes.reshape(1, -1),
        rows,
        features,
    )
    before = []
    for step in range(1, reach + 1):
        before.append(rotated(last, "ctx", -step))
    resid_out = join(scal, given)
    incoming = jnp.zeros_like(last[0])
    for step in range(reach, 0, -1):
        piece = before[step - 1]
        incoming = jnp.where(ctx_index >= step, piece[0] * incoming + piece[1], 0.0)
    states = local_state + cum_keep * incoming[None, :]
    return (resid_out, states.astype(BF16))


def local(queries, keyvals, segment_ids, residual, out_weight, *rest):
    nctx = lax.axis_size("ctx")
    near = (
        segment_ids.shape[0] <= WIN
        and nctx > 1
        and nctx & (nctx - 1) == 0
        and lax.axis_size("mp") % 2 == 0
        and queries.shape[1] == out_weight.shape[1]
    )
    form = local_near if near else local_wide
    return form(queries, keyvals, segment_ids, residual, out_weight, *rest)


def solution(mesh):
    in_specs = (
        P(("groups", "ctx"), "mp"),
        P(("groups", "ctx", "mp"), None),
        P("groups"),
        P(("groups", "ctx", "mp"), None),
        P("mp", "ctx"),
        P("ctx", "mp"),
        P(None, "mp"),
        P("mp", None, None),
        P("mp", None, None),
        P("mp"),
        P("mp"),
        P("mp"),
        P(),
    )
    out_specs = (P(("groups", "ctx", "mp"), None), P(("groups", "ctx"), "mp"))
    return jax.shard_map(local, mesh=mesh, in_specs=in_specs, out_specs=out_specs, check_vma=False)
```

```python
import functools
import math

import jax
import jax.numpy as jnp
from jax import lax
from jax.experimental import pallas as pl
from jax.experimental.pallas import tpu as pltpu
from jax.sharding import PartitionSpec as P

HD = 256
WIN = 2048
CONV = 4
LEVELS = 16
BW = 256


def shifted_2(value, axis, steps):
    count = lax.axis_size(axis)
    initial, last = (max(0, -steps), min(count, count - steps))
    return lax.ppermute(value, axis, [(source, source + steps) for source in range(initial, last)])


def decay_rates():
    levels = jnp.arange(LEVELS, dtype=jnp.float32)
    return 0.006 * jnp.exp(-levels * (math.log(3000.0) / (LEVELS - 1)))


def chain_link(former, latter):
    return (former[0] * latter[0], latter[0] * former[1] + latter[1])


def rms_scaled(values, norm_gain):
    value_f32 = values.astype(jnp.float32)
    inverse = lax.rsqrt(jnp.mean(value_f32 * value_f32, axis=-1, keepdims=True) + 1e-06)
    return (value_f32 * inverse * norm_gain).astype(jnp.bfloat16)


def attend_local(queries, keys_all, allowed):
    rows_here = queries.shape[0]
    heads_here = queries.shape[1] // HD
    query_heads = queries.reshape(rows_here, heads_here, HD)
    score_scale = 1.0 / math.sqrt(HD)
    scores = (
        jnp.einsum("thd,kd->htk", query_heads, keys_all[:, :HD], preferred_element_type=jnp.float32)
        * score_scale
    )
    scores = jnp.where(allowed[None], scores, -1e30)
    row_top = jnp.max(scores, axis=-1, keepdims=True)
    weights = jnp.exp(scores - row_top)
    probs = (weights / jnp.sum(weights, axis=-1, keepdims=True)).astype(jnp.bfloat16)
    gathered = jnp.einsum(
        "htk,kd->thd", probs, keys_all[:, HD:], preferred_element_type=jnp.float32
    )
    return gathered.reshape(rows_here, heads_here * HD).astype(jnp.bfloat16)


def local_wide(
    queries,
    keyvals,
    segment_ids,
    residual,
    out_weight,
    lru_weight,
    conv_weight,
    gate_decay_w,
    gate_input_w,
    gate_decay_b,
    gate_input_b,
    decay_codes,
    norm_gain,
):
    rows_here = queries.shape[0]
    ctx_index = lax.axis_index("ctx")
    back_blocks = WIN // rows_here
    own_kv = lax.all_gather(keyvals, "mp", axis=0, tiled=True)
    earlier = []
    moving = own_kv
    for _ in range(back_blocks):
        moving = shifted_2(moving, "ctx", 1)
        earlier = [moving] + earlier
    keys_all = jnp.concatenate(earlier + [own_kv], axis=0)
    pad_seg = jnp.concatenate([jnp.full((WIN,), -1, jnp.int32), segment_ids])
    query_seg = lax.dynamic_slice_in_dim(segment_ids, ctx_index * rows_here, rows_here)
    key_seg = lax.dynamic_slice_in_dim(
        pad_seg, ctx_index * rows_here, (back_blocks + 1) * rows_here
    )
    query_pos = ctx_index * rows_here + jnp.arange(rows_here, dtype=jnp.int32)
    key_pos = (ctx_index - back_blocks) * rows_here + jnp.arange(
        (back_blocks + 1) * rows_here, dtype=jnp.int32
    )
    distance = query_pos[:, None] - key_pos[None, :]
    allowed = (distance >= 0) & (distance < WIN) & (query_seg[:, None] == key_seg[None, :])
    attended = attend_local(queries, keys_all, allowed)
    head_part = jnp.dot(
        attended,
        lax.all_gather(out_weight, "ctx", axis=1, tiled=True),
        preferred_element_type=jnp.float32,
    )
    summed = lax.psum_scatter(
        head_part.astype(jnp.bfloat16), "mp", scatter_dimension=0, tiled=True
    ).astype(jnp.float32)
    resid_out = (summed + residual.astype(jnp.float32)).astype(jnp.bfloat16)
    normed = lax.all_gather(rms_scaled(resid_out, norm_gain), "mp", axis=0, tiled=True)
    channels = lru_weight.shape[1]
    lru_in = jnp.dot(
        normed,
        lax.all_gather(lru_weight, "ctx", axis=0, tiled=True),
        preferred_element_type=jnp.float32,
    ).astype(jnp.bfloat16)
    rim_rows = shifted_2(lru_in[rows_here - (CONV - 1) :], "ctx", 1)
    extended = jnp.concatenate([rim_rows, lru_in], axis=0)
    ext_seg = lax.dynamic_slice_in_dim(
        pad_seg, ctx_index * rows_here + WIN - (CONV - 1), rows_here + CONV - 1
    )
    conv_acc = jnp.zeros((rows_here, channels), jnp.float32)
    for offset in range(CONV):
        lag_rows = CONV - 1 - offset
        shifted = extended[lag_rows : lag_rows + rows_here].astype(jnp.float32)
        same_doc = (ext_seg[lag_rows : lag_rows + rows_here] == query_seg)[:, None]
        conv_acc = conv_acc + jnp.where(same_doc, conv_weight[offset] * shifted, 0.0)
    conv_out = conv_acc.astype(jnp.bfloat16)
    blocks_here = channels // BW
    grouped = conv_out.reshape(rows_here, blocks_here, BW)
    decay_gate = jax.nn.sigmoid(
        jnp.einsum(
            "tbi,bij->tbj", grouped, gate_decay_w, preferred_element_type=jnp.float32
        ).reshape(rows_here, channels)
        + gate_decay_b
    )
    input_gate = jax.nn.sigmoid(
        jnp.einsum(
            "tbi,bij->tbj", grouped, gate_input_w, preferred_element_type=jnp.float32
        ).reshape(rows_here, channels)
        + gate_input_b
    )
    levels = jnp.arange(LEVELS, dtype=jnp.int32)
    decay_rate = jnp.sum(
        jnp.where(decay_codes[:, None] == levels[None, :], decay_rates()[None, :], 0.0), axis=1
    )
    log_decay = -8.0 * decay_gate * decay_rate
    restart = (query_seg != ext_seg[CONV - 2 : CONV - 2 + rows_here])[:, None]
    keep_factor = jnp.where(restart, 0.0, jnp.exp(log_decay))
    input_scale = jnp.where(restart, 1.0, jnp.sqrt(-jnp.expm1(2.0 * log_decay)))
    driven = input_scale * input_gate * conv_out.astype(jnp.float32)
    cum_keep, local_state = lax.associative_scan(chain_link, (keep_factor, driven), axis=0)
    block_keep = cum_keep[rows_here - 1]
    block_state = local_state[rows_here - 1]

    def relay_turn(turn_index, state_in):
        return shifted_2(block_keep * state_in + block_state, "ctx", 1)

    incoming = lax.fori_loop(0, lax.axis_size("ctx") - 1, relay_turn, jnp.zeros_like(block_state))
    states = local_state + cum_keep * incoming[None, :]
    return (resid_out, states.astype(jnp.bfloat16))


F32 = jnp.float32
BF16 = jnp.bfloat16
VMEM = pl.BlockSpec(memory_space=pltpu.VMEM)
SMEM = pl.BlockSpec(memory_space=pltpu.SMEM)
TILE = 16
SUB = 8
LANES = 128
GRANT = 20 << 20


def rotated(value, axis, steps):
    count = lax.axis_size(axis)
    return lax.ppermute(value, axis, [(s, (s - steps) % count) for s in range(count)])


def swapped(value, axis, flip):
    count = lax.axis_size(axis)
    return lax.ppermute(value, axis, [(s, s ^ flip) for s in range(count)])


def segment_start(pos, low, high):
    return jnp.where(pos >= high, high, jnp.where(pos >= low, low, 0))


def pack_kernel(residual, segments, scal, *outs):
    cols = outs[0].shape[1]
    ctx_index = lax.axis_index("ctx")
    ids = segments[...]
    scal[0] = ctx_index
    scal[1] = lax.axis_index("mp")
    for at in (1, 2):
        scal[at + 1] = jnp.sum((ids < at).astype(F32)).astype(jnp.int32)
    for flip, out in enumerate(outs):
        block = jnp.bitwise_xor(ctx_index, flip)
        out[...] = residual[:, pl.ds(pl.multiple_of(block * cols, cols), cols)]


def pack(residual, segments, nctx):
    shard, width = residual.shape
    part = jax.ShapeDtypeStruct((shard, width // nctx), BF16)
    scal, *parts = pl.pallas_call(
        pack_kernel,
        out_shape=(jax.ShapeDtypeStruct((4,), jnp.int32),) + (part,) * nctx,
        in_specs=[VMEM, VMEM],
        out_specs=(SMEM,) + (VMEM,) * nctx,
        name="pack",
        compiler_params=pltpu.CompilerParams(vmem_limit_bytes=GRANT),
    )(residual, segments)
    return scal, parts


def join_kernel(scal, *refs):
    out = refs[-1]
    cols = refs[0].shape[1]
    for flip, part in enumerate(refs[:-1]):
        block = jnp.bitwise_xor(scal[0], flip)
        out[:, pl.ds(pl.multiple_of(block * cols, cols), cols)] = part[...]


def join(scal, parts):
    nctx = len(parts)
    shard, cols = parts[0].shape
    return pl.pallas_call(
        join_kernel,
        out_shape=jax.ShapeDtypeStruct((shard, nctx * cols), BF16),
        in_specs=[SMEM] + [VMEM] * nctx,
        out_specs=VMEM,
        name="join",
        compiler_params=pltpu.CompilerParams(vmem_limit_bytes=GRANT),
    )(scal, *parts)


def assemble_kernel(rows, shard, nctx, scal, *refs):
    out = refs[-1]
    ctx_index, mp_index = scal[0], scal[1]
    for flip, piece in enumerate(refs[:-1]):
        member = jnp.bitwise_xor(mp_index, flip)
        for step in range(nctx):
            block = jnp.bitwise_xor(ctx_index, step)
            first = pl.multiple_of(block * rows + member * shard, shard)
            out[pl.ds(first, shard), :] = piece[step * shard : (step + 1) * shard, :]


def assemble(scal, pieces, rows, shard, nctx):
    tokens = nctx * rows
    width = pieces[0].shape[1]
    return pl.pallas_call(
        functools.partial(assemble_kernel, rows, shard, nctx),
        out_shape=jax.ShapeDtypeStruct((tokens, width), BF16),
        in_specs=[SMEM] + [VMEM] * len(pieces),
        out_specs=VMEM,
        name="assemble",
        compiler_params=pltpu.CompilerParams(vmem_limit_bytes=GRANT),
    )(scal, *pieces)


def attend_kernel(nctx, back, steps, shard, scal, *refs):
    count = len(steps)
    q_refs, resid_refs = refs[:count], refs[count : 2 * count]
    kv, weight, keep, send, att, acc = refs[2 * count :]
    rows, width = att.shape
    heads = width // HD
    half = weight.shape[1] // 2
    ctx_index, mp_index, low, high = scal[0], scal[1], scal[2], scal[3]
    side = jnp.bitwise_and(mp_index, 1)
    window = min(back + 1, nctx) * rows
    scale = 1.0 / math.sqrt(HD)
    for j, step in enumerate(steps):
        block = jnp.bitwise_xor(ctx_index, step)
        first_key = pl.multiple_of(
            jnp.minimum(jnp.maximum(block - back, 0), nctx - window // rows) * rows, rows
        )
        qpos = block * rows + lax.broadcasted_iota(jnp.int32, (rows, 1), 0)
        start = segment_start(qpos, low, high)
        kpos = first_key + lax.broadcasted_iota(jnp.int32, (1, window), 1)
        allowed = (kpos <= qpos) & (kpos >= start) & (qpos - kpos < WIN)
        for h in range(heads):
            query = q_refs[j][:, h * HD : (h + 1) * HD]
            keys = kv[pl.ds(first_key, window), :HD]
            scores = lax.dot_general(
                query, keys, (((1,), (1,)), ((), ())), preferred_element_type=F32
            )
            scores = jnp.where(allowed, scores * scale, -1e30)
            top = jnp.max(scores, axis=1, keepdims=True)
            weights = jnp.exp(scores - top)
            total = jnp.sum(weights, axis=1, keepdims=True)
            values = kv[pl.ds(first_key, window), HD:]
            gathered = jnp.dot(weights.astype(BF16), values, preferred_element_type=F32)
            att[:, h * HD : (h + 1) * HD] = (gathered / total).astype(BF16)
        own = pl.ds(pl.multiple_of(mp_index * shard, shard), shard)
        for out, which in ((send, 1 - side), (keep, side)):
            cols = pl.ds(pl.multiple_of(which * half, half), half)
            acc[...] = jnp.dot(att[...], weight[:, cols], preferred_element_type=F32)
            acc[own, :] += resid_refs[j][:, cols].astype(F32)
            out[j * rows : (j + 1) * rows, :] = acc[...].astype(BF16)


def attend(scal, queries, residuals, kv, weight, nctx, back, steps, shard):
    rows, width = kv.shape[0] // nctx, queries[0].shape[1]
    count = len(steps)
    half = weight.shape[1] // 2
    shape = jax.ShapeDtypeStruct((count * rows, half), BF16)
    return pl.pallas_call(
        functools.partial(attend_kernel, nctx, back, steps, shard),
        out_shape=(shape, shape),
        in_specs=[SMEM] + [VMEM] * (2 * count + 2),
        out_specs=(VMEM, VMEM),
        scratch_shapes=[pltpu.VMEM((rows, width), BF16), pltpu.VMEM((rows, half), F32)],
        name="attend",
        compiler_params=pltpu.CompilerParams(vmem_limit_bytes=GRANT),
    )(scal, *queries, *residuals, kv, weight)


def split_weights(gain, weight, ctx_index, side):
    half = weight.shape[0] // 2
    out = []
    for which in (side, 1 - side):
        span = pl.multiple_of(which * half, half)
        cols = pl.ds(pl.multiple_of(ctx_index * 2 * half + span, half), half)
        out.append((gain[:, cols], weight[pl.ds(span, half), :]))
    return out


def project_kernel(count, scal, own, other, gain, weight, *outs):
    ctx_index, mp_index = scal[0], scal[1]
    side = jnp.bitwise_and(mp_index, 1)
    rows = own.shape[0] // count
    half = weight.shape[0] // 2
    shard = outs[1].shape[0]
    (gain_own, weight_own), (gain_other, weight_other) = split_weights(gain, weight, ctx_index, side)
    for j in range(count):
        span = slice(j * rows, (j + 1) * rows)
        scaled_own = (own[span, :].astype(F32) * gain_own).astype(BF16)
        scaled_other = (other[span, :].astype(F32) * gain_other).astype(BF16)
        outs[2 * j][...] = (
            jnp.dot(scaled_own, weight_own, preferred_element_type=F32)
            + jnp.dot(scaled_other, weight_other, preferred_element_type=F32)
        ).astype(BF16)
        mine = pl.ds(pl.multiple_of(j * rows + mp_index * shard, TILE), shard)
        for which, ref in ((side, own), (1 - side, other)):
            outs[2 * j + 1][:, pl.ds(pl.multiple_of(which * half, half), half)] = ref[mine, :]


def project(scal, own, other, gain, weight, count, shard):
    rows = own.shape[0] // count
    features, channels = weight.shape
    shapes = []
    for _ in range(count):
        shapes.append(jax.ShapeDtypeStruct((rows, channels), BF16))
        shapes.append(jax.ShapeDtypeStruct((shard, features), BF16))
    return pl.pallas_call(
        functools.partial(project_kernel, count),
        out_shape=tuple(shapes),
        in_specs=[SMEM] + [VMEM] * 4,
        out_specs=(VMEM,) * len(shapes),
        name="project",
        compiler_params=pltpu.CompilerParams(vmem_limit_bytes=GRANT),
    )(scal, own, other, gain, weight)


def tails_kernel(places, nhalves, rows, scal, *refs):
    nctx = len(places)
    halves, (gain, weight) = refs[:nhalves], refs[nhalves : nhalves + 2]
    outs = refs[nhalves + 2 : nhalves + 2 + nctx]
    edges, ends = refs[nhalves + 2 + nctx :]
    ctx_index = scal[0]
    side = jnp.bitwise_and(scal[1], 1)
    channels = weight.shape[1]
    half = weight.shape[0] // 2
    split = split_weights(gain, weight, ctx_index, side)
    ones = jnp.ones((SUB, half), BF16)

    def squares(piece):
        value = piece.astype(F32)
        return lax.dot_general(
            ones, (value * value).astype(BF16), (((1,), (1,)), ((), ())), preferred_element_type=F32
        )

    for flip, (at, first) in enumerate(places):
        block = jnp.bitwise_xor(ctx_index, flip)
        for k in range(2):
            piece = halves[2 * at + k][first + rows - LANES : first + rows, :]
            edges[k, pl.ds(pl.multiple_of(block * LANES, LANES), LANES), :] = piece
    sums = []
    for flip, (at, first) in enumerate(places):
        before = lax.rem(jnp.bitwise_xor(ctx_index, flip) + nctx - 1, nctx)
        main = edge = None
        for k in range(2):
            part = edges[k, pl.ds(pl.multiple_of(before * LANES, LANES), LANES), :]
            ends[k, flip * TILE : (flip + 1) * TILE, :] = part[LANES - TILE :, :]
            term, edge_term = squares(halves[2 * at + k][first : first + rows, :]), squares(part)
            main = term if main is None else main + term
            edge = edge_term if edge is None else edge + edge_term
        sums.append((main, edge))
    tails = None
    for k, (scale, matrix) in enumerate(split):
        term = jnp.dot(
            (ends[k].astype(F32) * scale).astype(BF16), matrix, preferred_element_type=F32
        )
        tails = term if tails is None else tails + term
    spare = channels - rows - LANES
    for flip, (main, edge) in enumerate(sums):
        pieces = [main, edge] + ([jnp.zeros((SUB, spare), F32)] if spare else [])
        line = jnp.concatenate(pieces, axis=1)
        coarse = line.astype(BF16).astype(F32)
        index = lax.broadcasted_iota(jnp.int32, line.shape, 0)
        line = jnp.where(index == 0, coarse, line - coarse)
        tail = tails[(flip + 1) * TILE - SUB : (flip + 1) * TILE, :]
        outs[flip][...] = jnp.concatenate([line, tail], axis=0).astype(BF16)


def tails(scal, halves, places, gain, weight, rows):
    nctx = len(places)
    half, channels = weight.shape[0] // 2, weight.shape[1]
    return pl.pallas_call(
        functools.partial(tails_kernel, places, len(halves), rows),
        out_shape=(jax.ShapeDtypeStruct((TILE, channels), BF16),) * nctx,
        in_specs=[SMEM] + [VMEM] * (len(halves) + 2),
        out_specs=(VMEM,) * nctx,
        scratch_shapes=[
            pltpu.VMEM((2, nctx * LANES, half), BF16),
            pltpu.VMEM((2, nctx * TILE, half), BF16),
        ],
        name="tails",
        compiler_params=pltpu.CompilerParams(vmem_limit_bytes=GRANT),
    )(scal, *halves, gain, weight)


def minus_expm1(x):
    series = jnp.full_like(x, 1.0 / 5040.0)
    for divisor in (720.0, 120.0, 24.0, 6.0, 2.0, 1.0):
        series = series * x + 1.0 / divisor
    return jnp.where(x > -0.3, -x * series, 1.0 - jnp.exp(x))


def recur_kernel(count, nlines, features, scal, *refs):
    mains, lines = refs[:count], refs[count : count + nlines]
    conv_w, decay_w, input_w, decay_b, input_b, codes = refs[count + nlines : count + nlines + 6]
    local_ref, cum_ref, last_ref, ext, keep_s, state_s, factor_s = refs[count + nlines + 6 :]
    rows, width = mains[0].shape
    ctx_index, low, high = scal[0], scal[2], scal[3]

    @pl.when(pl.program_id(0) == 0)
    def _():
        sums = None
        for line in lines:
            both = line[...].astype(F32)[0:2, : rows + LANES]
            term = both[0:1, :] + both[1:2, :]
            sums = term if sums is None else sums + term
        factor = lax.rsqrt(sums * (1.0 / features) + 1e-06)
        factor_s[...] = jnp.transpose(jnp.broadcast_to(factor, (LANES, rows + LANES)))

    lanes = pl.ds(pl.multiple_of(pl.program_id(0) * width, width), width)
    main = tail = None
    for piece in mains:
        term = piece[...].astype(F32)
        main = term if main is None else main + term
    for line in lines:
        term = line[:, lanes].astype(F32)[SUB:, :]
        tail = term if tail is None else tail + term
    ext[0:SUB, :] = (tail * factor_s[rows + LANES - SUB :, 0:1]).astype(BF16).astype(F32)
    ext[SUB : SUB + rows, :] = (main * factor_s[:rows, 0:1]).astype(BF16).astype(F32)
    pos = ctx_index * rows + lax.broadcasted_iota(jnp.int32, (rows, 1), 0)
    start = segment_start(pos, low, high)
    conv = None
    for lag in range(CONV):
        shifted = ext[SUB - lag : SUB - lag + rows, :]
        term = conv_w[lag : lag + 1, :] * shifted
        if lag:
            term = jnp.where(pos - lag >= start, term, 0.0)
        conv = term if conv is None else conv + term
    conv = conv.astype(BF16)
    gate_d = jax.nn.sigmoid(
        jnp.dot(conv, decay_w[0], preferred_element_type=F32) + decay_b[...]
    )
    gate_i = jax.nn.sigmoid(
        jnp.dot(conv, input_w[0], preferred_element_type=F32) + input_b[...]
    )
    rate = 0.006 * jnp.exp(-codes[...].astype(F32) * (math.log(3000.0) / (LEVELS - 1)))
    log_decay = -8.0 * gate_d * rate
    restart = pos == start
    keep = jnp.where(restart, 0.0, jnp.exp(log_decay))
    scale = jnp.where(restart, 1.0, jnp.sqrt(minus_expm1(2.0 * log_decay)))
    state = scale * gate_i * conv.astype(F32)
    tiles = rows // SUB
    keep = keep.reshape(tiles, SUB, width)
    state = state.reshape(tiles, SUB, width)
    index = lax.broadcasted_iota(jnp.int32, (tiles, SUB, width), 1)
    shift = 1
    while shift < SUB:
        inside = index >= shift
        prior_keep = jnp.where(inside, pltpu.roll(keep, shift, 1), 1.0)
        prior_state = jnp.where(inside, pltpu.roll(state, shift, 1), 0.0)
        state = keep * prior_state + state
        keep = keep * prior_keep
        shift *= 2
    keep_s[...] = keep
    state_s[...] = state
    run_keep = jnp.ones((1, width), F32)
    run_state = jnp.zeros((1, width), F32)
    for t in range(tiles):
        keep_t, state_t = keep_s[t], state_s[t]
        new_state = state_t + keep_t * run_state
        new_keep = keep_t * run_keep
        local_ref[t * SUB : (t + 1) * SUB, :] = new_state
        cum_ref[t * SUB : (t + 1) * SUB, :] = new_keep
        run_state, run_keep = new_state[SUB - 1 :, :], new_keep[SUB - 1 :, :]
    line = lax.broadcasted_iota(jnp.int32, (SUB, width), 0)
    last_ref[...] = jnp.where(line == 0, run_keep, run_state)


def recur(scal, mains, lines, conv_w, decay_w, input_w, decay_b, input_b, codes, rows, features):
    channels = conv_w.shape[1]
    tiles = rows // SUB
    by_block = pl.BlockSpec((rows, BW), lambda j: (0, j))
    row_spec = pl.BlockSpec((1, BW), lambda j: (0, j))
    gate_spec = pl.BlockSpec((1, BW, BW), lambda j: (j, 0, 0))
    line_spec = pl.BlockSpec((TILE, channels), lambda j: (0, 0))
    full = jax.ShapeDtypeStruct((rows, channels), F32)
    return pl.pallas_call(
        functools.partial(recur_kernel, len(mains), len(lines), features),
        grid=(channels // BW,),
        out_shape=(full, full, jax.ShapeDtypeStruct((SUB, channels), F32)),
        in_specs=[SMEM]
        + [by_block] * len(mains)
        + [line_spec] * len(lines)
        + [pl.BlockSpec((CONV, BW), lambda j: (0, j)), gate_spec, gate_spec]
        + [row_spec] * 3,
        out_specs=(by_block, by_block, pl.BlockSpec((SUB, BW), lambda j: (0, j))),
        scratch_shapes=[
            pltpu.VMEM((rows + SUB, BW), F32),
            pltpu.VMEM((tiles, SUB, BW), F32),
            pltpu.VMEM((tiles, SUB, BW), F32),
            pltpu.VMEM((rows + LANES, LANES), F32),
        ],
        name="recur",
        compiler_params=pltpu.CompilerParams(vmem_limit_bytes=GRANT),
    )(scal, *mains, *lines, conv_w, decay_w, input_w, decay_b, input_b, codes)


def local_near(
    queries,
    keyvals,
    segment_ids,
    residual,
    out_weight,
    lru_weight,
    conv_weight,
    gate_decay_w,
    gate_input_w,
    gate_decay_b,
    gate_input_b,
    decay_codes,
    norm_gain,
):
    rows = queries.shape[0]
    shard = keyvals.shape[0]
    tokens = segment_ids.shape[0]
    nctx, nmp = lax.axis_size("ctx"), lax.axis_size("mp")
    ctx_index = lax.axis_index("ctx")
    features = residual.shape[1]
    longest = tokens // 2
    back = -(-(min(WIN, longest) - 1) // rows)
    reach = min(nctx - 1, -(-longest // rows))

    visiting = {0: queries}
    for flip in range(nctx - 1, 0, -2):
        visiting[flip] = swapped(queries, "ctx", flip)
    for flip in range(nctx - 2, 0, -2):
        visiting[flip] = swapped(visiting[flip + 1], "ctx", 1)
    kv_parts = [keyvals]
    for flip in range(1, nctx):
        kv_parts.append(swapped(keyvals, "ctx", flip))
    scal, resid_parts = pack(residual, segment_ids.reshape(-1, LANES), nctx)
    for flip in range(1, nctx):
        resid_parts[flip] = swapped(resid_parts[flip], "ctx", flip)
    pieces = {0: jnp.concatenate(kv_parts, axis=0)}
    flip = nmp // 2
    while flip >= 1:
        for done in sorted(pieces):
            pieces[done | flip] = swapped(pieces[done], "mp", flip)
        flip //= 2
    kv = assemble(scal, [pieces[e] for e in range(nmp)], rows, shard, nctx)
    chunks = [0] + list(range(nctx - 1, 2, -2)) + [1] + list(range(nctx - 2, 1, -2))
    gain = norm_gain.reshape(1, features)
    halves, places = [], {}
    messages, give = {}, {}
    for at, e in enumerate(chunks):
        keep, send = attend(
            scal, [visiting[e]], [resid_parts[e]], kv, out_weight, nctx, back, (e,), shard
        )
        other = swapped(send, "mp", 1)
        mine = (keep.astype(F32) + other.astype(F32)).astype(BF16)
        flip = 2
        while flip < nmp:
            other = swapped(mine, "mp", flip)
            mine = (mine.astype(F32) + other.astype(F32)).astype(BF16)
            flip *= 2
        other = swapped(mine, "mp", 1)
        halves += [mine, other]
        places[e] = (at, 0)
        messages[e], give[e] = project(scal, mine, other, gain, lru_weight, 1, shard)
    lines = list(tails(scal, halves, [places[e] for e in range(nctx)], gain, lru_weight, rows))
    mains = [messages[0]]
    for flip in range(nctx - 1, 0, -1):
        if flip % 2 and flip > 1:
            passed = swapped(messages[flip], "ctx", 1)
            both = messages[flip - 1].astype(F32) + passed.astype(F32)
            messages[flip - 1] = both.astype(BF16)
        else:
            mains.append(swapped(messages[flip], "ctx", flip))
    for flip in range(1, nctx):
        lines[flip] = swapped(lines[flip], "ctx", flip)
    given = [give[0]]
    for flip in range(1, nctx):
        given.append(swapped(give[flip], "ctx", flip))
    local_state, cum_keep, last = recur(
        scal,
        mains,
        lines,
        conv_weight,
        gate_decay_w,
        gate_input_w,
        gate_decay_b.reshape(1, -1),
        gate_input_b.reshape(1, -1),
        decay_codes.reshape(1, -1),
        rows,
        features,
    )
    before = []
    for step in range(1, reach + 1):
        before.append(rotated(last, "ctx", -step))
    resid_out = join(scal, given)
    incoming = jnp.zeros_like(last[0])
    for step in range(reach, 0, -1):
        piece = before[step - 1]
        incoming = jnp.where(ctx_index >= step, piece[0] * incoming + piece[1], 0.0)
    states = local_state + cum_keep * incoming[None, :]
    return (resid_out, states.astype(BF16))


def local(queries, keyvals, segment_ids, residual, out_weight, *rest):
    nctx = lax.axis_size("ctx")
    near = (
        segment_ids.shape[0] <= WIN
        and nctx > 1
        and nctx & (nctx - 1) == 0
        and lax.axis_size("mp") % 2 == 0
        and queries.shape[1] == out_weight.shape[1]
    )
    form = local_near if near else local_wide
    return form(queries, keyvals, segment_ids, residual, out_weight, *rest)


def solution(mesh):
    in_specs = (
        P(("groups", "ctx"), "mp"),
        P(("groups", "ctx", "mp"), None),
        P("groups"),
        P(("groups", "ctx", "mp"), None),
        P("mp", "ctx"),
        P("ctx", "mp"),
        P(None, "mp"),
        P("mp", None, None),
        P("mp", None, None),
        P("mp"),
        P("mp"),
        P("mp"),
        P(),
    )
    out_specs = (P(("groups", "ctx", "mp"), None), P(("groups", "ctx"), "mp"))
    return jax.shard_map(local, mesh=mesh, in_specs=in_specs, out_specs=out_specs, check_vma=False)
```

```python
import functools
import math

import jax
import jax.numpy as jnp
from jax import lax
from jax.experimental import pallas as pl
from jax.experimental.pallas import tpu as pltpu
from jax.sharding import PartitionSpec as P

HD = 256
WIN = 2048
CONV = 4
LEVELS = 16
BW = 256


def shifted_2(value, axis, steps):
    count = lax.axis_size(axis)
    initial, last = (max(0, -steps), min(count, count - steps))
    return lax.ppermute(value, axis, [(source, source + steps) for source in range(initial, last)])


def decay_rates():
    levels = jnp.arange(LEVELS, dtype=jnp.float32)
    return 0.006 * jnp.exp(-levels * (math.log(3000.0) / (LEVELS - 1)))


def chain_link(former, latter):
    return (former[0] * latter[0], latter[0] * former[1] + latter[1])


def rms_scaled(values, norm_gain):
    value_f32 = values.astype(jnp.float32)
    inverse = lax.rsqrt(jnp.mean(value_f32 * value_f32, axis=-1, keepdims=True) + 1e-06)
    return (value_f32 * inverse * norm_gain).astype(jnp.bfloat16)


def attend_local(queries, keys_all, allowed):
    rows_here = queries.shape[0]
    heads_here = queries.shape[1] // HD
    query_heads = queries.reshape(rows_here, heads_here, HD)
    score_scale = 1.0 / math.sqrt(HD)
    scores = (
        jnp.einsum("thd,kd->htk", query_heads, keys_all[:, :HD], preferred_element_type=jnp.float32)
        * score_scale
    )
    scores = jnp.where(allowed[None], scores, -1e30)
    row_top = jnp.max(scores, axis=-1, keepdims=True)
    weights = jnp.exp(scores - row_top)
    probs = (weights / jnp.sum(weights, axis=-1, keepdims=True)).astype(jnp.bfloat16)
    gathered = jnp.einsum(
        "htk,kd->thd", probs, keys_all[:, HD:], preferred_element_type=jnp.float32
    )
    return gathered.reshape(rows_here, heads_here * HD).astype(jnp.bfloat16)


def local_wide(
    queries,
    keyvals,
    segment_ids,
    residual,
    out_weight,
    lru_weight,
    conv_weight,
    gate_decay_w,
    gate_input_w,
    gate_decay_b,
    gate_input_b,
    decay_codes,
    norm_gain,
):
    rows_here = queries.shape[0]
    ctx_index = lax.axis_index("ctx")
    back_blocks = WIN // rows_here
    own_kv = lax.all_gather(keyvals, "mp", axis=0, tiled=True)
    earlier = []
    moving = own_kv
    for _ in range(back_blocks):
        moving = shifted_2(moving, "ctx", 1)
        earlier = [moving] + earlier
    keys_all = jnp.concatenate(earlier + [own_kv], axis=0)
    pad_seg = jnp.concatenate([jnp.full((WIN,), -1, jnp.int32), segment_ids])
    query_seg = lax.dynamic_slice_in_dim(segment_ids, ctx_index * rows_here, rows_here)
    key_seg = lax.dynamic_slice_in_dim(
        pad_seg, ctx_index * rows_here, (back_blocks + 1) * rows_here
    )
    query_pos = ctx_index * rows_here + jnp.arange(rows_here, dtype=jnp.int32)
    key_pos = (ctx_index - back_blocks) * rows_here + jnp.arange(
        (back_blocks + 1) * rows_here, dtype=jnp.int32
    )
    distance = query_pos[:, None] - key_pos[None, :]
    allowed = (distance >= 0) & (distance < WIN) & (query_seg[:, None] == key_seg[None, :])
    attended = attend_local(queries, keys_all, allowed)
    head_part = jnp.dot(
        attended,
        lax.all_gather(out_weight, "ctx", axis=1, tiled=True),
        preferred_element_type=jnp.float32,
    )
    summed = lax.psum_scatter(
        head_part.astype(jnp.bfloat16), "mp", scatter_dimension=0, tiled=True
    ).astype(jnp.float32)
    resid_out = (summed + residual.astype(jnp.float32)).astype(jnp.bfloat16)
    normed = lax.all_gather(rms_scaled(resid_out, norm_gain), "mp", axis=0, tiled=True)
    channels = lru_weight.shape[1]
    lru_in = jnp.dot(
        normed,
        lax.all_gather(lru_weight, "ctx", axis=0, tiled=True),
        preferred_element_type=jnp.float32,
    ).astype(jnp.bfloat16)
    rim_rows = shifted_2(lru_in[rows_here - (CONV - 1) :], "ctx", 1)
    extended = jnp.concatenate([rim_rows, lru_in], axis=0)
    ext_seg = lax.dynamic_slice_in_dim(
        pad_seg, ctx_index * rows_here + WIN - (CONV - 1), rows_here + CONV - 1
    )
    conv_acc = jnp.zeros((rows_here, channels), jnp.float32)
    for offset in range(CONV):
        lag_rows = CONV - 1 - offset
        shifted = extended[lag_rows : lag_rows + rows_here].astype(jnp.float32)
        same_doc = (ext_seg[lag_rows : lag_rows + rows_here] == query_seg)[:, None]
        conv_acc = conv_acc + jnp.where(same_doc, conv_weight[offset] * shifted, 0.0)
    conv_out = conv_acc.astype(jnp.bfloat16)
    blocks_here = channels // BW
    grouped = conv_out.reshape(rows_here, blocks_here, BW)
    decay_gate = jax.nn.sigmoid(
        jnp.einsum(
            "tbi,bij->tbj", grouped, gate_decay_w, preferred_element_type=jnp.float32
        ).reshape(rows_here, channels)
        + gate_decay_b
    )
    input_gate = jax.nn.sigmoid(
        jnp.einsum(
            "tbi,bij->tbj", grouped, gate_input_w, preferred_element_type=jnp.float32
        ).reshape(rows_here, channels)
        + gate_input_b
    )
    levels = jnp.arange(LEVELS, dtype=jnp.int32)
    decay_rate = jnp.sum(
        jnp.where(decay_codes[:, None] == levels[None, :], decay_rates()[None, :], 0.0), axis=1
    )
    log_decay = -8.0 * decay_gate * decay_rate
    restart = (query_seg != ext_seg[CONV - 2 : CONV - 2 + rows_here])[:, None]
    keep_factor = jnp.where(restart, 0.0, jnp.exp(log_decay))
    input_scale = jnp.where(restart, 1.0, jnp.sqrt(-jnp.expm1(2.0 * log_decay)))
    driven = input_scale * input_gate * conv_out.astype(jnp.float32)
    cum_keep, local_state = lax.associative_scan(chain_link, (keep_factor, driven), axis=0)
    block_keep = cum_keep[rows_here - 1]
    block_state = local_state[rows_here - 1]

    def relay_turn(turn_index, state_in):
        return shifted_2(block_keep * state_in + block_state, "ctx", 1)

    incoming = lax.fori_loop(0, lax.axis_size("ctx") - 1, relay_turn, jnp.zeros_like(block_state))
    states = local_state + cum_keep * incoming[None, :]
    return (resid_out, states.astype(jnp.bfloat16))


F32 = jnp.float32
BF16 = jnp.bfloat16
VMEM = pl.BlockSpec(memory_space=pltpu.VMEM)
SMEM = pl.BlockSpec(memory_space=pltpu.SMEM)
TILE = 16
SUB = 8
LANES = 128
GRANT = 20 << 20


def rotated(value, axis, steps):
    count = lax.axis_size(axis)
    return lax.ppermute(value, axis, [(s, (s - steps) % count) for s in range(count)])


def swapped(value, axis, flip):
    count = lax.axis_size(axis)
    return lax.ppermute(value, axis, [(s, s ^ flip) for s in range(count)])


def segment_start(pos, low, high):
    return jnp.where(pos >= high, high, jnp.where(pos >= low, low, 0))


def pack_kernel(residual, segments, scal, *outs):
    cols = outs[0].shape[1]
    ctx_index = lax.axis_index("ctx")
    ids = segments[...]
    scal[0] = ctx_index
    scal[1] = lax.axis_index("mp")
    for at in (1, 2):
        scal[at + 1] = jnp.sum((ids < at).astype(F32)).astype(jnp.int32)
    for flip, out in enumerate(outs):
        block = jnp.bitwise_xor(ctx_index, flip)
        out[...] = residual[:, pl.ds(pl.multiple_of(block * cols, cols), cols)]


def pack(residual, segments, nctx):
    shard, width = residual.shape
    part = jax.ShapeDtypeStruct((shard, width // nctx), BF16)
    scal, *parts = pl.pallas_call(
        pack_kernel,
        out_shape=(jax.ShapeDtypeStruct((4,), jnp.int32),) + (part,) * nctx,
        in_specs=[VMEM, VMEM],
        out_specs=(SMEM,) + (VMEM,) * nctx,
        name="pack",
        compiler_params=pltpu.CompilerParams(vmem_limit_bytes=GRANT),
    )(residual, segments)
    return scal, parts


def join_kernel(scal, *refs):
    out = refs[-1]
    cols = refs[0].shape[1]
    for flip, part in enumerate(refs[:-1]):
        block = jnp.bitwise_xor(scal[0], flip)
        out[:, pl.ds(pl.multiple_of(block * cols, cols), cols)] = part[...]


def join(scal, parts):
    nctx = len(parts)
    shard, cols = parts[0].shape
    return pl.pallas_call(
        join_kernel,
        out_shape=jax.ShapeDtypeStruct((shard, nctx * cols), BF16),
        in_specs=[SMEM] + [VMEM] * nctx,
        out_specs=VMEM,
        name="join",
        compiler_params=pltpu.CompilerParams(vmem_limit_bytes=GRANT),
    )(scal, *parts)


def assemble_kernel(rows, shard, nctx, scal, *refs):
    out = refs[-1]
    ctx_index, mp_index = scal[0], scal[1]
    for flip, piece in enumerate(refs[:-1]):
        member = jnp.bitwise_xor(mp_index, flip)
        for step in range(nctx):
            block = jnp.bitwise_xor(ctx_index, step)
            first = pl.multiple_of(block * rows + member * shard, shard)
            out[pl.ds(first, shard), :] = piece[step * shard : (step + 1) * shard, :]


def assemble(scal, pieces, rows, shard, nctx):
    tokens = nctx * rows
    width = pieces[0].shape[1]
    return pl.pallas_call(
        functools.partial(assemble_kernel, rows, shard, nctx),
        out_shape=jax.ShapeDtypeStruct((tokens, width), BF16),
        in_specs=[SMEM] + [VMEM] * len(pieces),
        out_specs=VMEM,
        name="assemble",
        compiler_params=pltpu.CompilerParams(vmem_limit_bytes=GRANT),
    )(scal, *pieces)


def attend_kernel(nctx, back, steps, shard, scal, *refs):
    count = len(steps)
    q_refs, resid_refs = refs[:count], refs[count : 2 * count]
    kv, weight, keep, send, att, acc = refs[2 * count :]
    rows, width = att.shape
    heads = width // HD
    half = weight.shape[1] // 2
    ctx_index, mp_index, low, high = scal[0], scal[1], scal[2], scal[3]
    side = jnp.bitwise_and(mp_index, 1)
    window = min(back + 1, nctx) * rows
    scale = 1.0 / math.sqrt(HD)
    for j, step in enumerate(steps):
        block = jnp.bitwise_xor(ctx_index, step)
        first_key = pl.multiple_of(
            jnp.minimum(jnp.maximum(block - back, 0), nctx - window // rows) * rows, rows
        )
        qpos = block * rows + lax.broadcasted_iota(jnp.int32, (rows, 1), 0)
        start = segment_start(qpos, low, high)
        kpos = first_key + lax.broadcasted_iota(jnp.int32, (1, window), 1)
        allowed = (kpos <= qpos) & (kpos >= start) & (qpos - kpos < WIN)
        for h in range(heads):
            query = q_refs[j][:, h * HD : (h + 1) * HD]
            keys = kv[pl.ds(first_key, window), :HD]
            scores = lax.dot_general(
                query, keys, (((1,), (1,)), ((), ())), preferred_element_type=F32
            )
            scores = jnp.where(allowed, scores * scale, -1e30)
            top = jnp.max(scores, axis=1, keepdims=True)
            weights = jnp.exp(scores - top)
            total = jnp.sum(weights, axis=1, keepdims=True)
            values = kv[pl.ds(first_key, window), HD:]
            gathered = jnp.dot(weights.astype(BF16), values, preferred_element_type=F32)
            att[:, h * HD : (h + 1) * HD] = (gathered / total).astype(BF16)
        own = pl.ds(pl.multiple_of(mp_index * shard, shard), shard)
        for out, which in ((send, 1 - side), (keep, side)):
            cols = pl.ds(pl.multiple_of(which * half, half), half)
            acc[...] = jnp.dot(att[...], weight[:, cols], preferred_element_type=F32)
            acc[own, :] += resid_refs[j][:, cols].astype(F32)
            out[j * rows : (j + 1) * rows, :] = acc[...].astype(BF16)


def attend(scal, queries, residuals, kv, weight, nctx, back, steps, shard):
    rows, width = kv.shape[0] // nctx, queries[0].shape[1]
    count = len(steps)
    half = weight.shape[1] // 2
    shape = jax.ShapeDtypeStruct((count * rows, half), BF16)
    return pl.pallas_call(
        functools.partial(attend_kernel, nctx, back, steps, shard),
        out_shape=(shape, shape),
        in_specs=[SMEM] + [VMEM] * (2 * count + 2),
        out_specs=(VMEM, VMEM),
        scratch_shapes=[pltpu.VMEM((rows, width), BF16), pltpu.VMEM((rows, half), F32)],
        name="attend",
        compiler_params=pltpu.CompilerParams(vmem_limit_bytes=GRANT),
    )(scal, *queries, *residuals, kv, weight)


def split_weights(gain, weight, ctx_index, side):
    half = weight.shape[0] // 2
    out = []
    for which in (side, 1 - side):
        span = pl.multiple_of(which * half, half)
        cols = pl.ds(pl.multiple_of(ctx_index * 2 * half + span, half), half)
        out.append((gain[:, cols], weight[pl.ds(span, half), :]))
    return out


def project_kernel(count, scal, own, other, gain, weight, *outs):
    ctx_index, mp_index = scal[0], scal[1]
    side = jnp.bitwise_and(mp_index, 1)
    rows = own.shape[0] // count
    half = weight.shape[0] // 2
    shard = outs[1].shape[0]
    (gain_own, weight_own), (gain_other, weight_other) = split_weights(gain, weight, ctx_index, side)
    for j in range(count):
        span = slice(j * rows, (j + 1) * rows)
        scaled_own = (own[span, :].astype(F32) * gain_own).astype(BF16)
        scaled_other = (other[span, :].astype(F32) * gain_other).astype(BF16)
        outs[2 * j][...] = (
            jnp.dot(scaled_own, weight_own, preferred_element_type=F32)
            + jnp.dot(scaled_other, weight_other, preferred_element_type=F32)
        ).astype(BF16)
        mine = pl.ds(pl.multiple_of(j * rows + mp_index * shard, TILE), shard)
        for which, ref in ((side, own), (1 - side, other)):
            outs[2 * j + 1][:, pl.ds(pl.multiple_of(which * half, half), half)] = ref[mine, :]


def project(scal, own, other, gain, weight, count, shard):
    rows = own.shape[0] // count
    features, channels = weight.shape
    shapes = []
    for _ in range(count):
        shapes.append(jax.ShapeDtypeStruct((rows, channels), BF16))
        shapes.append(jax.ShapeDtypeStruct((shard, features), BF16))
    return pl.pallas_call(
        functools.partial(project_kernel, count),
        out_shape=tuple(shapes),
        in_specs=[SMEM] + [VMEM] * 4,
        out_specs=(VMEM,) * len(shapes),
        name="project",
        compiler_params=pltpu.CompilerParams(vmem_limit_bytes=GRANT),
    )(scal, own, other, gain, weight)


def tails_kernel(places, nhalves, rows, scal, *refs):
    nctx = len(places)
    halves, (gain, weight) = refs[:nhalves], refs[nhalves : nhalves + 2]
    outs = refs[nhalves + 2 : nhalves + 2 + nctx]
    edges, ends = refs[nhalves + 2 + nctx :]
    ctx_index = scal[0]
    side = jnp.bitwise_and(scal[1], 1)
    channels = weight.shape[1]
    half = weight.shape[0] // 2
    split = split_weights(gain, weight, ctx_index, side)
    ones = jnp.ones((SUB, half), BF16)

    def squares(piece):
        value = piece.astype(F32)
        return lax.dot_general(
            ones, (value * value).astype(BF16), (((1,), (1,)), ((), ())), preferred_element_type=F32
        )

    for flip, (at, first) in enumerate(places):
        block = jnp.bitwise_xor(ctx_index, flip)
        for k in range(2):
            piece = halves[2 * at + k][first + rows - LANES : first + rows, :]
            edges[k, pl.ds(pl.multiple_of(block * LANES, LANES), LANES), :] = piece
    sums = []
    for flip, (at, first) in enumerate(places):
        before = lax.rem(jnp.bitwise_xor(ctx_index, flip) + nctx - 1, nctx)
        main = edge = None
        for k in range(2):
            part = edges[k, pl.ds(pl.multiple_of(before * LANES, LANES), LANES), :]
            ends[k, flip * TILE : (flip + 1) * TILE, :] = part[LANES - TILE :, :]
            term, edge_term = squares(halves[2 * at + k][first : first + rows, :]), squares(part)
            main = term if main is None else main + term
            edge = edge_term if edge is None else edge + edge_term
        sums.append((main, edge))
    tails = None
    for k, (scale, matrix) in enumerate(split):
        term = jnp.dot(
            (ends[k].astype(F32) * scale).astype(BF16), matrix, preferred_element_type=F32
        )
        tails = term if tails is None else tails + term
    spare = channels - rows - LANES
    for flip, (main, edge) in enumerate(sums):
        pieces = [main, edge] + ([jnp.zeros((SUB, spare), F32)] if spare else [])
        line = jnp.concatenate(pieces, axis=1)
        coarse = line.astype(BF16).astype(F32)
        index = lax.broadcasted_iota(jnp.int32, line.shape, 0)
        line = jnp.where(index == 0, coarse, line - coarse)
        tail = tails[(flip + 1) * TILE - SUB : (flip + 1) * TILE, :]
        outs[flip][...] = jnp.concatenate([line, tail], axis=0).astype(BF16)


def tails(scal, halves, places, gain, weight, rows):
    nctx = len(places)
    half, channels = weight.shape[0] // 2, weight.shape[1]
    return pl.pallas_call(
        functools.partial(tails_kernel, places, len(halves), rows),
        out_shape=(jax.ShapeDtypeStruct((TILE, channels), BF16),) * nctx,
        in_specs=[SMEM] + [VMEM] * (len(halves) + 2),
        out_specs=(VMEM,) * nctx,
        scratch_shapes=[
            pltpu.VMEM((2, nctx * LANES, half), BF16),
            pltpu.VMEM((2, nctx * TILE, half), BF16),
        ],
        name="tails",
        compiler_params=pltpu.CompilerParams(vmem_limit_bytes=GRANT),
    )(scal, *halves, gain, weight)


def minus_expm1(x):
    series = jnp.full_like(x, 1.0 / 5040.0)
    for divisor in (720.0, 120.0, 24.0, 6.0, 2.0, 1.0):
        series = series * x + 1.0 / divisor
    return jnp.where(x > -0.3, -x * series, 1.0 - jnp.exp(x))


def recur_kernel(count, nlines, features, first, scal, *refs):
    mains, lines = refs[:count], refs[count : count + nlines]
    conv_w, decay_w, input_w, decay_b, input_b, codes = refs[count + nlines : count + nlines + 6]
    local_ref, cum_ref, last_ref, ext, keep_s, state_s, factor_s = refs[count + nlines + 6 :]
    rows, width = mains[0].shape
    ctx_index, low, high = scal[0], scal[2], scal[3]

    @pl.when(pl.program_id(0) == 0)
    def _():
        sums = None
        for line in lines:
            both = line[...].astype(F32)[0:2, : rows + LANES]
            term = both[0:1, :] + both[1:2, :]
            sums = term if sums is None else sums + term
        factor = lax.rsqrt(sums * (1.0 / features) + 1e-06)
        factor_s[...] = jnp.transpose(jnp.broadcast_to(factor, (LANES, rows + LANES)))

    lanes = pl.ds(pl.multiple_of((first + pl.program_id(0)) * width, width), width)
    main = tail = None
    for piece in mains:
        term = piece[...].astype(F32)
        main = term if main is None else main + term
    for line in lines:
        term = line[:, lanes].astype(F32)[SUB:, :]
        tail = term if tail is None else tail + term
    ext[0:SUB, :] = (tail * factor_s[rows + LANES - SUB :, 0:1]).astype(BF16).astype(F32)
    ext[SUB : SUB + rows, :] = (main * factor_s[:rows, 0:1]).astype(BF16).astype(F32)
    pos = ctx_index * rows + lax.broadcasted_iota(jnp.int32, (rows, 1), 0)
    start = segment_start(pos, low, high)
    conv = None
    for lag in range(CONV):
        shifted = ext[SUB - lag : SUB - lag + rows, :]
        term = conv_w[lag : lag + 1, :] * shifted
        if lag:
            term = jnp.where(pos - lag >= start, term, 0.0)
        conv = term if conv is None else conv + term
    conv = conv.astype(BF16)
    gate_d = jax.nn.sigmoid(
        jnp.dot(conv, decay_w[0], preferred_element_type=F32) + decay_b[...]
    )
    gate_i = jax.nn.sigmoid(
        jnp.dot(conv, input_w[0], preferred_element_type=F32) + input_b[...]
    )
    rate = 0.006 * jnp.exp(-codes[...].astype(F32) * (math.log(3000.0) / (LEVELS - 1)))
    log_decay = -8.0 * gate_d * rate
    restart = pos == start
    keep = jnp.where(restart, 0.0, jnp.exp(log_decay))
    scale = jnp.where(restart, 1.0, jnp.sqrt(minus_expm1(2.0 * log_decay)))
    state = scale * gate_i * conv.astype(F32)
    tiles = rows // SUB
    keep = keep.reshape(tiles, SUB, width)
    state = state.reshape(tiles, SUB, width)
    index = lax.broadcasted_iota(jnp.int32, (tiles, SUB, width), 1)
    shift = 1
    while shift < SUB:
        inside = index >= shift
        prior_keep = jnp.where(inside, pltpu.roll(keep, shift, 1), 1.0)
        prior_state = jnp.where(inside, pltpu.roll(state, shift, 1), 0.0)
        state = keep * prior_state + state
        keep = keep * prior_keep
        shift *= 2
    keep_s[...] = keep
    state_s[...] = state
    run_keep = jnp.ones((1, width), F32)
    run_state = jnp.zeros((1, width), F32)
    for t in range(tiles):
        keep_t, state_t = keep_s[t], state_s[t]
        new_state = state_t + keep_t * run_state
        new_keep = keep_t * run_keep
        local_ref[t * SUB : (t + 1) * SUB, :] = new_state
        cum_ref[t * SUB : (t + 1) * SUB, :] = new_keep
        run_state, run_keep = new_state[SUB - 1 :, :], new_keep[SUB - 1 :, :]
    line = lax.broadcasted_iota(jnp.int32, (SUB, width), 0)
    last_ref[...] = jnp.where(line == 0, run_keep, run_state)


def recur(scal, mains, lines, conv_w, decay_w, input_w, decay_b, input_b, codes, features, first, count):
    channels = conv_w.shape[1]
    rows = mains[0].shape[0]
    tiles = rows // SUB
    main_specs = [
        pl.BlockSpec(
            (rows, BW), functools.partial(lambda at, j: (0, at + j), first if m.shape[1] == channels else 0)
        )
        for m in mains
    ]
    by_block = pl.BlockSpec((rows, BW), lambda j: (0, j))
    row_spec = pl.BlockSpec((1, BW), lambda j: (0, first + j))
    gate_spec = pl.BlockSpec((1, BW, BW), lambda j: (first + j, 0, 0))
    line_spec = pl.BlockSpec((TILE, channels), lambda j: (0, 0))
    full = jax.ShapeDtypeStruct((rows, count * BW), F32)
    return pl.pallas_call(
        functools.partial(recur_kernel, len(mains), len(lines), features, first),
        grid=(count,),
        out_shape=(full, full, jax.ShapeDtypeStruct((SUB, count * BW), F32)),
        in_specs=[SMEM]
        + main_specs
        + [line_spec] * len(lines)
        + [pl.BlockSpec((CONV, BW), lambda j: (0, first + j)), gate_spec, gate_spec]
        + [row_spec] * 3,
        out_specs=(by_block, by_block, pl.BlockSpec((SUB, BW), lambda j: (0, j))),
        scratch_shapes=[
            pltpu.VMEM((rows + SUB, BW), F32),
            pltpu.VMEM((tiles, SUB, BW), F32),
            pltpu.VMEM((tiles, SUB, BW), F32),
            pltpu.VMEM((rows + LANES, LANES), F32),
        ],
        name="recur",
        compiler_params=pltpu.CompilerParams(vmem_limit_bytes=GRANT),
    )(scal, *mains, *lines, conv_w, decay_w, input_w, decay_b, input_b, codes)


def finish_kernel(parts, scal, *refs):
    states, cums, before, out = refs[:parts], refs[parts : 2 * parts], refs[2 * parts : -1], refs[-1]
    incoming = jnp.zeros((1, out.shape[1]), F32)
    for step in range(len(before), 0, -1):
        piece = before[step - 1]
        incoming = piece[0:1, :] * incoming + piece[1:2, :]
        incoming = jnp.where(scal[0] >= step, incoming, 0.0)
    first = 0
    for state, cum in zip(states, cums):
        stop = first + state.shape[1]
        out[:, first:stop] = (state[...] + cum[...] * incoming[:, first:stop]).astype(BF16)
        first = stop


def finish(scal, states, cums, before):
    rows = states[0].shape[0]
    channels = before[0].shape[1]
    return pl.pallas_call(
        functools.partial(finish_kernel, len(states)),
        out_shape=jax.ShapeDtypeStruct((rows, channels), BF16),
        in_specs=[SMEM] + [VMEM] * (2 * len(states) + len(before)),
        out_specs=VMEM,
        name="finish",
        compiler_params=pltpu.CompilerParams(vmem_limit_bytes=GRANT),
    )(scal, *states, *cums, *before)


def local_near(
    queries,
    keyvals,
    segment_ids,
    residual,
    out_weight,
    lru_weight,
    conv_weight,
    gate_decay_w,
    gate_input_w,
    gate_decay_b,
    gate_input_b,
    decay_codes,
    norm_gain,
):
    rows = queries.shape[0]
    shard = keyvals.shape[0]
    tokens = segment_ids.shape[0]
    nctx, nmp = lax.axis_size("ctx"), lax.axis_size("mp")
    features = residual.shape[1]
    cols = out_weight.shape[1]
    longest = tokens // 2
    back = -(-(min(WIN, longest) - 1) // rows)
    reach = min(nctx - 1, -(-longest // rows))

    visiting = {0: queries}
    for flip in range(nctx - 1, 0, -2):
        visiting[flip] = swapped(queries, "ctx", flip)
    for flip in range(nctx - 2, 0, -2):
        visiting[flip] = swapped(visiting[flip + 1], "ctx", 1)
    kv_parts = [keyvals]
    for flip in range(1, nctx):
        kv_parts.append(swapped(keyvals, "ctx", flip))
    scal, resid_parts = pack(residual, segment_ids.reshape(-1, LANES), nctx)
    for flip in range(1, nctx):
        resid_parts[flip] = swapped(resid_parts[flip], "ctx", flip)
    pieces = {0: jnp.concatenate(kv_parts, axis=0)}
    flip = nmp // 2
    while flip >= 1:
        for done in sorted(pieces):
            pieces[done | flip] = swapped(pieces[done], "mp", flip)
        flip //= 2
    kv = assemble(scal, [pieces[e] for e in range(nmp)], rows, shard, nctx)
    chunks = [0] + list(range(nctx - 1, 2, -2)) + [1] + list(range(nctx - 2, 1, -2))
    gain = norm_gain.reshape(1, features)
    halves, places = [], {}
    messages, give = {}, {}
    for at, e in enumerate(chunks):
        keep, send = attend(
            scal, [visiting[e]], [resid_parts[e]], kv, out_weight, nctx, back, (e,), shard
        )
        other = swapped(send, "mp", 1)
        mine = (keep.astype(F32) + other.astype(F32)).astype(BF16)
        flip = 2
        while flip < nmp:
            other = swapped(mine, "mp", flip)
            mine = (mine.astype(F32) + other.astype(F32)).astype(BF16)
            flip *= 2
        other = swapped(mine, "mp", 1)
        halves += [mine, other]
        places[e] = (at, 0)
        messages[e], give[e] = project(scal, mine, other, gain, lru_weight, 1, shard)
    lines = list(tails(scal, halves, [places[e] for e in range(nctx)], gain, lru_weight, rows))
    blocks = lru_weight.shape[1] // BW
    parts = 2 if blocks % 2 == 0 else 1
    span = lru_weight.shape[1] // parts
    mains = [[messages[0]] for _ in range(parts)]
    for flip in range(nctx - 1, 0, -1):
        if flip % 2 and flip > 1:
            passed = swapped(messages[flip], "ctx", 1)
            merged = []
            for part in range(parts):
                cols = slice(part * span, (part + 1) * span)
                both = messages[flip - 1][:, cols].astype(F32) + passed[:, cols].astype(F32)
                merged.append(both.astype(BF16))
            messages[flip - 1] = merged
        elif flip > 1:
            for part in range(parts):
                mains[part].append(swapped(messages[flip][part], "ctx", flip))
        else:
            got = swapped(messages[1], "ctx", 1)
            for main in mains:
                main.append(got)
    for flip in range(1, nctx):
        lines[flip] = swapped(lines[flip], "ctx", flip)
    given = [give[0]]
    for flip in range(1, nctx):
        given.append(swapped(give[flip], "ctx", flip))
    states, cums, lasts = [], [], []
    for part in range(parts):
        state, cum, last = recur(
            scal,
            mains[part],
            lines,
            conv_weight,
            gate_decay_w,
            gate_input_w,
            gate_decay_b.reshape(1, -1),
            gate_input_b.reshape(1, -1),
            decay_codes.reshape(1, -1),
            features,
            part * blocks // parts,
            blocks // parts,
        )
        states.append(state)
        cums.append(cum)
        lasts.append(last)
    last = jnp.concatenate(lasts, axis=1)
    before = []
    for step in range(1, reach + 1):
        before.append(rotated(last, "ctx", -step))
    resid_out = join(scal, given)
    out = finish(scal, states, cums, before)
    return (resid_out, out)


def local(queries, keyvals, segment_ids, residual, out_weight, *rest):
    nctx = lax.axis_size("ctx")
    near = (
        segment_ids.shape[0] <= WIN
        and nctx > 1
        and nctx & (nctx - 1) == 0
        and lax.axis_size("mp") % 2 == 0
        and queries.shape[1] == out_weight.shape[1]
    )
    form = local_near if near else local_wide
    return form(queries, keyvals, segment_ids, residual, out_weight, *rest)


def solution(mesh):
    in_specs = (
        P(("groups", "ctx"), "mp"),
        P(("groups", "ctx", "mp"), None),
        P("groups"),
        P(("groups", "ctx", "mp"), None),
        P("mp", "ctx"),
        P("ctx", "mp"),
        P(None, "mp"),
        P("mp", None, None),
        P("mp", None, None),
        P("mp"),
        P("mp"),
        P("mp"),
        P(),
    )
    out_specs = (P(("groups", "ctx", "mp"), None), P(("groups", "ctx"), "mp"))
    return jax.shard_map(local, mesh=mesh, in_specs=in_specs, out_specs=out_specs, check_vma=False)
```

```python
import functools
import math

import jax
import jax.numpy as jnp
from jax import lax
from jax.experimental import pallas as pl
from jax.experimental.pallas import tpu as pltpu
from jax.sharding import PartitionSpec as P

HD = 256
WIN = 2048
CONV = 4
LEVELS = 16
BW = 256


def shifted_2(value, axis, steps):
    count = lax.axis_size(axis)
    initial, last = (max(0, -steps), min(count, count - steps))
    return lax.ppermute(value, axis, [(source, source + steps) for source in range(initial, last)])


def decay_rates():
    levels = jnp.arange(LEVELS, dtype=jnp.float32)
    return 0.006 * jnp.exp(-levels * (math.log(3000.0) / (LEVELS - 1)))


def chain_link(former, latter):
    return (former[0] * latter[0], latter[0] * former[1] + latter[1])


def rms_scaled(values, norm_gain):
    value_f32 = values.astype(jnp.float32)
    inverse = lax.rsqrt(jnp.mean(value_f32 * value_f32, axis=-1, keepdims=True) + 1e-06)
    return (value_f32 * inverse * norm_gain).astype(jnp.bfloat16)


def attend_local(queries, keys_all, allowed):
    rows_here = queries.shape[0]
    heads_here = queries.shape[1] // HD
    query_heads = queries.reshape(rows_here, heads_here, HD)
    score_scale = 1.0 / math.sqrt(HD)
    scores = (
        jnp.einsum("thd,kd->htk", query_heads, keys_all[:, :HD], preferred_element_type=jnp.float32)
        * score_scale
    )
    scores = jnp.where(allowed[None], scores, -1e30)
    row_top = jnp.max(scores, axis=-1, keepdims=True)
    weights = jnp.exp(scores - row_top)
    probs = (weights / jnp.sum(weights, axis=-1, keepdims=True)).astype(jnp.bfloat16)
    gathered = jnp.einsum(
        "htk,kd->thd", probs, keys_all[:, HD:], preferred_element_type=jnp.float32
    )
    return gathered.reshape(rows_here, heads_here * HD).astype(jnp.bfloat16)


def local_wide(
    queries,
    keyvals,
    segment_ids,
    residual,
    out_weight,
    lru_weight,
    conv_weight,
    gate_decay_w,
    gate_input_w,
    gate_decay_b,
    gate_input_b,
    decay_codes,
    norm_gain,
):
    rows_here = queries.shape[0]
    ctx_index = lax.axis_index("ctx")
    back_blocks = WIN // rows_here
    own_kv = lax.all_gather(keyvals, "mp", axis=0, tiled=True)
    earlier = []
    moving = own_kv
    for _ in range(back_blocks):
        moving = shifted_2(moving, "ctx", 1)
        earlier = [moving] + earlier
    keys_all = jnp.concatenate(earlier + [own_kv], axis=0)
    pad_seg = jnp.concatenate([jnp.full((WIN,), -1, jnp.int32), segment_ids])
    query_seg = lax.dynamic_slice_in_dim(segment_ids, ctx_index * rows_here, rows_here)
    key_seg = lax.dynamic_slice_in_dim(
        pad_seg, ctx_index * rows_here, (back_blocks + 1) * rows_here
    )
    query_pos = ctx_index * rows_here + jnp.arange(rows_here, dtype=jnp.int32)
    key_pos = (ctx_index - back_blocks) * rows_here + jnp.arange(
        (back_blocks + 1) * rows_here, dtype=jnp.int32
    )
    distance = query_pos[:, None] - key_pos[None, :]
    allowed = (distance >= 0) & (distance < WIN) & (query_seg[:, None] == key_seg[None, :])
    attended = attend_local(queries, keys_all, allowed)
    head_part = jnp.dot(
        attended,
        lax.all_gather(out_weight, "ctx", axis=1, tiled=True),
        preferred_element_type=jnp.float32,
    )
    summed = lax.psum_scatter(
        head_part.astype(jnp.bfloat16), "mp", scatter_dimension=0, tiled=True
    ).astype(jnp.float32)
    resid_out = (summed + residual.astype(jnp.float32)).astype(jnp.bfloat16)
    normed = lax.all_gather(rms_scaled(resid_out, norm_gain), "mp", axis=0, tiled=True)
    channels = lru_weight.shape[1]
    lru_in = jnp.dot(
        normed,
        lax.all_gather(lru_weight, "ctx", axis=0, tiled=True),
        preferred_element_type=jnp.float32,
    ).astype(jnp.bfloat16)
    rim_rows = shifted_2(lru_in[rows_here - (CONV - 1) :], "ctx", 1)
    extended = jnp.concatenate([rim_rows, lru_in], axis=0)
    ext_seg = lax.dynamic_slice_in_dim(
        pad_seg, ctx_index * rows_here + WIN - (CONV - 1), rows_here + CONV - 1
    )
    conv_acc = jnp.zeros((rows_here, channels), jnp.float32)
    for offset in range(CONV):
        lag_rows = CONV - 1 - offset
        shifted = extended[lag_rows : lag_rows + rows_here].astype(jnp.float32)
        same_doc = (ext_seg[lag_rows : lag_rows + rows_here] == query_seg)[:, None]
        conv_acc = conv_acc + jnp.where(same_doc, conv_weight[offset] * shifted, 0.0)
    conv_out = conv_acc.astype(jnp.bfloat16)
    blocks_here = channels // BW
    grouped = conv_out.reshape(rows_here, blocks_here, BW)
    decay_gate = jax.nn.sigmoid(
        jnp.einsum(
            "tbi,bij->tbj", grouped, gate_decay_w, preferred_element_type=jnp.float32
        ).reshape(rows_here, channels)
        + gate_decay_b
    )
    input_gate = jax.nn.sigmoid(
        jnp.einsum(
            "tbi,bij->tbj", grouped, gate_input_w, preferred_element_type=jnp.float32
        ).reshape(rows_here, channels)
        + gate_input_b
    )
    levels = jnp.arange(LEVELS, dtype=jnp.int32)
    decay_rate = jnp.sum(
        jnp.where(decay_codes[:, None] == levels[None, :], decay_rates()[None, :], 0.0), axis=1
    )
    log_decay = -8.0 * decay_gate * decay_rate
    restart = (query_seg != ext_seg[CONV - 2 : CONV - 2 + rows_here])[:, None]
    keep_factor = jnp.where(restart, 0.0, jnp.exp(log_decay))
    input_scale = jnp.where(restart, 1.0, jnp.sqrt(-jnp.expm1(2.0 * log_decay)))
    driven = input_scale * input_gate * conv_out.astype(jnp.float32)
    cum_keep, local_state = lax.associative_scan(chain_link, (keep_factor, driven), axis=0)
    block_keep = cum_keep[rows_here - 1]
    block_state = local_state[rows_here - 1]

    def relay_turn(turn_index, state_in):
        return shifted_2(block_keep * state_in + block_state, "ctx", 1)

    incoming = lax.fori_loop(0, lax.axis_size("ctx") - 1, relay_turn, jnp.zeros_like(block_state))
    states = local_state + cum_keep * incoming[None, :]
    return (resid_out, states.astype(jnp.bfloat16))


F32 = jnp.float32
BF16 = jnp.bfloat16
VMEM = pl.BlockSpec(memory_space=pltpu.VMEM)
SMEM = pl.BlockSpec(memory_space=pltpu.SMEM)
TILE = 16
SUB = 8
LANES = 128
GRANT = 20 << 20


def rotated(value, axis, steps):
    count = lax.axis_size(axis)
    return lax.ppermute(value, axis, [(s, (s - steps) % count) for s in range(count)])


def swapped(value, axis, flip):
    count = lax.axis_size(axis)
    return lax.ppermute(value, axis, [(s, s ^ flip) for s in range(count)])


def segment_start(pos, low, high):
    return jnp.where(pos >= high, high, jnp.where(pos >= low, low, 0))


def pack_kernel(residual, segments, scal, *outs):
    cols = outs[0].shape[1]
    ctx_index = lax.axis_index("ctx")
    ids = segments[...]
    scal[0] = ctx_index
    scal[1] = lax.axis_index("mp")
    for at in (1, 2):
        scal[at + 1] = jnp.sum((ids < at).astype(F32)).astype(jnp.int32)
    for flip, out in enumerate(outs):
        block = jnp.bitwise_xor(ctx_index, flip)
        out[...] = residual[:, pl.ds(pl.multiple_of(block * cols, cols), cols)]


def pack(residual, segments, nctx):
    shard, width = residual.shape
    part = jax.ShapeDtypeStruct((shard, width // nctx), BF16)
    scal, *parts = pl.pallas_call(
        pack_kernel,
        out_shape=(jax.ShapeDtypeStruct((4,), jnp.int32),) + (part,) * nctx,
        in_specs=[VMEM, VMEM],
        out_specs=(SMEM,) + (VMEM,) * nctx,
        name="pack",
        compiler_params=pltpu.CompilerParams(vmem_limit_bytes=GRANT),
    )(residual, segments)
    return scal, parts


def join_kernel(scal, *refs):
    out = refs[-1]
    cols = refs[0].shape[1]
    for flip, part in enumerate(refs[:-1]):
        block = jnp.bitwise_xor(scal[0], flip)
        out[:, pl.ds(pl.multiple_of(block * cols, cols), cols)] = part[...]


def join(scal, parts):
    nctx = len(parts)
    shard, cols = parts[0].shape
    return pl.pallas_call(
        join_kernel,
        out_shape=jax.ShapeDtypeStruct((shard, nctx * cols), BF16),
        in_specs=[SMEM] + [VMEM] * nctx,
        out_specs=VMEM,
        name="join",
        compiler_params=pltpu.CompilerParams(vmem_limit_bytes=GRANT),
    )(scal, *parts)


def assemble_kernel(rows, shard, nctx, scal, *refs):
    out = refs[-1]
    ctx_index, mp_index = scal[0], scal[1]
    for flip, piece in enumerate(refs[:-1]):
        member = jnp.bitwise_xor(mp_index, flip)
        for step in range(nctx):
            block = jnp.bitwise_xor(ctx_index, step)
            first = pl.multiple_of(block * rows + member * shard, shard)
            out[pl.ds(first, shard), :] = piece[step * shard : (step + 1) * shard, :]


def assemble(scal, pieces, rows, shard, nctx):
    tokens = nctx * rows
    width = pieces[0].shape[1]
    return pl.pallas_call(
        functools.partial(assemble_kernel, rows, shard, nctx),
        out_shape=jax.ShapeDtypeStruct((tokens, width), BF16),
        in_specs=[SMEM] + [VMEM] * len(pieces),
        out_specs=VMEM,
        name="assemble",
        compiler_params=pltpu.CompilerParams(vmem_limit_bytes=GRANT),
    )(scal, *pieces)


def attend_kernel(nctx, back, steps, shard, count_resid, scal, *refs):
    count = len(steps)
    q_refs, resid_refs = refs[:count], refs[count : count + count_resid]
    kv, weight, keep, send, att, acc = refs[count + count_resid :]
    rows, width = att.shape
    heads = width // HD
    half = weight.shape[1] // 2
    ctx_index, mp_index, low, high = scal[0], scal[1], scal[2], scal[3]
    side = jnp.bitwise_and(mp_index, 1)
    window = min(back + 1, nctx) * rows
    scale = math.log2(math.e) / math.sqrt(HD)
    for j, step in enumerate(steps):
        block = jnp.bitwise_xor(ctx_index, step)
        first_key = pl.multiple_of(
            jnp.minimum(jnp.maximum(block - back, 0), nctx - window // rows) * rows, rows
        )
        qpos = block * rows + lax.broadcasted_iota(jnp.int32, (rows, 1), 0)
        start = segment_start(qpos, low, high)
        kpos = first_key + lax.broadcasted_iota(jnp.int32, (1, window), 1)
        allowed = (kpos <= qpos) & (kpos >= jnp.maximum(start, qpos - (WIN - 1)))
        for h in range(heads):
            query = q_refs[j][:, h * HD : (h + 1) * HD]
            keys = kv[pl.ds(first_key, window), :HD]
            scores = lax.dot_general(
                query, keys, (((1,), (1,)), ((), ())), preferred_element_type=F32
            )
            scores = jnp.where(allowed, scores, -1e30)
            top = jnp.max(scores, axis=1, keepdims=True)
            weights = jnp.exp2((scores - top) * scale)
            total = jnp.sum(weights, axis=1, keepdims=True)
            values = kv[pl.ds(first_key, window), HD:]
            gathered = jnp.dot(weights.astype(BF16), values, preferred_element_type=F32)
            att[:, h * HD : (h + 1) * HD] = (gathered / total).astype(BF16)
        own = pl.ds(pl.multiple_of(mp_index * shard, shard), shard)
        for out, which in ((send, 1 - side), (keep, side)):
            cols = pl.ds(pl.multiple_of(which * half, half), half)
            acc[...] = jnp.dot(att[...], weight[:, cols], preferred_element_type=F32)
            if count_resid:
                acc[own, :] += resid_refs[j][:, cols].astype(F32)
            out[j * rows : (j + 1) * rows, :] = acc[...].astype(BF16)


def attend(scal, queries, residuals, kv, weight, nctx, back, steps, shard):
    rows, width = kv.shape[0] // nctx, queries[0].shape[1]
    count = len(steps)
    half = weight.shape[1] // 2
    shape = jax.ShapeDtypeStruct((count * rows, half), BF16)
    return pl.pallas_call(
        functools.partial(attend_kernel, nctx, back, steps, shard, len(residuals)),
        out_shape=(shape, shape),
        in_specs=[SMEM] + [VMEM] * (count + len(residuals) + 2),
        out_specs=(VMEM, VMEM),
        scratch_shapes=[pltpu.VMEM((rows, width), BF16), pltpu.VMEM((rows, half), F32)],
        name="attend",
        compiler_params=pltpu.CompilerParams(vmem_limit_bytes=GRANT),
    )(scal, *queries, *residuals, kv, weight)


def topped_kernel(shard, scal, keep, send, resid, keep_out, send_out):
    half = keep.shape[1]
    side = jnp.bitwise_and(scal[1], 1)
    own = pl.ds(pl.multiple_of(scal[1] * shard, shard), shard)
    for piece, out, which in ((send, send_out, 1 - side), (keep, keep_out, side)):
        cols = pl.ds(pl.multiple_of(which * half, half), half)
        out[...] = piece[...]
        out[own, :] = (piece[own, :].astype(F32) + resid[:, cols].astype(F32)).astype(BF16)


def topped(scal, keep, send, resid):
    shape = jax.ShapeDtypeStruct(keep.shape, BF16)
    return pl.pallas_call(
        functools.partial(topped_kernel, resid.shape[0]),
        out_shape=(shape, shape),
        in_specs=[SMEM] + [VMEM] * 3,
        out_specs=(VMEM, VMEM),
        name="topped",
        compiler_params=pltpu.CompilerParams(vmem_limit_bytes=GRANT),
    )(scal, keep, send, resid)


def split_weights(gain, weight, ctx_index, side):
    half = weight.shape[0] // 2
    out = []
    for which in (side, 1 - side):
        span = pl.multiple_of(which * half, half)
        cols = pl.ds(pl.multiple_of(ctx_index * 2 * half + span, half), half)
        out.append((gain[:, cols], weight[pl.ds(span, half), :]))
    return out


def project_kernel(count, scal, own, other, gain, weight, *outs):
    ctx_index, mp_index = scal[0], scal[1]
    side = jnp.bitwise_and(mp_index, 1)
    rows = own.shape[0] // count
    half = weight.shape[0] // 2
    shard = outs[1].shape[0]
    (gain_own, weight_own), (gain_other, weight_other) = split_weights(gain, weight, ctx_index, side)
    for j in range(count):
        span = slice(j * rows, (j + 1) * rows)
        scaled_own = (own[span, :].astype(F32) * gain_own).astype(BF16)
        scaled_other = (other[span, :].astype(F32) * gain_other).astype(BF16)
        outs[2 * j][...] = (
            jnp.dot(scaled_own, weight_own, preferred_element_type=F32)
            + jnp.dot(scaled_other, weight_other, preferred_element_type=F32)
        ).astype(BF16)
        mine = pl.ds(pl.multiple_of(j * rows + mp_index * shard, TILE), shard)
        for which, ref in ((side, own), (1 - side, other)):
            outs[2 * j + 1][:, pl.ds(pl.multiple_of(which * half, half), half)] = ref[mine, :]


def project(scal, own, other, gain, weight, count, shard):
    rows = own.shape[0] // count
    features, channels = weight.shape
    shapes = []
    for _ in range(count):
        shapes.append(jax.ShapeDtypeStruct((rows, channels), BF16))
        shapes.append(jax.ShapeDtypeStruct((shard, features), BF16))
    return pl.pallas_call(
        functools.partial(project_kernel, count),
        out_shape=tuple(shapes),
        in_specs=[SMEM] + [VMEM] * 4,
        out_specs=(VMEM,) * len(shapes),
        name="project",
        compiler_params=pltpu.CompilerParams(vmem_limit_bytes=GRANT),
    )(scal, own, other, gain, weight)


def tails_kernel(places, nhalves, rows, scal, *refs):
    nctx = len(places)
    halves, (gain, weight) = refs[:nhalves], refs[nhalves : nhalves + 2]
    outs = refs[nhalves + 2 : nhalves + 2 + nctx]
    edges, ends = refs[nhalves + 2 + nctx :]
    ctx_index = scal[0]
    side = jnp.bitwise_and(scal[1], 1)
    channels = weight.shape[1]
    half = weight.shape[0] // 2
    split = split_weights(gain, weight, ctx_index, side)
    ones = jnp.ones((SUB, half), BF16)

    def squares(piece):
        value = piece.astype(F32)
        return lax.dot_general(
            ones, (value * value).astype(BF16), (((1,), (1,)), ((), ())), preferred_element_type=F32
        )

    for flip, (at, first) in enumerate(places):
        block = jnp.bitwise_xor(ctx_index, flip)
        for k in range(2):
            piece = halves[2 * at + k][first + rows - LANES : first + rows, :]
            edges[k, pl.ds(pl.multiple_of(block * LANES, LANES), LANES), :] = piece
    sums = []
    for flip, (at, first) in enumerate(places):
        before = lax.rem(jnp.bitwise_xor(ctx_index, flip) + nctx - 1, nctx)
        main = edge = None
        for k in range(2):
            part = edges[k, pl.ds(pl.multiple_of(before * LANES, LANES), LANES), :]
            ends[k, flip * TILE : (flip + 1) * TILE, :] = part[LANES - TILE :, :]
            term, edge_term = squares(halves[2 * at + k][first : first + rows, :]), squares(part)
            main = term if main is None else main + term
            edge = edge_term if edge is None else edge + edge_term
        sums.append((main, edge))
    tails = None
    for k, (scale, matrix) in enumerate(split):
        term = jnp.dot(
            (ends[k].astype(F32) * scale).astype(BF16), matrix, preferred_element_type=F32
        )
        tails = term if tails is None else tails + term
    spare = channels - rows - LANES
    for flip, (main, edge) in enumerate(sums):
        pieces = [main, edge] + ([jnp.zeros((SUB, spare), F32)] if spare else [])
        line = jnp.concatenate(pieces, axis=1)
        coarse = line.astype(BF16).astype(F32)
        index = lax.broadcasted_iota(jnp.int32, line.shape, 0)
        line = jnp.where(index == 0, coarse, line - coarse)
        tail = tails[(flip + 1) * TILE - SUB : (flip + 1) * TILE, :]
        outs[flip][...] = jnp.concatenate([line, tail], axis=0).astype(BF16)


def tails(scal, halves, places, gain, weight, rows):
    nctx = len(places)
    half, channels = weight.shape[0] // 2, weight.shape[1]
    return pl.pallas_call(
        functools.partial(tails_kernel, places, len(halves), rows),
        out_shape=(jax.ShapeDtypeStruct((TILE, channels), BF16),) * nctx,
        in_specs=[SMEM] + [VMEM] * (len(halves) + 2),
        out_specs=(VMEM,) * nctx,
        scratch_shapes=[
            pltpu.VMEM((2, nctx * LANES, half), BF16),
            pltpu.VMEM((2, nctx * TILE, half), BF16),
        ],
        name="tails",
        compiler_params=pltpu.CompilerParams(vmem_limit_bytes=GRANT),
    )(scal, *halves, gain, weight)


def minus_expm1(x):
    series = jnp.full_like(x, 1.0 / 5040.0)
    for divisor in (720.0, 120.0, 24.0, 6.0, 2.0, 1.0):
        series = series * x + 1.0 / divisor
    return jnp.where(x > -0.3, -x * series, 1.0 - jnp.exp(x))


def recur_kernel(count, nlines, features, first, scal, *refs):
    mains, lines = refs[:count], refs[count : count + nlines]
    conv_w, decay_w, input_w, decay_b, input_b, codes = refs[count + nlines : count + nlines + 6]
    local_ref, cum_ref, last_ref, ext, keep_s, state_s, factor_s = refs[count + nlines + 6 :]
    rows, width = mains[0].shape
    ctx_index, low, high = scal[0], scal[2], scal[3]

    @pl.when(pl.program_id(0) == 0)
    def _():
        sums = None
        for line in lines:
            both = line[...].astype(F32)[0:2, : rows + LANES]
            term = both[0:1, :] + both[1:2, :]
            sums = term if sums is None else sums + term
        factor = lax.rsqrt(sums * (1.0 / features) + 1e-06)
        factor_s[...] = jnp.transpose(jnp.broadcast_to(factor, (LANES, rows + LANES)))

    lanes = pl.ds(pl.multiple_of((first + pl.program_id(0)) * width, width), width)
    main = tail = None
    for piece in mains:
        term = piece[...].astype(F32)
        main = term if main is None else main + term
    for line in lines:
        term = line[:, lanes].astype(F32)[SUB:, :]
        tail = term if tail is None else tail + term
    ext[0:SUB, :] = (tail * factor_s[rows + LANES - SUB :, 0:1]).astype(BF16).astype(F32)
    ext[SUB : SUB + rows, :] = (main * factor_s[:rows, 0:1]).astype(BF16).astype(F32)
    pos = ctx_index * rows + lax.broadcasted_iota(jnp.int32, (rows, 1), 0)
    start = segment_start(pos, low, high)
    conv = None
    for lag in range(CONV):
        shifted = ext[SUB - lag : SUB - lag + rows, :]
        term = conv_w[lag : lag + 1, :] * shifted
        if lag:
            term = jnp.where(pos - lag >= start, term, 0.0)
        conv = term if conv is None else conv + term
    conv = conv.astype(BF16)
    gate_d = jax.nn.sigmoid(
        jnp.dot(conv, decay_w[0], preferred_element_type=F32) + decay_b[...]
    )
    gate_i = jax.nn.sigmoid(
        jnp.dot(conv, input_w[0], preferred_element_type=F32) + input_b[...]
    )
    rate = 0.006 * jnp.exp(-codes[...].astype(F32) * (math.log(3000.0) / (LEVELS - 1)))
    log_decay = -8.0 * gate_d * rate
    restart = pos == start
    keep = jnp.where(restart, 0.0, jnp.exp(log_decay))
    scale = jnp.where(restart, 1.0, jnp.sqrt(minus_expm1(2.0 * log_decay)))
    state = scale * gate_i * conv.astype(F32)
    tiles = rows // SUB
    keep = keep.reshape(tiles, SUB, width)
    state = state.reshape(tiles, SUB, width)
    index = lax.broadcasted_iota(jnp.int32, (tiles, SUB, width), 1)
    shift = 1
    while shift < SUB:
        inside = index >= shift
        prior_keep = jnp.where(inside, pltpu.roll(keep, shift, 1), 1.0)
        prior_state = jnp.where(inside, pltpu.roll(state, shift, 1), 0.0)
        state = keep * prior_state + state
        keep = keep * prior_keep
        shift *= 2
    keep_s[...] = keep
    state_s[...] = state
    run_keep = jnp.ones((1, width), F32)
    run_state = jnp.zeros((1, width), F32)
    for t in range(tiles):
        keep_t, state_t = keep_s[t], state_s[t]
        new_state = state_t + keep_t * run_state
        new_keep = keep_t * run_keep
        local_ref[t * SUB : (t + 1) * SUB, :] = new_state
        cum_ref[t * SUB : (t + 1) * SUB, :] = new_keep
        run_state, run_keep = new_state[SUB - 1 :, :], new_keep[SUB - 1 :, :]
    line = lax.broadcasted_iota(jnp.int32, (SUB, width), 0)
    last_ref[...] = jnp.where(line == 0, run_keep, run_state)


def recur(scal, mains, lines, conv_w, decay_w, input_w, decay_b, input_b, codes, features, first, count):
    channels = conv_w.shape[1]
    rows = mains[0].shape[0]
    tiles = rows // SUB
    main_specs = [
        pl.BlockSpec(
            (rows, BW), functools.partial(lambda at, j: (0, at + j), first if m.shape[1] == channels else 0)
        )
        for m in mains
    ]
    by_block = pl.BlockSpec((rows, BW), lambda j: (0, j))
    row_spec = pl.BlockSpec((1, BW), lambda j: (0, first + j))
    gate_spec = pl.BlockSpec((1, BW, BW), lambda j: (first + j, 0, 0))
    line_spec = pl.BlockSpec((TILE, channels), lambda j: (0, 0))
    full = jax.ShapeDtypeStruct((rows, count * BW), F32)
    return pl.pallas_call(
        functools.partial(recur_kernel, len(mains), len(lines), features, first),
        grid=(count,),
        out_shape=(full, full, jax.ShapeDtypeStruct((SUB, count * BW), F32)),
        in_specs=[SMEM]
        + main_specs
        + [line_spec] * len(lines)
        + [pl.BlockSpec((CONV, BW), lambda j: (0, first + j)), gate_spec, gate_spec]
        + [row_spec] * 3,
        out_specs=(by_block, by_block, pl.BlockSpec((SUB, BW), lambda j: (0, j))),
        scratch_shapes=[
            pltpu.VMEM((rows + SUB, BW), F32),
            pltpu.VMEM((tiles, SUB, BW), F32),
            pltpu.VMEM((tiles, SUB, BW), F32),
            pltpu.VMEM((rows + LANES, LANES), F32),
        ],
        name="recur",
        compiler_params=pltpu.CompilerParams(vmem_limit_bytes=GRANT),
    )(scal, *mains, *lines, conv_w, decay_w, input_w, decay_b, input_b, codes)


def finish_kernel(parts, scal, *refs):
    states, cums, before, out = refs[:parts], refs[parts : 2 * parts], refs[2 * parts : -1], refs[-1]
    incoming = jnp.zeros((1, out.shape[1]), F32)
    for step in range(len(before), 0, -1):
        piece = before[step - 1]
        incoming = piece[0:1, :] * incoming + piece[1:2, :]
        incoming = jnp.where(scal[0] >= step, incoming, 0.0)
    first = 0
    for state, cum in zip(states, cums):
        stop = first + state.shape[1]
        out[:, first:stop] = (state[...] + cum[...] * incoming[:, first:stop]).astype(BF16)
        first = stop


def finish(scal, states, cums, before):
    rows = states[0].shape[0]
    channels = before[0].shape[1]
    return pl.pallas_call(
        functools.partial(finish_kernel, len(states)),
        out_shape=jax.ShapeDtypeStruct((rows, channels), BF16),
        in_specs=[SMEM] + [VMEM] * (2 * len(states) + len(before)),
        out_specs=VMEM,
        name="finish",
        compiler_params=pltpu.CompilerParams(vmem_limit_bytes=GRANT),
    )(scal, *states, *cums, *before)


def local_near(
    queries,
    keyvals,
    segment_ids,
    residual,
    out_weight,
    lru_weight,
    conv_weight,
    gate_decay_w,
    gate_input_w,
    gate_decay_b,
    gate_input_b,
    decay_codes,
    norm_gain,
):
    rows = queries.shape[0]
    shard = keyvals.shape[0]
    tokens = segment_ids.shape[0]
    nctx, nmp = lax.axis_size("ctx"), lax.axis_size("mp")
    features = residual.shape[1]
    cols = out_weight.shape[1]
    longest = tokens // 2
    back = -(-(min(WIN, longest) - 1) // rows)
    reach = min(nctx - 1, -(-longest // rows))

    visiting = {0: queries}
    for flip in range(nctx - 1, 0, -2):
        visiting[flip] = swapped(queries, "ctx", flip)
    for flip in range(nctx - 2, 0, -2):
        visiting[flip] = swapped(visiting[flip + 1], "ctx", 1)
    kv_parts = [keyvals]
    for flip in range(1, nctx):
        kv_parts.append(swapped(keyvals, "ctx", flip))
    scal, resid_parts = pack(residual, segment_ids.reshape(-1, LANES), nctx)
    for flip in range(1, nctx):
        resid_parts[flip] = swapped(resid_parts[flip], "ctx", flip)
    pieces = {0: jnp.concatenate(kv_parts, axis=0)}
    flip = nmp // 2
    while flip >= 1:
        for done in sorted(pieces):
            pieces[done | flip] = swapped(pieces[done], "mp", flip)
        flip //= 2
    kv = assemble(scal, [pieces[e] for e in range(nmp)], rows, shard, nctx)
    chunks = [0] + list(range(nctx - 1, 2, -2)) + [1] + list(range(nctx - 2, 1, -2))
    gain = norm_gain.reshape(1, features)
    halves, places = [], {}
    messages, give = {}, {}
    for at, e in enumerate(chunks):
        now = [] if e in (1, nctx - 1) else [resid_parts[e]]
        keep, send = attend(scal, [visiting[e]], now, kv, out_weight, nctx, back, (e,), shard)
        if not now:
            keep, send = topped(scal, keep, send, resid_parts[e])
        other = swapped(send, "mp", 1)
        mine = (keep.astype(F32) + other.astype(F32)).astype(BF16)
        flip = 2
        while flip < nmp:
            other = swapped(mine, "mp", flip)
            mine = (mine.astype(F32) + other.astype(F32)).astype(BF16)
            flip *= 2
        other = swapped(mine, "mp", 1)
        halves += [mine, other]
        places[e] = (at, 0)
        messages[e], give[e] = project(scal, mine, other, gain, lru_weight, 1, shard)
    lines = list(tails(scal, halves, [places[e] for e in range(nctx)], gain, lru_weight, rows))
    blocks = lru_weight.shape[1] // BW
    parts = [(0, blocks - blocks // 2), (blocks - blocks // 2, blocks // 2)] if blocks > 1 else [(0, blocks)]
    mains = [[messages[0]] for _ in parts]
    for flip in range(nctx - 1, 0, -1):
        if flip % 2 and flip > 1:
            passed = swapped(messages[flip], "ctx", 1)
            merged = []
            for first, count in parts:
                cols = slice(first * BW, (first + count) * BW)
                both = messages[flip - 1][:, cols].astype(F32) + passed[:, cols].astype(F32)
                merged.append(both.astype(BF16))
            messages[flip - 1] = merged
        elif flip > 1:
            for part in range(len(parts)):
                mains[part].append(swapped(messages[flip][part], "ctx", flip))
        else:
            got = swapped(messages[1], "ctx", 1)
            for main in mains:
                main.append(got)
    for flip in range(1, nctx):
        lines[flip] = swapped(lines[flip], "ctx", flip)
    given = [give[0]]
    for flip in range(1, nctx):
        given.append(swapped(give[flip], "ctx", flip))
    states, cums, lasts = [], [], []
    for part, (first, count) in enumerate(parts):
        state, cum, last = recur(
            scal,
            mains[part],
            lines,
            conv_weight,
            gate_decay_w,
            gate_input_w,
            gate_decay_b.reshape(1, -1),
            gate_input_b.reshape(1, -1),
            decay_codes.reshape(1, -1),
            features,
            first,
            count,
        )
        states.append(state)
        cums.append(cum)
        lasts.append(last)
    last = jnp.concatenate(lasts, axis=1)
    before = []
    for step in range(1, reach + 1):
        before.append(rotated(last, "ctx", -step))
    resid_out = join(scal, given)
    out = finish(scal, states, cums, before)
    return (resid_out, out)


def local(queries, keyvals, segment_ids, residual, out_weight, *rest):
    nctx = lax.axis_size("ctx")
    near = (
        segment_ids.shape[0] <= WIN
        and nctx > 1
        and nctx & (nctx - 1) == 0
        and lax.axis_size("mp") % 2 == 0
        and queries.shape[1] == out_weight.shape[1]
    )
    form = local_near if near else local_wide
    return form(queries, keyvals, segment_ids, residual, out_weight, *rest)


def solution(mesh):
    in_specs = (
        P(("groups", "ctx"), "mp"),
        P(("groups", "ctx", "mp"), None),
        P("groups"),
        P(("groups", "ctx", "mp"), None),
        P("mp", "ctx"),
        P("ctx", "mp"),
        P(None, "mp"),
        P("mp", None, None),
        P("mp", None, None),
        P("mp"),
        P("mp"),
        P("mp"),
        P(),
    )
    out_specs = (P(("groups", "ctx", "mp"), None), P(("groups", "ctx"), "mp"))
    return jax.shard_map(local, mesh=mesh, in_specs=in_specs, out_specs=out_specs, check_vma=False)
```
